128 devices in a mesh: dp: 4 (over x), seq: 8 (over z, core), tensor: 4 (over y).
Axes of the slice: x: 4, y: 4, z: 4, core: 2. Of those that a mesh axis runs over, the one named last changes fastest.
Arguments:
- block_input: bfloat16 [2048, 4, 1024], P('seq', 'dp', 'tensor'), may hold values from -6 to 6
- attn_gain: bfloat16 [1024], P(('dp', 'seq')), may hold values from 0.099609375 to 1.8984375
- ffn_gain: bfloat16 [1024], P(('dp', 'seq')), may hold values from 0.099609375 to 1.8984375
- query_gain: bfloat16 [64], replicated, may hold values from 0.5 to 2.5
- key_gain: bfloat16 [64], replicated, may hold values from 0.5 to 2.5
- query_weight: bfloat16 [1024, 1024], P(('dp', 'seq'), 'tensor'), may hold values from -0.1875 to 0.1875
- key_weight: bfloat16 [1024, 512], P(('dp', 'seq'), 'tensor'), may hold values from -0.1875 to 0.1875
- value_weight: bfloat16 [1024, 512], P(('dp', 'seq'), 'tensor'), may hold values from -0.1875 to 0.1875
- out_weight: bfloat16 [1024, 1024], P(('dp', 'seq'), 'tensor'), may hold values from -2 to 2
- gate_weight: bfloat16 [1024, 4608], P(('dp', 'seq'), 'tensor'), may hold values from -0.1875 to 0.1875
- up_weight: bfloat16 [1024, 4608], P(('dp', 'seq'), 'tensor'), may hold values from -0.1875 to 0.1875
- down_weight: bfloat16 [1024, 4608], P(('dp', 'seq'), 'tensor'), may hold values from -0.09375 to 0.09375
- cotangent: bfloat16 [2048, 4, 1024], P('seq', 'dp', 'tensor'), may hold values from -6 to 6
Outputs:
- block_output: bfloat16 [2048, 4, 1024], P('seq', 'dp', 'tensor')
- input_grad: bfloat16 [2048, 4, 1024], P('seq', 'dp', 'tensor')
- attn_gain_grad: float32 [1024], P(('dp', 'seq'))
- ffn_gain_grad: float32 [1024], P(('dp', 'seq'))
- query_gain_grad: float32 [64], replicated
- key_gain_grad: float32 [64], replicated
- query_grad: float32 [1024, 1024], P(('dp', 'seq'), 'tensor')
- key_grad: float32 [1024, 512], P(('dp', 'seq'), 'tensor')
- value_grad: float32 [1024, 512], P(('dp', 'seq'), 'tensor')
- out_grad: float32 [1024, 1024], P(('dp', 'seq'), 'tensor')
- gate_grad: float32 [1024, 4608], P(('dp', 'seq'), 'tensor')
- up_grad: float32 [1024, 4608], P(('dp', 'seq'), 'tensor')
- down_grad: float32 [1024, 4608], P(('dp', 'seq'), 'tensor')
The draws below stay inside these ranges and needn't reach their ends.
All inputs are finite; a program needn't handle non-finite values.
Results may differ from the reference program's by a relative error of at most 0.03.
Values may be sent and summed in bfloat16 or wider, within the bound.
No kernel may reach another device: no remote copies, remote signals or barrier semaphores. Data moves between devices by JAX's collectives and lax.ppermute only.
A program may use at most 64 MiB of HBM per device.

```python
import math
import jax
import jax.numpy as jnp
from jax import lax

D = 1024
HD = 64
FF = 4608
QW = 1024
KW = 512
LEN = 2048
SEQS = 4


def levels(rng, shape, shards, low, high):
    level, own = 1.0, jax.random.fold_in(rng, 6)
    for dim, shards_of in shards:
        steps = jnp.exp(jax.random.uniform(jax.random.fold_in(own, dim), (shards_of,), jnp.float32, low / len(shards), high / len(shards)))
        level = level * jnp.repeat(steps, shape[dim] // shards_of).reshape([-1 if axis == dim else 1 for axis in range(len(shape))])
    return level


def scatter_about(rng, dims, deviation, most, shards=(), kind=jnp.bfloat16):
    drawn = deviation * jax.random.normal(rng, dims, jnp.float32)
    if shards:
        drawn = drawn * levels(rng, dims, shards, -0.22, 0.18)
    return jnp.clip(drawn, -most, most).astype(kind)


def setup_inputs(seed: int = 0) -> dict:
    key_of = jax.random.split(jax.random.key(seed), 14)
    block_input = scatter_about(key_of[0], (LEN, SEQS, D), 1.0, 6.0, ((0, 8), (1, 4), (2, 4)))
    attn_gain = jnp.clip(1.0 + 0.18 * jax.random.normal(key_of[1], (D,), jnp.float32), 0.099609375, 1.8984375).astype(jnp.bfloat16)
    ffn_gain = jnp.clip(1.0 + 0.18 * jax.random.normal(key_of[2], (D,), jnp.float32), 0.099609375, 1.8984375).astype(jnp.bfloat16)
    query_gain = jnp.clip(jnp.exp(jax.random.uniform(key_of[3], (HD,), jnp.float32, math.log(0.5), math.log(2.5))), 0.5, 2.5).astype(jnp.bfloat16)
    key_gain = jnp.clip(jnp.exp(jax.random.uniform(key_of[4], (HD,), jnp.float32, math.log(0.5), math.log(2.5))), 0.5, 2.5).astype(jnp.bfloat16)
    query_weight = scatter_about(key_of[5], (D, QW), D ** -0.5, 0.1875, ((0, 32), (1, 4)))
    key_weight = scatter_about(key_of[6], (D, KW), D ** -0.5, 0.1875, ((0, 32), (1, 4)))
    value_weight = scatter_about(key_of[7], (D, KW), D ** -0.5, 0.1875, ((0, 32), (1, 4)))
    out_weight = scatter_about(key_of[8], (D, QW), (QW // 128) ** -0.5, 2.0, ((0, 32), (1, 4)))
    gate_weight = scatter_about(key_of[9], (D, FF), D ** -0.5, 0.1875, ((0, 32), (1, 4)))
    up_weight = scatter_about(key_of[10], (D, FF), D ** -0.5, 0.1875, ((0, 32), (1, 4)))
    down_weight = scatter_about(key_of[11], (D, FF), FF ** -0.5, 0.09375, ((0, 32), (1, 4)))
    cotangent = scatter_about(key_of[12], (LEN, SEQS, D), 1.0, 6.0, ((0, 8), (1, 4), (2, 4)))
    return {"block_input": block_input, "attn_gain": attn_gain, "ffn_gain": ffn_gain, "query_gain": query_gain, "key_gain": key_gain, "query_weight": query_weight, "key_weight": key_weight, "value_weight": value_weight, "out_weight": out_weight, "gate_weight": gate_weight, "up_weight": up_weight, "down_weight": down_weight, "cotangent": cotangent}


epsilon = 1e-05
rope_base = 1000000.0
far_below = -1e+30

def rounded(values):
    return lax.optimization_barrier(values.astype(jnp.bfloat16))

def widened(values):
    return values.astype(jnp.float32)

def rms_scale(values, gain):
    return values * lax.rsqrt(lax.optimization_barrier(jnp.mean(values * values, axis=-1, keepdims=True)) + epsilon) * gain

def swiglu(gate, up_part):
    return jax.nn.silu(gate) * up_part

def rotate(values, cosine, sine):
    half = values.shape[-1] // 2
    first = values[..., :half]
    second = values[..., half:]
    return jnp.concatenate([first * cosine - second * sine, second * cosine + first * sine], axis=-1)

def project(left, right):
    return jnp.dot(left, right, preferred_element_type=jnp.float32)

def masked_scores(query_block, first, keys):
    scores = jnp.einsum('qkgd,tkd->qkgt', widened(query_block), widened(keys)) * HD ** (-0.5)
    query_pos = first + jnp.arange(query_block.shape[0], dtype=jnp.int32)
    key_pos = jnp.arange(keys.shape[0], dtype=jnp.int32)
    allowed = (query_pos[:, None] >= key_pos[None, :])[:, None, None, :]
    return (scores, allowed)

def attend_block(query_block, first, keys, values):
    scores, allowed = masked_scores(query_block, first, keys)
    top = lax.optimization_barrier(jnp.max(jnp.where(allowed, scores, far_below), axis=-1))
    expo = jnp.where(allowed, jnp.exp(scores - top[..., None]), 0.0)
    total = lax.optimization_barrier(jnp.sum(expo, axis=-1))
    mixed = jnp.einsum('qkgt,tkd->qkgd', widened(rounded(expo)), widened(values)) / total[..., None]
    return (mixed, top + jnp.log(total))

def attend_back(query_block, first, keys, values, log_total, grad_block, delta):
    scores, allowed = masked_scores(query_block, first, keys)
    probs = jnp.where(allowed, jnp.exp(scores - log_total[..., None]), 0.0)
    prob_grad = jnp.einsum('qkgd,tkd->qkgt', widened(grad_block), widened(values))
    score_grad = widened(rounded(probs * (prob_grad - delta[..., None])))
    query_part = jnp.einsum('qkgt,tkd->qkgd', score_grad, widened(keys)) * HD ** (-0.5)
    key_part = jnp.einsum('qkgt,qkgd->tkd', score_grad, widened(query_block)) * HD ** (-0.5)
    value_part = jnp.einsum('qkgt,qkgd->tkd', widened(rounded(probs)), widened(grad_block))
    return (query_part, key_part, value_part)

def reference(block_input, attn_gain, ffn_gain, query_gain, key_gain, query_weight, key_weight, value_weight, out_weight, gate_weight, up_weight, down_weight, cotangent):
    gain_one = widened(attn_gain)
    gain_two = widened(ffn_gain)
    head_query = widened(query_gain)
    head_key = widened(key_gain)
    kv_heads = key_weight.shape[1] // HD
    group = query_weight.shape[1] // key_weight.shape[1]
    block = min(512, LEN)
    blocks = LEN // block
    positions = jnp.arange(LEN, dtype=jnp.int32)
    frequency = jnp.power(rope_base, -2.0 * jnp.arange(HD // 2, dtype=jnp.float32) / HD)
    angle = widened(positions)[:, None] * frequency[None, :]
    cosine = jnp.cos(angle)[:, None, :]
    sine = jnp.sin(angle)[:, None, :]
    block_starts = jnp.arange(blocks, dtype=jnp.int32) * block

    def shape_heads(raw, gain):
        heads = raw.reshape(raw.shape[0], raw.shape[1] // HD, HD)
        return rotate(rms_scale(heads, gain), cosine, sine)

    def one_sequence(sums, pair):
        source, cot = pair
        base = widened(source)
        normed_one = rounded(rms_scale(base, gain_one))
        query_raw = project(normed_one, query_weight)
        key_raw = project(normed_one, key_weight)
        value_raw = project(normed_one, value_weight)
        query_rot, pull_query = jax.vjp(shape_heads, query_raw, head_query)
        key_rot, pull_key = jax.vjp(shape_heads, key_raw, head_key)
        query_b = rounded(query_rot).reshape(blocks, block, kv_heads, group, HD)
        key_b = rounded(key_rot)
        value_b = rounded(value_raw).reshape(LEN, kv_heads, HD)
        mixed, log_total = lax.map(lambda item: attend_block(item[0], item[1], key_b, value_b), (query_b, block_starts))
        attn_values = mixed.reshape(LEN, kv_heads, group, HD)
        attn_b = rounded(attn_values.reshape(LEN, -1))
        middle = base + project(attn_b, out_weight.T)
        normed_two = rounded(rms_scale(middle, gain_two))
        gate = project(normed_two, gate_weight)
        up_part = project(normed_two, up_weight)
        hidden = rounded(swiglu(gate, up_part))
        output = (middle + project(hidden, down_weight.T)).astype(jnp.bfloat16)
        hidden_grad = project(cot, down_weight)
        down_sum = project(cot.T, hidden)
        _, pull_swiglu = jax.vjp(swiglu, gate, up_part)
        gate_grad, up_grad = pull_swiglu(hidden_grad)
        gate_gb = rounded(gate_grad)
        up_gb = rounded(up_grad)
        normed_two_grad = project(gate_gb, gate_weight.T) + project(up_gb, up_weight.T)
        gate_sum = project(normed_two.T, gate_gb)
        up_sum = project(normed_two.T, up_gb)
        _, pull_two = jax.vjp(rms_scale, middle, gain_two)
        middle_norm_grad, gain_two_grad = pull_two(normed_two_grad)
        middle_grad = widened(cot) + middle_norm_grad
        middle_gb = rounded(middle_grad)
        attn_grad = project(middle_gb, out_weight)
        out_sum = project(middle_gb.T, attn_b)
        attn_gb = rounded(attn_grad).reshape(blocks, block, kv_heads, group, HD)
        delta = lax.optimization_barrier(jnp.sum(attn_grad.reshape(LEN, kv_heads, group, HD) * attn_values, axis=-1)).reshape(blocks, block, kv_heads, group)
        query_hgrad, key_parts, value_parts = lax.map(lambda item: attend_back(item[0], item[1], key_b, value_b, item[2], item[3], item[4]), (query_b, block_starts, log_total, attn_gb, delta))
        query_raw_grad, query_gain_grad = pull_query(query_hgrad.reshape(LEN, kv_heads * group, HD))
        key_raw_grad, key_gain_grad = pull_key(lax.optimization_barrier(jnp.sum(key_parts, axis=0)))
        query_gb = rounded(query_raw_grad)
        key_gb = rounded(key_raw_grad)
        value_gb = rounded(lax.optimization_barrier(jnp.sum(value_parts, axis=0)).reshape(LEN, -1))
        normed_one_grad = project(query_gb, query_weight.T) + project(key_gb, key_weight.T) + project(value_gb, value_weight.T)
        _, pull_one = jax.vjp(rms_scale, base, gain_one)
        base_norm_grad, gain_one_grad = pull_one(normed_one_grad)
        input_grad = (middle_grad + base_norm_grad).astype(jnp.bfloat16)
        terms = (gain_one_grad, gain_two_grad, query_gain_grad, key_gain_grad, project(normed_one.T, query_gb), project(normed_one.T, key_gb), project(normed_one.T, value_gb), out_sum, gate_sum, up_sum, down_sum)
        return (tuple((total + term for total, term in zip(sums, terms))), (output, input_grad))
    initial = tuple((jnp.zeros(item.shape, jnp.float32) for item in (attn_gain, ffn_gain, query_gain, key_gain, query_weight, key_weight, value_weight, out_weight, gate_weight, up_weight, down_weight)))
    sums, (outputs, input_grads) = lax.scan(one_sequence, initial, (jnp.swapaxes(block_input, 0, 1), jnp.swapaxes(cotangent, 0, 1)))
    return (jnp.swapaxes(outputs, 0, 1), jnp.swapaxes(input_grads, 0, 1), sums[0], sums[1], sums[2], sums[3], sums[4], sums[5], sums[6], sums[7], sums[8], sums[9], sums[10])
```

```python
import numpy as np
import jax
import jax.numpy as jnp
from jax import lax
from jax.sharding import Mesh, PartitionSpec as P

HD = 64
epsilon = 1e-05
rope_base = 1000000.0
far_below = -1e30
bf16 = jnp.bfloat16
f32 = jnp.float32


def rms_scale(values, gain):
    return values * lax.rsqrt(jnp.mean(values * values, axis=-1, keepdims=True) + epsilon) * gain


def swiglu(gate, up_part):
    return jax.nn.silu(gate) * up_part


def rotate(values, cosine, sine):
    half = values.shape[-1] // 2
    first = values[..., :half]
    second = values[..., half:]
    return jnp.concatenate(
        [first * cosine - second * sine, second * cosine + first * sine], axis=-1
    )


def project(left, right):
    return jnp.dot(left, right, preferred_element_type=f32)


def contract_rows(left, right):
    return lax.dot_general(left, right, (((0,), (0,)), ((), ())), preferred_element_type=f32)


def contract_cols(left, right):
    return lax.dot_general(left, right, (((1,), (1,)), ((), ())), preferred_element_type=f32)


def shift(x, axis, k):
    n = lax.axis_size(axis)
    return lax.ppermute(x, axis, [(i, (i + k) % n) for i in range(n)])


def gather_parts(x, axis):
    n = lax.axis_size(axis)
    me = lax.axis_index(axis)
    parts = [x] + [shift(x, axis, k) for k in range(1, n)]
    out = jnp.zeros((n,) + x.shape, x.dtype)
    for k, part in enumerate(parts):
        out = lax.dynamic_update_slice_in_dim(out, part[None], (me - k + n) % n, 0)
    return out


def scatter_sum(x, axis):
    n = lax.axis_size(axis)
    me = lax.axis_index(axis)

    def piece(k):
        return lax.dynamic_index_in_dim(x, (me + k) % n, 0, keepdims=False)

    got = [shift(piece(k), axis, k) for k in range(1, n)]
    total = piece(0).astype(f32)
    for part in got:
        total = total + part.astype(f32)
    return total


def scatter_rows(x):
    nd, nz, nc = (lax.axis_size(a) for a in ("dp", "z", "core"))
    rows, width = x.shape
    own = rows // (nd * nz * nc)
    x = x.reshape(nd * nz, nc, own, width).swapaxes(0, 1)
    x = scatter_sum(x, "core").astype(bf16)
    x = x.reshape(nd, nz * own, width)
    x = scatter_sum(x, "dp").astype(bf16)
    x = x.reshape(nz, own, width)
    return scatter_sum(x, "z")


def body(
    block_input,
    attn_gain,
    ffn_gain,
    query_gain,
    key_gain,
    query_weight,
    key_weight,
    value_weight,
    out_weight,
    gate_weight,
    up_weight,
    down_weight,
    cotangent,
):
    span, seq_local, part = block_input.shape
    row_count = span * seq_local
    tensor = lax.axis_size("tensor")
    width = part * tensor
    own_rows = query_weight.shape[0]
    seq_devices = lax.axis_size("z") * lax.axis_size("core")
    my_first = (lax.axis_index("z") * lax.axis_size("core") + lax.axis_index("core")) * span
    q_cols = query_weight.shape[1]
    kv_cols = key_weight.shape[1]
    out_cols = out_weight.shape[1]
    ff_cols = gate_weight.shape[1]
    kv_heads = kv_cols // HD
    group = q_cols // kv_cols
    score_scale = HD ** (-0.5)
    full_length = span * seq_devices

    ffn_local = jnp.concatenate([gate_weight, up_weight, down_weight], axis=1)
    ffn_full = lax.all_gather(ffn_local, ("dp", "z", "core"), axis=0, tiled=True)

    gains_local = jnp.concatenate(
        [
            attn_gain[:, None],
            ffn_gain[:, None],
            jnp.zeros((own_rows, 126), bf16),
        ],
        axis=1,
    )
    attn_local = jnp.concatenate(
        [query_weight, key_weight, value_weight, out_weight, gains_local], axis=1
    )

    def gather_rows(x):
        x = gather_parts(x, "dp")
        x = gather_parts(x, "z")
        x = gather_parts(x, "core")
        nc, nz, nd, r, w = x.shape
        return x.transpose(2, 1, 0, 3, 4).reshape(nc * nz * nd * r, w)

    attn_full = gather_rows(attn_local)
    source = gather_parts(block_input.reshape(row_count, part), "tensor")
    base = source.swapaxes(0, 1).reshape(row_count, width).astype(f32)
    cot_full = (
        gather_parts(cotangent.reshape(row_count, part), "tensor")
        .swapaxes(0, 1)
        .reshape(row_count, width)
    )
    qkv_cols = q_cols + 2 * kv_cols
    qkv_full = attn_full[:, :qkv_cols]
    out_full = attn_full[:, qkv_cols : qkv_cols + out_cols]
    gain_one = attn_full[:, qkv_cols + out_cols].astype(f32)
    gain_two = attn_full[:, qkv_cols + out_cols + 1].astype(f32)
    gate_full = ffn_full[:, :ff_cols]
    up_full = ffn_full[:, ff_cols : 2 * ff_cols]
    down_full = ffn_full[:, 2 * ff_cols :]

    head_query = query_gain.astype(f32)
    head_key = key_gain.astype(f32)
    positions = my_first + jnp.arange(span, dtype=jnp.int32)
    frequency = jnp.power(rope_base, -2.0 * jnp.arange(HD // 2, dtype=f32) / HD)
    angle = positions.astype(f32)[:, None] * frequency[None, :]
    cosine = jnp.cos(angle)[:, None, :]
    sine = jnp.sin(angle)[:, None, :]

    def shape_heads(raw, gain):
        heads = raw.reshape(row_count, raw.shape[1] // HD, HD)
        return rotate(rms_scale(heads, gain), cosine, sine)

    normed_one = rms_scale(base, gain_one).astype(bf16)
    qkv_raw = project(normed_one, qkv_full)
    query_raw = qkv_raw[:, :q_cols]
    key_raw = qkv_raw[:, q_cols : q_cols + kv_cols]
    value_raw = qkv_raw[:, q_cols + kv_cols :]
    query_rot, pull_query = jax.vjp(shape_heads, query_raw, head_query)
    key_rot, pull_key = jax.vjp(shape_heads, key_raw, head_key)
    query_b = query_rot.astype(bf16).reshape(row_count, kv_heads, group, HD)
    packed = jnp.concatenate(
        [key_rot.astype(bf16).reshape(row_count, kv_cols), value_raw.astype(bf16)], axis=-1
    )
    piece = gather_parts(gather_parts(packed, "z"), "core")
    piece = piece.swapaxes(0, 1).reshape(full_length, 2 * kv_cols)
    keys = piece[:, :kv_cols].reshape(full_length, kv_heads, HD)
    values = piece[:, kv_cols:].reshape(full_length, kv_heads, HD)

    key_pos = jnp.arange(full_length, dtype=jnp.int32)
    allowed = (positions[:, None] >= key_pos[None, :])[:, None, None, :]

    def scores():
        return (
            jnp.einsum("ckgd,pkd->ckgp", query_b, keys, preferred_element_type=f32) * score_scale
        )

    raw = jnp.where(allowed, scores(), far_below)
    top = jnp.max(raw, axis=-1)
    expo = jnp.exp(raw - top[..., None])
    total = jnp.sum(expo, axis=-1)
    accum = jnp.einsum("ckgp,pkd->ckgd", expo.astype(bf16), values, preferred_element_type=f32)
    attn_values = accum / total[..., None]
    log_total = top + jnp.log(total)
    attn_b = attn_values.reshape(row_count, -1).astype(bf16)

    def by_features(x):
        return x.reshape(row_count, tensor, part).swapaxes(0, 1)

    def all_sum(x):
        mine = scatter_sum(by_features(x.astype(bf16)), "tensor").astype(bf16)
        return gather_parts(mine, "tensor").swapaxes(0, 1).reshape(row_count, width).astype(f32)

    middle = base + all_sum(contract_cols(attn_b, out_full))
    normed_two = rms_scale(middle, gain_two).astype(bf16)
    gate = project(normed_two, gate_full)
    up_part = project(normed_two, up_full)
    hidden = swiglu(gate, up_part).astype(bf16)

    hidden_grad = project(cot_full, down_full)
    _, pull_swiglu = jax.vjp(swiglu, gate, up_part)
    gate_grad, up_grad = pull_swiglu(hidden_grad)
    gate_gb = gate_grad.astype(bf16)
    up_gb = up_grad.astype(bf16)
    normed_two_grad = all_sum(contract_cols(gate_gb, gate_full) + contract_cols(up_gb, up_full))

    down_sum = contract_rows(cot_full, hidden).astype(bf16)
    gate_sum = contract_rows(normed_two, gate_gb).astype(bf16)
    up_sum = contract_rows(normed_two, up_gb).astype(bf16)
    ffn_sum = scatter_rows(jnp.concatenate([gate_sum, up_sum, down_sum], axis=1))

    ffn_mine = scatter_sum(
        by_features(contract_cols(hidden, down_full).astype(bf16)), "tensor"
    )
    middle_mine = lax.dynamic_index_in_dim(
        by_features(middle), lax.axis_index("tensor"), 0, keepdims=False
    )
    block_output = (middle_mine + ffn_mine).astype(bf16).reshape(span, seq_local, part)

    _, pull_two = jax.vjp(rms_scale, middle, gain_two)
    middle_norm_grad, gain_two_grad = pull_two(normed_two_grad)
    middle_grad = cot_full.astype(f32) + middle_norm_grad
    middle_gb = middle_grad.astype(bf16)
    attn_grad = project(middle_gb, out_full)
    out_sum = contract_rows(middle_gb, attn_b).astype(bf16)
    attn_heads = attn_grad.reshape(row_count, kv_heads, group, HD)
    attn_gb = attn_heads.astype(bf16)
    delta = jnp.sum(attn_heads * attn_values, axis=-1)

    probs = jnp.where(allowed, jnp.exp(scores() - log_total[..., None]), 0.0)
    prob_grad = jnp.einsum("ckgd,pkd->ckgp", attn_gb, values, preferred_element_type=f32)
    score_gb = (probs * (prob_grad - delta[..., None])).astype(bf16)
    query_hgrad = (
        jnp.einsum("ckgp,pkd->ckgd", score_gb, keys, preferred_element_type=f32) * score_scale
    )
    key_part = (
        jnp.einsum("ckgp,ckgd->pkd", score_gb, query_b, preferred_element_type=f32) * score_scale
    )
    value_part = jnp.einsum(
        "ckgp,ckgd->pkd", probs.astype(bf16), attn_gb, preferred_element_type=f32
    )
    kv_total = jnp.concatenate(
        [key_part.reshape(full_length, kv_cols), value_part.reshape(full_length, kv_cols)], axis=-1
    ).astype(bf16)
    nz, nc = lax.axis_size("z"), lax.axis_size("core")
    kv_total = kv_total.reshape(nz, nc, row_count, 2 * kv_cols).swapaxes(0, 1)
    kv_mine = scatter_sum(scatter_sum(kv_total, "core").astype(bf16), "z")

    query_raw_grad, query_gain_part = pull_query(
        query_hgrad.reshape(row_count, kv_heads * group, HD)
    )
    key_raw_grad, key_gain_part = pull_key(kv_mine[:, :kv_cols].reshape(row_count, kv_heads, HD))
    qkv_gb = jnp.concatenate(
        [query_raw_grad.astype(bf16), key_raw_grad.astype(bf16), kv_mine[:, kv_cols:].astype(bf16)],
        axis=1,
    )
    norm_part = contract_cols(qkv_gb, qkv_full)
    scale_one = lax.rsqrt(jnp.mean(base * base, axis=-1, keepdims=True) + epsilon)
    normal_one = base * scale_one
    gain_one_part = jnp.sum(norm_part * normal_one, axis=0)
    dot_part = jnp.sum(norm_part * gain_one * normal_one, axis=1)
    norm_mine = scatter_sum(by_features(norm_part.astype(bf16)), "tensor")
    dot_all = sum([dot_part] + [shift(dot_part, "tensor", k) for k in range(1, tensor)])
    me_t = lax.axis_index("tensor")
    mine = lambda x: lax.dynamic_index_in_dim(by_features(x), me_t, 0, keepdims=False)
    gain_mine = lax.dynamic_slice_in_dim(gain_one, me_t * part, part, 0)
    input_grad = (
        mine(middle_grad)
        + scale_one * (norm_mine * gain_mine - mine(normal_one) * (dot_all / width)[:, None])
    ).astype(bf16)

    qkv_sum = contract_rows(normed_one, qkv_gb).astype(bf16)

    pieces = width // own_rows

    def halves(x):
        high = x.astype(bf16)
        return high, (x - high.astype(f32)).astype(bf16)

    heads_high, heads_low = halves(jnp.concatenate([query_gain_part, key_gain_part]))
    one_high, one_low = halves(gain_one_part.reshape(pieces, own_rows))
    two_high, two_low = halves(gain_two_grad.reshape(pieces, own_rows))
    pad = lambda x: jnp.pad(x, ((0, 0), (0, 128 - own_rows)))
    spread = lambda x: jnp.broadcast_to(x[None], (pieces, 128))
    extra = jnp.stack(
        [spread(heads_high), spread(heads_low), pad(one_high), pad(one_low), pad(two_high), pad(two_low)], axis=1
    )
    extra = jnp.pad(extra, ((0, 0), (0, own_rows - 6), (0, 0))).reshape(width, 128)
    attn_sum = scatter_rows(jnp.concatenate([qkv_sum, out_sum, extra], axis=1))
    small = attn_sum[:8, qkv_cols + out_cols :]
    small_all = sum([small] + [shift(small, "tensor", k) for k in range(1, tensor)])
    head_sum = small_all[0] + small_all[1]
    gain_one_sum = (small_all[2] + small_all[3])[:own_rows]
    gain_two_sum = (small[4] + small[5])[:own_rows]
    return (
        block_output,
        input_grad.reshape(span, seq_local, part),
        gain_one_sum,
        gain_two_sum,
        head_sum[:HD],
        head_sum[HD:],
        attn_sum[:, :q_cols],
        attn_sum[:, q_cols : q_cols + kv_cols],
        attn_sum[:, q_cols + kv_cols : qkv_cols],
        attn_sum[:, qkv_cols : qkv_cols + out_cols],
        ffn_sum[:, :ff_cols],
        ffn_sum[:, ff_cols : 2 * ff_cols],
        ffn_sum[:, 2 * ff_cols :],
    )


def solution(mesh):
    dp, seq, tensor = (mesh.shape[a] for a in ("dp", "seq", "tensor"))
    grid = Mesh(
        np.asarray(mesh.devices).reshape(dp, seq // 2, 2, tensor), ("dp", "z", "core", "tensor")
    )
    tokens = P(("z", "core"), "dp", "tensor")
    rows = P(("dp", "z", "core"))
    weight = P(("dp", "z", "core"), "tensor")
    return jax.shard_map(
        body,
        mesh=grid,
        in_specs=(tokens, rows, rows, P(), P()) + (weight,) * 7 + (tokens,),
        out_specs=(tokens, tokens, rows, rows, P(), P()) + (weight,) * 7,
        check_vma=False,
    )
```

```python
import functools

import numpy as np
import jax
import jax.numpy as jnp
from jax import lax
from jax.experimental import pallas as pl
from jax.experimental.pallas import tpu as pltpu
from jax.sharding import Mesh, PartitionSpec as P

HD = 64
HALF = HD // 2
EPS = 1e-05
ROPE_BASE = 1000000.0
SCALE = HD ** (-0.5)
PAD = 128
bf16 = jnp.bfloat16
f32 = jnp.float32
NN = (((1,), (0,)), ((), ()))
NT = (((1,), (1,)), ((), ()))


def dot(a, b, dims=NN):
    return lax.dot_general(a, b, dims, preferred_element_type=f32)


def rot_index(a, k, n):
    return lax.rem(a + k, n)


def ds(start, size):
    return pl.ds(pl.multiple_of(start * size, size), size)


def shift(x, axis, k):
    n = lax.axis_size(axis)
    return lax.ppermute(x, axis, [(i, (i + k) % n) for i in range(n)])


def gathered(x, axis):
    return [x] + [shift(x, axis, k) for k in range(1, lax.axis_size(axis))]


def summed(pieces, axis):
    total = pieces[0].astype(f32)
    for k in range(1, lax.axis_size(axis)):
        total = total + shift(pieces[k], axis, k).astype(f32)
    return total


def call(kernel, outs, ins, scratch=(), grid=None, in_specs=None, out_specs=None, flops=0):
    vm = pl.BlockSpec(memory_space=pltpu.VMEM)
    nbytes = sum(x.size * x.dtype.itemsize for x in list(ins) + list(outs))
    kwargs = {} if grid is None else {"grid": grid}
    return pl.pallas_call(
        kernel,
        out_shape=outs,
        in_specs=in_specs or [pl.BlockSpec(memory_space=pltpu.SMEM)] + [vm] * (len(ins) - 1),
        out_specs=out_specs or [vm] * len(outs),
        scratch_shapes=list(scratch),
        cost_estimate=pl.CostEstimate(flops=flops, bytes_accessed=nbytes, transcendentals=0),
        **kwargs,
    )(*ins)


def sds(shape, dtype):
    return jax.ShapeDtypeStruct(shape, dtype)


def store_relative(dims, idx, dst, src, own):
    nx, nz, nc, _ = dims
    x, z, c = idx[0], idx[1], idx[2]
    at = 0
    for other in range(nc):
        core = c if other == 0 else 1 - c
        for xr in range(nx):
            for zr in range(nz):
                row = (rot_index(x, xr, nx) * nz + rot_index(z, zr, nz)) * nc + core
                dst[at * own : (at + 1) * own, :] = src[ds(row, own), :]
                at += 1


def assemble(idx, n, pieces, dst, first=0):
    part = dst.shape[1] // n
    for k in range(n):
        dst[:, ds(rot_index(idx[3], n - k, n), part)] = pieces[k][:, first : first + part]


def cot_kernel(dims, own, idx, *refs):
    n = dims[3]
    pieces, (full, rel, turned) = refs[:n], refs[n:]
    assemble(idx, n, pieces, full, full.shape[1] // n)
    turned[...] = full[...].T
    store_relative(dims, idx, rel, turned, own)


def turn_heads(raw, gain, cosine, sine, heads):
    outs = []
    for h in range(heads):
        v = raw[h * HD : (h + 1) * HD]
        v = v * lax.rsqrt(jnp.mean(v * v, axis=0, keepdims=True) + EPS) * gain
        a, b = v[:HALF], v[HALF:]
        outs += [a * cosine - b * sine, b * cosine + a * sine]
    return jnp.concatenate(outs, axis=0)


def turn_heads_back(raw, grad, gain, cosine, sine, heads):
    outs, gain_grad = [], jnp.zeros((HD, 1), f32)
    for h in range(heads):
        v = raw[h * HD : (h + 1) * HD]
        g = grad[h * HD : (h + 1) * HD]
        ga, gb = g[:HALF], g[HALF:]
        g = jnp.concatenate([ga * cosine + gb * sine, gb * cosine - ga * sine], axis=0)
        r = lax.rsqrt(jnp.mean(v * v, axis=0, keepdims=True) + EPS)
        n = v * r
        gain_grad = gain_grad + jnp.sum(g * n, axis=1, keepdims=True)
        g = g * gain
        outs.append(r * (g - n * jnp.mean(g * n, axis=0, keepdims=True)))
    return jnp.concatenate(outs, axis=0), gain_grad


def qkv_kernel(dims, own, qc, kc, oc, idx, *refs):
    nx, nz, nc, n = dims
    pieces = refs[:n]
    w_own, w_partner, gq, gk, cosine, sine = refs[n : n + 6]
    w, base, gains, q_t, raw_t, kv, rel, turned = refs[n + 6 :]
    assemble(idx, n, pieces, base)
    for other, src in enumerate((w_own, w_partner)):
        core = idx[2] if other == 0 else 1 - idx[2]
        for zr in range(nz):
            for xr in range(nx):
                row = (rot_index(idx[0], nx - xr, nx) * nz + rot_index(idx[1], nz - zr, nz)) * nc + core
                at = xr * nz + zr
                w[ds(row, own), :] = src[at * own : (at + 1) * own, :]
    qkv = qc + 2 * kc
    gains[...] = w[:, qkv:].astype(f32).T[:8]
    b = base[...].astype(f32)
    normed = b * lax.rsqrt(jnp.mean(b * b, axis=1, keepdims=True) + EPS) * gains[0:1, :]
    normed = normed.astype(bf16)
    raw = dot(normed, w[:, :qkv])
    turned[...] = normed.T
    store_relative(dims, idx, rel, turned, own)
    kv[:, kc:] = raw[:, qc + kc :].astype(bf16)
    rt = raw[:, : qc + kc].T
    raw_t[...] = rt
    co, si = cosine[...], sine[...]
    q_t[...] = turn_heads(rt[:qc], gq[...], co, si, qc // HD).astype(bf16)
    kv[:, :kc] = turn_heads(rt[qc:], gk[...], co, si, kc // HD).T.astype(bf16)


def attend_kernel(dims, qc, kc, oc, idx, q_t, kv_own, kv_partner, w_low, w_high, *refs):
    nx, nz, nc, n = dims
    kv, attn_t, attn_b, log_total = refs[:4]
    pieces = refs[4 : 4 + n]
    acc, tot = refs[4 + n :]
    span = q_t.shape[1]
    me = idx[1] * nc + idx[2]
    for other, src in enumerate((kv_own, kv_partner)):
        core = idx[2] if other == 0 else 1 - idx[2]
        for zr in range(nz):
            block = rot_index(idx[1], nz - zr, nz) * nc + core
            kv[ds(block, span), :] = src[zr * span : (zr + 1) * span, :]
    heads, kv_heads = qc // HD, kc // HD
    group = heads // kv_heads
    acc[...] = jnp.zeros_like(acc)
    tot[...] = jnp.zeros_like(tot)
    keys_at = lax.broadcasted_iota(jnp.int32, (span, span), 0)
    query_at = lax.broadcasted_iota(jnp.int32, (span, span), 1)

    def step(j, carry):
        kb = kv[ds(j, span), :kc]
        vt = kv[ds(j, span), kc:].T
        allowed = keys_at + j * span <= query_at + me * span
        for h in range(heads):
            g = h // group
            s = dot(kb[:, g * HD : (g + 1) * HD], q_t[h * HD : (h + 1) * HD, :])
            e = jnp.where(allowed, jnp.exp(s * SCALE), 0.0)
            tot[h : h + 1, :] += jnp.sum(e, axis=0, keepdims=True)
            acc[h * HD : (h + 1) * HD, :] += dot(vt[g * HD : (g + 1) * HD], e.astype(bf16))
        return carry

    lax.fori_loop(0, me + 1, step, 0)
    for h in range(heads):
        rows = slice(h * HD, (h + 1) * HD)
        attn_t[rows, :] = acc[rows, :] / tot[h : h + 1, :]
    log_total[...] = jnp.log(jnp.maximum(tot[...], 1e-30))
    attn = attn_t[...].T.astype(bf16)
    attn_b[...] = attn
    part = w_low.shape[0] // n
    for k in range(n):
        rows = ds(rot_index(idx[3], k, n), part)
        out = dot(attn[:, :PAD], w_low[rows, :], NT) + dot(attn[:, PAD:], w_high[rows, :], NT)
        pieces[k][...] = out.astype(bf16)


def ffn_kernel(dims, own, idx, base, gains, cot, *refs):
    n = dims[3]
    sums = refs[:n]
    wg, wu, wd = refs[n : n + 3]
    middle, normed, big = refs[n + 3 : n + 6]
    pieces = refs[n + 6 : n + 6 + n]
    acc = refs[n + 6 + n]
    j = pl.program_id(0)
    part = sums[0].shape[1]

    @pl.when(j == 0)
    def _():
        for k in range(n):
            at = ds(rot_index(idx[3], n - k, n), part)
            middle[:, at] = base[:, at].astype(f32) + sums[k][...].astype(f32)
        m = middle[...]
        v = m * lax.rsqrt(jnp.mean(m * m, axis=1, keepdims=True) + EPS) * gains[1:2, :]
        v = v.astype(bf16)
        normed[...] = v
        acc[...] = jnp.zeros_like(acc)

    v = normed[...]
    block = wg.shape[1]
    ff = big.shape[1] // 3
    gate = dot(v, wg[...])
    up = dot(v, wu[...])
    hg = dot(cot[...], wd[...])
    sig = 1.0 / (1.0 + jnp.exp(-gate))
    act = gate * sig
    hidden = (act * up).astype(bf16)
    gate_gb = (hg * up * (sig + act * (1.0 - sig))).astype(bf16)
    up_gb = (hg * act).astype(bf16)
    big[:, pl.ds(pl.multiple_of(j * block, block), block)] = gate_gb
    big[:, pl.ds(pl.multiple_of(ff + j * block, PAD), block)] = up_gb
    big[:, pl.ds(pl.multiple_of(2 * ff + j * block, PAD), block)] = hidden
    acc[...] += dot(gate_gb, wg[...], NT) + dot(up_gb, wu[...], NT)

    @pl.when(j == pl.num_programs(0) - 1)
    def _():
        for k in range(n):
            pieces[k][...] = acc[:, ds(rot_index(idx[3], k, n), part)].astype(bf16)


def down_kernel(dims, idx, hidden, wd, *refs):
    n = dims[3]
    part = wd.shape[0] // n
    for k in range(n):
        rows = ds(rot_index(idx[3], k, n), part)
        refs[k][...] = dot(hidden[...], wd[rows, :], NT).astype(bf16)


def ffn_grad_kernel(dims, own, idx, normed, cot_rel, big, keep, send, normed_rel, turned):
    j = pl.program_id(0)

    @pl.when(j == 0)
    def _():
        turned[...] = normed[...].T
        store_relative(dims, idx, normed_rel, turned, own)

    half = keep.shape[0]
    of_down = j * 3 >= pl.num_programs(0) * 2

    def write(left):
        out = dot(left[...], big[...]).astype(bf16)
        keep[...] = out[:half]
        send[...] = out[half:]

    pl.when(jnp.logical_not(of_down))(lambda: write(normed_rel))
    pl.when(of_down)(lambda: write(cot_rel))


def attend_back_kernel(dims, own, qc, kc, oc, idx, middle, gains, cot, *refs):
    nx, nz, nc, n = dims
    grads = refs[:n]
    w_low, w_high, attn_t, q_t, raw_t, kv, log_total, gq, cosine, sine = refs[n : n + 10]
    mine, rel, gain_two, q_gb, gq_grad, kv_keep, kv_send = refs[n + 10 : n + 17]
    full, turned, dq, do_t, delta, mid_grad = refs[n + 17 :]
    span = q_t.shape[1]
    me = idx[1] * nc + idx[2]
    heads, kv_heads = qc // HD, kc // HD
    group = heads // kv_heads
    assemble(idx, n, grads, full)
    m = middle[...]
    r = lax.rsqrt(jnp.mean(m * m, axis=1, keepdims=True) + EPS)
    unit = m * r
    ng = full[...].astype(f32)
    gain_two[...] = jnp.broadcast_to(jnp.sum(ng * unit, axis=0, keepdims=True), gain_two.shape)
    gg = ng * gains[1:2, :]
    mg = cot[...].astype(f32) + r * (gg - unit * jnp.mean(gg * unit, axis=1, keepdims=True))
    mid_grad[...] = mg
    part = grads[0].shape[1]
    mine[...] = mid_grad[:, ds(idx[3], part)]
    mgb = mg.astype(bf16)
    turned[...] = mgb.T
    store_relative(dims, idx, rel, turned, own)
    ag = jnp.concatenate([dot(mgb, w_low[...]), dot(mgb, w_high[...])], axis=1)
    do = ag.astype(bf16)
    ag_t = ag.T
    do_t[...] = ag_t.astype(bf16)
    prod = ag_t * attn_t[...]
    for h in range(heads):
        delta[h : h + 1, :] = jnp.sum(prod[h * HD : (h + 1) * HD], axis=0, keepdims=True)
    q = q_t[...].T
    dq[...] = jnp.zeros_like(dq)
    keys_at = lax.broadcasted_iota(jnp.int32, (span, span), 0)
    query_at = lax.broadcasted_iota(jnp.int32, (span, span), 1)
    for other, out in enumerate((kv_keep, kv_send)):
        core = idx[2] if other == 0 else 1 - idx[2]

        def step(zr, carry, out=out, core=core):
            j = rot_index(idx[1], zr, nz) * nc + core
            at = ds(zr, span)

            @pl.when(j > me)
            def _():
                out[at, :] = jnp.zeros((span, 2 * kc), bf16)

            @pl.when(j <= me)
            def _():
                kb = kv[ds(j, span), :kc]
                vb = kv[ds(j, span), kc:]
                kt = kb.T
                allowed = keys_at + j * span <= query_at + me * span
                for g in range(kv_heads):
                    cols = slice(g * HD, (g + 1) * HD)
                    dk = jnp.zeros((span, HD), f32)
                    dv = jnp.zeros((span, HD), f32)
                    for h in range(g * group, (g + 1) * group):
                        rows = slice(h * HD, (h + 1) * HD)
                        s = dot(kb[:, cols], q_t[rows, :])
                        p = jnp.where(allowed, jnp.exp(s * SCALE - log_total[h : h + 1, :]), 0.0)
                        dp = dot(vb[:, cols], do_t[rows, :])
                        sg = (p * (dp - delta[h : h + 1, :])).astype(bf16)
                        dq[rows, :] += dot(kt[cols], sg)
                        dk = dk + dot(sg, q[:, rows])
                        dv = dv + dot(p.astype(bf16), do[:, rows])
                    out[at, g * HD : (g + 1) * HD] = (dk * SCALE).astype(bf16)
                    out[at, kc + g * HD : kc + (g + 1) * HD] = dv.astype(bf16)

            return carry

        lax.fori_loop(0, nz, step, 0)
    raw_grad, gain_grad = turn_heads_back(
        raw_t[:qc, :], dq[...] * SCALE, gq[...], cosine[...], sine[...], heads
    )
    gq_grad[...] = gain_grad
    q_gb[...] = raw_grad.T.astype(bf16)


def input_grad_kernel(dims, qc, kc, idx, *refs):
    n, nz = dims[3], dims[1]
    kv_parts = refs[:nz]
    raw_t, gk, cosine, sine, q_gb, w, base, gains = refs[nz : nz + 8]
    qkv_gb, gain_one, gk_grad = refs[nz + 8 : nz + 11]
    pieces = refs[nz + 11 : nz + 11 + n]
    acc = refs[nz + 11 + n]
    total = kv_parts[0][...].astype(f32)
    for k in range(1, nz):
        total = total + kv_parts[k][...].astype(f32)
    raw_grad, gain_grad = turn_heads_back(
        raw_t[qc:, :], total[:, :kc].T, gk[...], cosine[...], sine[...], kc // HD
    )
    gk_grad[...] = gain_grad
    qkv_gb[:, :qc] = q_gb[...]
    qkv_gb[:, qc : qc + kc] = raw_grad.T.astype(bf16)
    qkv_gb[:, qc + kc :] = total[:, kc:].astype(bf16)
    ng = dot(qkv_gb[...], w[:, : qc + 2 * kc], NT)
    acc[...] = ng
    b = base[...].astype(f32)
    unit = b * lax.rsqrt(jnp.mean(b * b, axis=1, keepdims=True) + EPS)
    prod = ng * unit
    gain_one[...] = jnp.broadcast_to(jnp.sum(prod, axis=0, keepdims=True), gain_one.shape)
    along = jnp.sum(prod * gains[0:1, :], axis=1, keepdims=True)
    along = jnp.broadcast_to(along, (along.shape[0], PAD)).T[:16]
    high = along.astype(bf16)
    low = (along - high.astype(f32)).astype(bf16)
    row = lax.broadcasted_iota(jnp.int32, along.shape, 0)
    tail = jnp.where(row == 0, high.astype(f32), low.astype(f32)).astype(bf16)
    part = acc.shape[1] // n
    for k in range(n):
        pieces[k][: along.shape[1], :] = acc[:, ds(rot_index(idx[3], k, n), part)].astype(bf16)
        pieces[k][along.shape[1] :, :] = tail


def attn_grad_kernel(dims, own, qc, kc, oc, idx, one_rel, mid_rel, qkv_gb, attn_b, gain_one, gain_two, gq_grad, gk_grad, keep, send, extra, extra_rel):
    half = keep.shape[0]
    qkv = qc + 2 * kc
    width = one_rel.shape[0]

    def halves(v):
        high = v.astype(bf16).astype(f32)
        return high, v - high

    rows = lax.broadcasted_iota(jnp.int32, (PAD, width), 0)
    lines = jnp.zeros((PAD, width), f32)
    values = halves(gain_one[0:1, :]) + halves(gain_two[0:1, :])
    for i, v in enumerate(values):
        lines = lines + jnp.where(rows == i, v, 0.0)
    cols = lines.T
    heads = jnp.concatenate([gq_grad[...], gk_grad[...]], axis=0)
    high, low = halves(heads)
    lane = lax.broadcasted_iota(jnp.int32, (own, PAD), 1)
    tile = jnp.zeros((own, PAD), f32)
    count = 2 * HD // own
    for i in range(count):
        at = slice(i * own, (i + 1) * own)
        tile = tile + jnp.where(lane == 4 + i, high[at], 0.0)
        tile = tile + jnp.where(lane == 4 + count + i, low[at], 0.0)
    for i in range(width // own):
        extra[i * own : (i + 1) * own, :] = (cols[i * own : (i + 1) * own] + tile).astype(bf16)
    store_relative(dims, idx, extra_rel, extra, own)
    a = dot(one_rel[...], qkv_gb[...]).astype(bf16)
    b = dot(mid_rel[...], attn_b[...]).astype(bf16)
    for out, at in ((keep, slice(0, half)), (send, slice(half, 2 * half))):
        out[:, :qkv] = a[at]
        out[:, qkv : qkv + oc] = b[at]
        out[:, qkv + oc :] = extra_rel[at, :]


def core_sum(keep, send, n):
    got = shift(send, "core", 1)
    step = keep.shape[0] // n
    return [
        (keep[k * step : (k + 1) * step].astype(f32) + got[k * step : (k + 1) * step].astype(f32)).astype(bf16)
        for k in range(n)
    ]


def row_sum(x, axis):
    step = x.shape[0] // lax.axis_size(axis)
    return summed([x[k * step : (k + 1) * step] for k in range(lax.axis_size(axis))], axis)


def after(values, others):
    return lax.optimization_barrier((list(values), others))[0]


def body(
    block_input,
    attn_gain,
    ffn_gain,
    query_gain,
    key_gain,
    query_weight,
    key_weight,
    value_weight,
    out_weight,
    gate_weight,
    up_weight,
    down_weight,
    cotangent,
):
    span, seq_local, part = block_input.shape
    axes = ("dp", "z", "core", "tensor")
    dims = tuple(lax.axis_size(a) for a in axes)
    nx, nz, nc, n = dims
    idx = jnp.stack([lax.axis_index(a) for a in axes]).astype(jnp.int32)
    width = part * n
    own = query_weight.shape[0]
    qc, kc, oc, ff = (w.shape[1] for w in (query_weight, key_weight, out_weight, gate_weight))
    qkv = qc + 2 * kc
    aw = qkv + oc + PAD

    ffn_local = jnp.concatenate([gate_weight, up_weight, down_weight, out_weight], axis=1)
    ffn_w = lax.all_gather(ffn_local, ("dp", "z", "core"), axis=0, tiled=True)

    gains_local = jnp.pad(jnp.stack([attn_gain, ffn_gain], axis=1), ((0, 0), (0, PAD - 2)))
    attn_local = jnp.concatenate([query_weight, key_weight, value_weight, gains_local], axis=1)
    by_z = jnp.concatenate(gathered(attn_local, "z"), axis=0)
    both = jnp.concatenate([block_input.reshape(span, part), cotangent.reshape(span, part)], axis=1)
    both_parts = gathered(both, "tensor")
    w_own = jnp.concatenate(gathered(by_z, "dp"), axis=0)
    cot, cot_rel = call(
        functools.partial(cot_kernel, dims, own),
        [sds((span, width), bf16), sds((width, span), bf16)],
        [idx] + both_parts,
        [pltpu.VMEM((width, span), bf16)],
    )
    w_own, (cot, cot_rel) = lax.optimization_barrier((w_own, (cot, cot_rel)))
    w_partner = shift(w_own, "core", 1)

    my_first = (idx[1] * nc + idx[2]) * span
    positions = (my_first + jnp.arange(span, dtype=jnp.int32)).astype(f32)
    frequency = jnp.power(ROPE_BASE, -2.0 * jnp.arange(HALF, dtype=f32) / HD)
    angle = frequency[:, None] * positions[None, :]
    cosine, sine = jnp.cos(angle), jnp.sin(angle)
    gq = query_gain.astype(f32)[:, None]
    gk = key_gain.astype(f32)[:, None]

    w, base, gains, q_t, raw_t, kv, one_rel = call(
        functools.partial(qkv_kernel, dims, own, qc, kc, oc),
        [
            sds((width, qkv + PAD), bf16),
            sds((span, width), bf16),
            sds((8, width), f32),
            sds((qc, span), bf16),
            sds((qc + kc, span), f32),
            sds((span, 2 * kc), bf16),
            sds((width, span), bf16),
        ],
        [idx] + both_parts + [w_own, w_partner, gq, gk, cosine, sine],
        [pltpu.VMEM((width, span), bf16)],
        flops=2 * span * width * qkv,
    )
    kv_own = jnp.concatenate(gathered(kv, "z"), axis=0)
    kv_partner = shift(kv_own, "core", 1)

    length = span * nz * nc
    block = 384
    const = lambda s: pl.BlockSpec(s, lambda j: (0, 0))
    steps = ff // block
    out_blocks = [pl.BlockSpec((width, PAD), lambda j, o=o: (0, o)) for o in (3 * ff // PAD, 3 * ff // PAD + 1)]
    res = call(
        functools.partial(attend_kernel, dims, qc, kc, oc),
        [
            sds((length, 2 * kc), bf16),
            sds((qc, span), f32),
            sds((span, qc), bf16),
            sds((8, span), f32),
        ]
        + [sds((span, part), bf16)] * n,
        [idx, q_t, kv_own, kv_partner, ffn_w, ffn_w],
        [pltpu.VMEM((qc, span), f32), pltpu.VMEM((8, span), f32)],
        grid=(1,),
        in_specs=[pl.BlockSpec(memory_space=pltpu.SMEM), const((qc, span)), const((length // 2, 2 * kc)), const((length // 2, 2 * kc))]
        + out_blocks,
        out_specs=[const((length, 2 * kc)), const((qc, span)), const((span, qc)), const((8, span))]
        + [const((span, part))] * n,
        flops=4 * span * length * qc,
    )
    kv_full, attn_t, attn_b, log_total = res[:4]
    attn_mine = summed(res[4:], "tensor").astype(bf16)
    attn_parts = gathered(attn_mine, "tensor")

    res = call(
        functools.partial(ffn_kernel, dims, own),
        [sds((span, width), f32), sds((span, width), bf16), sds((span, 3 * ff), bf16)]
        + [sds((span, part), bf16)] * n,
        [idx, base, gains, cot] + attn_parts + [ffn_w] * 3,
        [pltpu.VMEM((span, width), f32)],
        grid=(steps,),
        in_specs=[pl.BlockSpec(memory_space=pltpu.SMEM)]
        + [const((span, width)), const((8, width)), const((span, width))]
        + [const((span, part))] * n
        + [pl.BlockSpec((width, block), lambda j, o=o: (0, o + j)) for o in (0, steps, 2 * steps)],
        out_specs=[const((span, width)), const((span, width)), const((span, 3 * ff))]
        + [const((span, part))] * n,
        flops=10 * span * width * ff,
    )
    middle, normed_two, big = res[:3]
    grad_mine = summed(res[3:], "tensor").astype(bf16)
    grad_parts = gathered(grad_mine, "tensor")

    ffn_keep, ffn_send = call(
        functools.partial(ffn_grad_kernel, dims, own),
        [sds((width // 2, 3 * ff), bf16)] * 2,
        [idx, normed_two, cot_rel, big],
        [pltpu.VMEM((width, span), bf16)] * 2,
        grid=(3 * steps,),
        in_specs=[pl.BlockSpec(memory_space=pltpu.SMEM), const((span, width)), const((width, span)), pl.BlockSpec((span, block), lambda j: (0, j))],
        out_specs=[pl.BlockSpec((width // 2, block), lambda j: (0, j))] * 2,
        flops=6 * span * width * ff,
    )
    ffn_pieces = core_sum(ffn_keep, ffn_send, nx)
    ffn_x = summed(ffn_pieces, "dp").astype(bf16)

    down_parts = call(
        functools.partial(down_kernel, dims),
        [sds((span, part), bf16)] * n,
        [idx, big, ffn_w],
        grid=(1,),
        in_specs=[
            pl.BlockSpec(memory_space=pltpu.SMEM),
            pl.BlockSpec((span, ff), lambda j: (0, 2)),
            pl.BlockSpec((width, ff), lambda j: (0, 2)),
        ],
        out_specs=[const((span, part))] * n,
        flops=2 * span * width * ff,
    )
    me_t = idx[3]
    middle_mine = lax.dynamic_slice_in_dim(middle, me_t * part, part, 1)
    block_output = (middle_mine + summed(down_parts, "tensor")).astype(bf16)

    mine, mid_rel, gain_two, q_gb, gq_grad, kv_keep, kv_send = call(
        functools.partial(attend_back_kernel, dims, own, qc, kc, oc),
        [
            sds((span, part), f32),
            sds((width, span), bf16),
            sds((8, width), f32),
            sds((span, qc), bf16),
            sds((HD, 1), f32),
            sds((length // 2, 2 * kc), bf16),
            sds((length // 2, 2 * kc), bf16),
        ],
        [idx, middle, gains, cot] + grad_parts + [ffn_w, ffn_w, attn_t, q_t, raw_t, kv_full, log_total, gq, cosine, sine],
        [
            pltpu.VMEM((span, width), bf16),
            pltpu.VMEM((width, span), bf16),
            pltpu.VMEM((qc, span), f32),
            pltpu.VMEM((qc, span), bf16),
            pltpu.VMEM((8, span), f32),
            pltpu.VMEM((span, width), f32),
        ],
        grid=(1,),
        in_specs=[pl.BlockSpec(memory_space=pltpu.SMEM), const((span, width)), const((8, width)), const((span, width))]
        + [const((span, part))] * n
        + out_blocks
        + [const(v.shape) for v in (attn_t, q_t, raw_t, kv_full, log_total, gq, cosine, sine)],
        out_specs=[
            const((span, part)),
            const((width, span)),
            const((8, width)),
            const((span, qc)),
            const((HD, 1)),
            const((length // 2, 2 * kc)),
            const((length // 2, 2 * kc)),
        ],
        flops=10 * span * length * qc,
    )
    kv_pieces = core_sum(kv_keep, kv_send, nz)
    kv_parts = [kv_pieces[0]] + [shift(kv_pieces[k], "z", k) for k in range(1, nz)]
    kv_parts, ffn_x = lax.optimization_barrier((kv_parts, ffn_x))

    res = call(
        functools.partial(input_grad_kernel, dims, qc, kc),
        [sds((span, qkv), bf16), sds((8, width), f32), sds((HD, 1), f32)]
        + [sds((span + 16, part), bf16)] * n,
        [idx] + kv_parts + [raw_t, gk, cosine, sine, q_gb, w, base, gains],
        [pltpu.VMEM((span, width), f32)],
        flops=2 * span * width * qkv,
    )
    qkv_gb, gain_one, gk_grad = res[:3]
    norm_mine = summed(res[3:], "tensor")
    along = (norm_mine[span] + norm_mine[span + 1])[:, None] * (1.0 / width)
    base_f = base.astype(f32)
    scale_one = lax.rsqrt(jnp.mean(base_f * base_f, axis=1, keepdims=True) + EPS)
    unit_mine = block_input.reshape(span, part).astype(f32) * scale_one
    gain_mine = lax.dynamic_slice_in_dim(gains, me_t * part, part, 1)[0:1]
    input_grad = (mine + scale_one * (norm_mine[:span] * gain_mine - unit_mine * along)).astype(bf16)

    keep, send = call(
        functools.partial(attn_grad_kernel, dims, own, qc, kc, oc),
        [sds((width // 2, aw), bf16)] * 2,
        [idx, one_rel, mid_rel, qkv_gb, attn_b, gain_one, gain_two, gq_grad, gk_grad],
        [pltpu.VMEM((width, PAD), bf16), pltpu.VMEM((width, PAD), bf16)],
        flops=2 * span * width * (qkv + oc),
    )
    (keep, send), ffn_x = lax.optimization_barrier(((keep, send), ffn_x))
    ffn_sum = row_sum(ffn_x, "z")
    attn_x = summed(core_sum(keep, send, nx), "dp").astype(bf16)
    attn_sum = row_sum(attn_x, "z")
    small = attn_sum[:, qkv + oc :]
    small_all = sum(gathered(small, "tensor"))
    count = 2 * HD // own
    head_sum = (small_all[:, 4 : 4 + count] + small_all[:, 4 + count : 4 + 2 * count]).T.reshape(-1)
    return (
        block_output.reshape(span, seq_local, part),
        input_grad.reshape(span, seq_local, part),
        small_all[:, 0] + small_all[:, 1],
        small[:, 2] + small[:, 3],
        head_sum[:HD],
        head_sum[HD:],
        attn_sum[:, :qc],
        attn_sum[:, qc : qc + kc],
        attn_sum[:, qc + kc : qkv],
        attn_sum[:, qkv : qkv + oc],
        ffn_sum[:, :ff],
        ffn_sum[:, ff : 2 * ff],
        ffn_sum[:, 2 * ff :],
    )


def solution(mesh):
    dp, seq, tensor = (mesh.shape[a] for a in ("dp", "seq", "tensor"))
    grid = Mesh(
        np.asarray(mesh.devices).reshape(dp, seq // 2, 2, tensor), ("dp", "z", "core", "tensor")
    )
    tokens = P(("z", "core"), "dp", "tensor")
    rows = P(("dp", "z", "core"))
    weight = P(("dp", "z", "core"), "tensor")
    return jax.shard_map(
        body,
        mesh=grid,
        in_specs=(tokens, rows, rows, P(), P()) + (weight,) * 7 + (tokens,),
        out_specs=(tokens, tokens, rows, rows, P(), P()) + (weight,) * 7,
        check_vma=False,
    )
```

```python
import functools

import numpy as np
import jax
import jax.numpy as jnp
from jax import lax
from jax.experimental import pallas as pl
from jax.experimental.pallas import tpu as pltpu
from jax.sharding import Mesh, PartitionSpec as P

HD = 64
HALF = HD // 2
EPS = 1e-05
ROPE_BASE = 1000000.0
SCALE = HD ** (-0.5)
PAD = 128
bf16 = jnp.bfloat16
f32 = jnp.float32
NN = (((1,), (0,)), ((), ()))
NT = (((1,), (1,)), ((), ()))


def dot(a, b, dims=NN):
    return lax.dot_general(a, b, dims, preferred_element_type=f32)


def rot_index(a, k, n):
    return lax.rem(a + k, n)


def ds(start, size):
    return pl.ds(pl.multiple_of(start * size, size), size)


def shift(x, axis, k):
    n = lax.axis_size(axis)
    return lax.ppermute(x, axis, [(i, (i + k) % n) for i in range(n)])


def gathered(x, axis):
    return [x] + [shift(x, axis, k) for k in range(1, lax.axis_size(axis))]


def summed(pieces, axis):
    total = pieces[0].astype(f32)
    for k in range(1, lax.axis_size(axis)):
        total = total + shift(pieces[k], axis, k).astype(f32)
    return total


def call(kernel, outs, ins, scratch=(), grid=None, in_specs=None, out_specs=None, flops=0):
    vm = pl.BlockSpec(memory_space=pltpu.VMEM)
    nbytes = sum(x.size * x.dtype.itemsize for x in list(ins) + list(outs))
    kwargs = {} if grid is None else {"grid": grid}
    return pl.pallas_call(
        kernel,
        out_shape=outs,
        in_specs=in_specs or [pl.BlockSpec(memory_space=pltpu.SMEM)] + [vm] * (len(ins) - 1),
        out_specs=out_specs or [vm] * len(outs),
        scratch_shapes=list(scratch),
        cost_estimate=pl.CostEstimate(flops=flops, bytes_accessed=nbytes, transcendentals=0),
        **kwargs,
    )(*ins)


def sds(shape, dtype):
    return jax.ShapeDtypeStruct(shape, dtype)


def store_relative(dims, idx, dst, src, own):
    nx, nz, nc, _ = dims
    x, z, c = idx[0], idx[1], idx[2]
    at = 0
    for other in range(nc):
        core = c if other == 0 else 1 - c
        for xr in range(nx):
            for zr in range(nz):
                row = (rot_index(x, xr, nx) * nz + rot_index(z, zr, nz)) * nc + core
                dst[at * own : (at + 1) * own, :] = src[ds(row, own), :]
                at += 1


def assemble(idx, n, pieces, dst, first=0):
    part = dst.shape[1] // n
    for k in range(n):
        dst[:, ds(rot_index(idx[3], n - k, n), part)] = pieces[k][:, first : first + part]


def cot_kernel(dims, idx, *refs):
    n = dims[3]
    pieces, (full, turned) = refs[:n], refs[n:]
    assemble(idx, n, pieces, full, full.shape[1] // n)
    turned[...] = full[...].T


def head_columns(ref):
    turned = jnp.broadcast_to(ref[...].astype(f32), (8, 2 * HD)).T
    return turned[:HD, :1], turned[HD:, :1]


def to_groups(dst, rows):
    span = rows.shape[1]
    group = dst.shape[1] // span
    for h in range(rows.shape[0] // HD):
        g, at = h // group, h % group
        dst[g * HD : (g + 1) * HD, at * span : (at + 1) * span] = rows[h * HD : (h + 1) * HD]


def from_groups(x, span):
    group = x.shape[1] // span
    return jnp.concatenate(
        [
            x[h // group * HD : (h // group + 1) * HD, h % group * span : (h % group + 1) * span]
            for h in range(x.shape[0] // HD * group)
        ],
        axis=0,
    )


def turn_heads(raw, gain, cosine, sine, heads):
    outs = []
    for h in range(heads):
        v = raw[h * HD : (h + 1) * HD]
        v = v * lax.rsqrt(jnp.mean(v * v, axis=0, keepdims=True) + EPS) * gain
        a, b = v[:HALF], v[HALF:]
        outs += [a * cosine - b * sine, b * cosine + a * sine]
    return jnp.concatenate(outs, axis=0)


def turn_heads_back(raw, grad, gain, cosine, sine, heads):
    outs, gain_grad = [], jnp.zeros((HD, 1), f32)
    for h in range(heads):
        v = raw[h * HD : (h + 1) * HD]
        g = grad[h * HD : (h + 1) * HD]
        ga, gb = g[:HALF], g[HALF:]
        g = jnp.concatenate([ga * cosine + gb * sine, gb * cosine - ga * sine], axis=0)
        r = lax.rsqrt(jnp.mean(v * v, axis=0, keepdims=True) + EPS)
        n = v * r
        gain_grad = gain_grad + jnp.sum(g * n, axis=1, keepdims=True)
        g = g * gain
        outs.append(r * (g - n * jnp.mean(g * n, axis=0, keepdims=True)))
    return jnp.concatenate(outs, axis=0), gain_grad


def qkv_kernel(dims, own, qc, kc, oc, idx, *refs):
    nx, nz, nc, n = dims
    pieces = refs[:n]
    w_own, w_partner, head_gains, cosine, sine = refs[n : n + 5]
    w, base, gains, q_t, raw_t, kv, rel, turned = refs[n + 5 :]
    gq, gk = head_columns(head_gains)
    assemble(idx, n, pieces, base)
    for other, src in enumerate((w_own, w_partner)):
        core = idx[2] if other == 0 else 1 - idx[2]
        for zr in range(nz):
            for xr in range(nx):
                row = (rot_index(idx[0], nx - xr, nx) * nz + rot_index(idx[1], nz - zr, nz)) * nc + core
                at = xr * nz + zr
                w[ds(row, own), :] = src[at * own : (at + 1) * own, :]
    qkv = qc + 2 * kc
    gains[...] = w[:, qkv:].astype(f32).T[:8]
    b = base[...].astype(f32)
    normed = b * lax.rsqrt(jnp.mean(b * b, axis=1, keepdims=True) + EPS) * gains[0:1, :]
    normed = normed.astype(bf16)
    raw = dot(normed, w[:, :qkv])
    turned[...] = normed.T
    store_relative(dims, idx, rel, turned, own)
    kv[:, kc:] = raw[:, qc + kc :].astype(bf16)
    rt = raw[:, : qc + kc].T
    raw_t[...] = rt
    co, si = cosine[...], sine[...]
    q = (turn_heads(rt[:qc], gq, co, si, qc // HD) * SCALE).astype(bf16)
    to_groups(q_t, q)
    kv[:, :kc] = turn_heads(rt[qc:], gk, co, si, kc // HD).T.astype(bf16)


def attend_kernel(dims, qc, kc, oc, idx, q_t, kv_own, kv_partner, kv, attn_t, attn_b, log_total, acc, tot):
    nx, nz, nc, n = dims
    span = attn_b.shape[0]
    group = qc // kc
    me = idx[1] * nc + idx[2]
    for other, src in enumerate((kv_own, kv_partner)):
        core = idx[2] if other == 0 else 1 - idx[2]
        for zr in range(nz):
            block = rot_index(idx[1], nz - zr, nz) * nc + core
            kv[ds(block, span), :] = src[zr * span : (zr + 1) * span, :]
    acc[...] = jnp.zeros_like(acc)
    tot[...] = jnp.zeros_like(tot)
    keys_at = lax.broadcasted_iota(jnp.int32, (span, span), 0)
    query_at = lax.broadcasted_iota(jnp.int32, (span, span), 1)
    ahead = keys_at - query_at
    ahead = jnp.concatenate([ahead] * group, axis=1)

    def step(j, carry):
        vt = kv[ds(j, span), kc:].T
        allowed = ahead <= (me - j) * span
        for g in range(kc // HD):
            rows = slice(g * HD, (g + 1) * HD)
            s = dot(kv[ds(j, span), rows], q_t[rows, :])
            e = jnp.where(allowed, jnp.exp(s), 0.0)
            tot[g : g + 1, :] += jnp.sum(e, axis=0, keepdims=True)
            acc[rows, :] += dot(vt[rows], e.astype(bf16))
        return carry

    lax.fori_loop(0, me + 1, step, 0)
    for g in range(kc // HD):
        rows = slice(g * HD, (g + 1) * HD)
        attn_t[rows, :] = acc[rows, :] / tot[g : g + 1, :]
    log_total[...] = jnp.log(jnp.maximum(tot[...], 1e-30))
    attn = from_groups(attn_t[...], span).T.astype(bf16)
    attn_b[...] = attn


def out_kernel(dims, idx, attn_b, w_low, w_high, *pieces):
    n = dims[3]
    attn = attn_b[...]
    part = w_low.shape[0] // n
    for k in range(n):
        rows = ds(rot_index(idx[3], k, n), part)
        out = dot(attn[:, :PAD], w_low[rows, :], NT) + dot(attn[:, PAD:], w_high[rows, :], NT)
        pieces[k][...] = out.astype(bf16)


def hidden_grad_kernel(cot, wd, out):
    out[...] = dot(cot[...], wd[...])


def ffn_kernel(dims, own, idx, base, gains, *refs):
    n = dims[3]
    sums = refs[:n]
    wg, wu, hgrad = refs[n : n + 3]
    middle, normed, big = refs[n + 3 : n + 6]
    pieces = refs[n + 6 : n + 6 + n]
    acc = refs[n + 6 + n]
    j = pl.program_id(0)
    part = sums[0].shape[1]

    @pl.when(j == 0)
    def _():
        for k in range(n):
            at = ds(rot_index(idx[3], n - k, n), part)
            middle[:, at] = base[:, at].astype(f32) + sums[k][...].astype(f32)
        m = middle[...]
        v = m * lax.rsqrt(jnp.mean(m * m, axis=1, keepdims=True) + EPS) * gains[1:2, :]
        v = v.astype(bf16)
        normed[...] = v
        acc[...] = jnp.zeros_like(acc)

    v = normed[...]
    block = wg.shape[1]
    ff = big.shape[1] // 3
    gate = dot(v, wg[...])
    up = dot(v, wu[...])
    hg = hgrad[...]
    sig = 1.0 / (1.0 + jnp.exp(-gate))
    act = gate * sig
    hidden = (act * up).astype(bf16)
    gate_gb = (hg * up * (sig + act * (1.0 - sig))).astype(bf16)
    up_gb = (hg * act).astype(bf16)
    big[:, pl.ds(pl.multiple_of(j * block, block), block)] = gate_gb
    big[:, pl.ds(pl.multiple_of(ff + j * block, PAD), block)] = up_gb
    big[:, pl.ds(pl.multiple_of(2 * ff + j * block, PAD), block)] = hidden
    acc[...] += dot(gate_gb, wg[...], NT) + dot(up_gb, wu[...], NT)

    @pl.when(j == pl.num_programs(0) - 1)
    def _():
        for k in range(n):
            pieces[k][...] = acc[:, ds(rot_index(idx[3], k, n), part)].astype(bf16)


def down_kernel(dims, idx, hidden, wd, *refs):
    n = dims[3]
    part = wd.shape[0] // n
    for k in range(n):
        rows = ds(rot_index(idx[3], k, n), part)
        refs[k][...] = dot(hidden[...], wd[rows, :], NT).astype(bf16)


def ffn_grad_kernel(normed, cot_t, big, out, turned):
    j = pl.program_id(0)

    @pl.when(j == 0)
    def _():
        turned[...] = normed[...].T

    @pl.when(j < 2)
    def _():
        out[...] = dot(turned[...], big[...]).astype(bf16)

    @pl.when(j == 2)
    def _():
        out[...] = dot(cot_t[...], big[...]).astype(bf16)


def attend_back_kernel(dims, own, qc, kc, oc, idx, middle, gains, cot, *refs):
    nx, nz, nc, n = dims
    grads = refs[:n]
    w_low, w_high, attn_t, q_t, raw_t, kv, log_total, head_gains, cosine, sine = refs[n : n + 10]
    mine, rel, gain_two, q_gb, gq_grad, kv_keep, kv_send = refs[n + 10 : n + 17]
    full, turned, dq, do_t, delta, mid_grad, do_f, q_n, do_n = refs[n + 17 :]
    span = mine.shape[0]
    group = qc // kc
    me = idx[1] * nc + idx[2]
    assemble(idx, n, grads, full)
    m = middle[...]
    r = lax.rsqrt(jnp.mean(m * m, axis=1, keepdims=True) + EPS)
    unit = m * r
    ng = full[...].astype(f32)
    gain_two[...] = jnp.broadcast_to(jnp.sum(ng * unit, axis=0, keepdims=True), gain_two.shape)
    gg = ng * gains[1:2, :]
    mg = cot[...].astype(f32) + r * (gg - unit * jnp.mean(gg * unit, axis=1, keepdims=True))
    mid_grad[...] = mg
    part = grads[0].shape[1]
    mine[...] = mid_grad[:, ds(idx[3], part)]
    mgb = mg.astype(bf16)
    turned[...] = mgb.T
    store_relative(dims, idx, rel, turned, own)
    ag = jnp.concatenate([dot(mgb, w_low[...]), dot(mgb, w_high[...])], axis=1)
    to_groups(do_f, ag.T)
    prod = do_f[...] * attn_t[...]
    do_t[...] = do_f[...].astype(bf16)
    for g in range(kc // HD):
        rows = slice(g * HD, (g + 1) * HD)
        delta[g : g + 1, :] = jnp.sum(prod[rows], axis=0, keepdims=True)
        q_n[g * q_t.shape[1] : (g + 1) * q_t.shape[1], :] = q_t[rows, :].T
        do_n[g * q_t.shape[1] : (g + 1) * q_t.shape[1], :] = do_t[rows, :].T
    dq[...] = jnp.zeros_like(dq)
    keys_at = lax.broadcasted_iota(jnp.int32, (span, span), 0)
    query_at = lax.broadcasted_iota(jnp.int32, (span, span), 1)
    ahead = keys_at - query_at
    ahead = jnp.concatenate([ahead] * group, axis=1)
    for other, out in enumerate((kv_keep, kv_send)):
        core = idx[2] if other == 0 else 1 - idx[2]

        def step(zr, carry, out=out, core=core):
            j = rot_index(idx[1], zr, nz) * nc + core
            at = ds(zr, span)

            @pl.when(j > me)
            def _():
                out[at, :] = jnp.zeros((span, 2 * kc), bf16)

            @pl.when(j <= me)
            def _():
                kt = kv[ds(j, span), :kc].T
                allowed = ahead <= (me - j) * span
                wide = q_t.shape[1]
                for g in range(kc // HD):
                    rows = slice(g * HD, (g + 1) * HD)
                    s = dot(kv[ds(j, span), rows], q_t[rows, :])
                    p = jnp.where(allowed, jnp.exp(s - log_total[g : g + 1, :]), 0.0)
                    dp = dot(kv[ds(j, span), kc + g * HD : kc + (g + 1) * HD], do_t[rows, :])
                    sg = (p * (dp - delta[g : g + 1, :])).astype(bf16)
                    dq[rows, :] += dot(kt[rows], sg)
                    dk = dot(sg, q_n[g * wide : (g + 1) * wide, :])
                    dv = dot(p.astype(bf16), do_n[g * wide : (g + 1) * wide, :])
                    out[at, rows] = dk.astype(bf16)
                    out[at, kc + g * HD : kc + (g + 1) * HD] = dv.astype(bf16)

            return carry

        lax.fori_loop(0, nz, step, 0)
    raw_grad, gain_grad = turn_heads_back(
        raw_t[:qc, :], from_groups(dq[...], span) * SCALE, head_columns(head_gains)[0], cosine[...], sine[...], qc // HD
    )
    gq_grad[...] = gain_grad
    q_gb[...] = raw_grad.T.astype(bf16)


def input_grad_kernel(dims, qc, kc, idx, *refs):
    n, nz = dims[3], dims[1]
    kv_parts = refs[:nz]
    raw_t, head_gains, cosine, sine, q_gb, w, base, gains = refs[nz : nz + 8]
    qkv_gb, gain_one, gk_grad = refs[nz + 8 : nz + 11]
    pieces = refs[nz + 11 : nz + 11 + n]
    acc = refs[nz + 11 + n]
    total = kv_parts[0][...].astype(f32)
    for k in range(1, nz):
        total = total + kv_parts[k][...].astype(f32)
    raw_grad, gain_grad = turn_heads_back(
        raw_t[qc:, :], total[:, :kc].T, head_columns(head_gains)[1], cosine[...], sine[...], kc // HD
    )
    gk_grad[...] = gain_grad
    qkv_gb[:, :qc] = q_gb[...]
    qkv_gb[:, qc : qc + kc] = raw_grad.T.astype(bf16)
    qkv_gb[:, qc + kc :] = total[:, kc:].astype(bf16)
    ng = dot(qkv_gb[...], w[:, : qc + 2 * kc], NT)
    acc[...] = ng
    b = base[...].astype(f32)
    unit = b * lax.rsqrt(jnp.mean(b * b, axis=1, keepdims=True) + EPS)
    prod = ng * unit
    gain_one[...] = jnp.broadcast_to(jnp.sum(prod, axis=0, keepdims=True), gain_one.shape)
    along = jnp.sum(prod * gains[0:1, :], axis=1, keepdims=True)
    along = jnp.broadcast_to(along, (along.shape[0], PAD)).T[:16]
    high = along.astype(bf16)
    low = (along - high.astype(f32)).astype(bf16)
    row = lax.broadcasted_iota(jnp.int32, along.shape, 0)
    tail = jnp.where(row == 0, high.astype(f32), low.astype(f32)).astype(bf16)
    part = acc.shape[1] // n
    for k in range(n):
        pieces[k][: along.shape[1], :] = acc[:, ds(rot_index(idx[3], k, n), part)].astype(bf16)
        pieces[k][along.shape[1] :, :] = tail


def attn_grad_kernel(dims, own, qc, kc, oc, idx, one_rel, mid_rel, qkv_gb, attn_b, gain_one, gain_two, gq_grad, gk_grad, keep, send, extra, extra_rel):
    half = keep.shape[0]
    qkv = qc + 2 * kc
    width = one_rel.shape[0]

    def halves(v):
        high = v.astype(bf16).astype(f32)
        return high, v - high

    rows = lax.broadcasted_iota(jnp.int32, (PAD, width), 0)
    lines = jnp.zeros((PAD, width), f32)
    values = halves(gain_one[0:1, :]) + halves(gain_two[0:1, :])
    for i, v in enumerate(values):
        lines = lines + jnp.where(rows == i, v, 0.0)
    cols = lines.T
    heads = jnp.concatenate([gq_grad[...], gk_grad[...]], axis=0)
    high, low = halves(heads)
    lane = lax.broadcasted_iota(jnp.int32, (own, PAD), 1)
    tile = jnp.zeros((own, PAD), f32)
    count = 2 * HD // own
    for i in range(count):
        at = slice(i * own, (i + 1) * own)
        tile = tile + jnp.where(lane == 4 + i, high[at], 0.0)
        tile = tile + jnp.where(lane == 4 + count + i, low[at], 0.0)
    for i in range(width // own):
        extra[i * own : (i + 1) * own, :] = (cols[i * own : (i + 1) * own] + tile).astype(bf16)
    store_relative(dims, idx, extra_rel, extra, own)
    a = dot(one_rel[...], qkv_gb[...]).astype(bf16)
    b = dot(mid_rel[...], attn_b[...]).astype(bf16)
    for out, at in ((keep, slice(0, half)), (send, slice(half, 2 * half))):
        out[:, :qkv] = a[at]
        out[:, qkv : qkv + oc] = b[at]
        out[:, qkv + oc :] = extra_rel[at, :]


def core_sum(keep, send, n):
    got = shift(send, "core", 1)
    step = keep.shape[0] // n
    return [
        (keep[k * step : (k + 1) * step].astype(f32) + got[k * step : (k + 1) * step].astype(f32)).astype(bf16)
        for k in range(n)
    ]


def row_sum(x, axis):
    step = x.shape[0] // lax.axis_size(axis)
    return summed([x[k * step : (k + 1) * step] for k in range(lax.axis_size(axis))], axis)


def after(values, others):
    return lax.optimization_barrier((list(values), others))[0]


def body(
    block_input,
    attn_gain,
    ffn_gain,
    query_gain,
    key_gain,
    query_weight,
    key_weight,
    value_weight,
    out_weight,
    gate_weight,
    up_weight,
    down_weight,
    cotangent,
):
    span, seq_local, part = block_input.shape
    axes = ("dp", "z", "core", "tensor")
    dims = tuple(lax.axis_size(a) for a in axes)
    nx, nz, nc, n = dims
    idx = jnp.stack([lax.axis_index(a) for a in axes]).astype(jnp.int32)
    width = part * n
    own = query_weight.shape[0]
    qc, kc, oc, ff = (w.shape[1] for w in (query_weight, key_weight, out_weight, gate_weight))
    qkv = qc + 2 * kc
    aw = qkv + oc + PAD

    ffn_local = jnp.concatenate([gate_weight, up_weight, down_weight, out_weight], axis=1)
    ffn_w = lax.all_gather(ffn_local, ("dp", "z", "core"), axis=0, tiled=True)

    gains_local = jnp.pad(jnp.stack([attn_gain, ffn_gain], axis=1), ((0, 0), (0, PAD - 2)))
    attn_local = jnp.concatenate([query_weight, key_weight, value_weight, gains_local], axis=1)
    by_z = jnp.concatenate(gathered(attn_local, "z"), axis=0)
    both = jnp.concatenate([block_input.reshape(span, part), cotangent.reshape(span, part)], axis=1)
    both_parts = gathered(both, "tensor")
    my_first = (idx[1] * nc + idx[2]) * span
    positions = (my_first + jnp.arange(span, dtype=jnp.int32)).astype(f32)
    frequency = jnp.power(ROPE_BASE, -2.0 * jnp.arange(HALF, dtype=f32) / HD)
    angle = frequency[:, None] * positions[None, :]
    cosine, sine = jnp.cos(angle), jnp.sin(angle)
    head_gains = jnp.concatenate([query_gain, key_gain])[None, :]
    dp_parts = gathered(by_z, "dp")
    dp_parts, both_parts, cosine, sine, head_gains = lax.optimization_barrier(
        (dp_parts, both_parts, cosine, sine, head_gains)
    )
    w_own = jnp.concatenate(dp_parts, axis=0)
    w_partner = shift(w_own, "core", 1)
    cot, cot_t = call(
        functools.partial(cot_kernel, dims),
        [sds((span, width), bf16), sds((width, span), bf16)],
        [idx] + both_parts,
    )

    w, base, gains, q_t, raw_t, kv, one_rel = call(
        functools.partial(qkv_kernel, dims, own, qc, kc, oc),
        [
            sds((width, qkv + PAD), bf16),
            sds((span, width), bf16),
            sds((8, width), f32),
            sds((kc, qc // kc * span), bf16),
            sds((qc + kc, span), f32),
            sds((span, 2 * kc), bf16),
            sds((width, span), bf16),
        ],
        [idx] + both_parts + [w_own, w_partner, head_gains, cosine, sine],
        [pltpu.VMEM((width, span), bf16)],
        flops=2 * span * width * qkv,
    )
    kv_own = jnp.concatenate(gathered(kv, "z"), axis=0)
    kv_partner = shift(kv_own, "core", 1)

    length = span * nz * nc
    (kv_own, kv_partner), (cot, cot_t) = lax.optimization_barrier(((kv_own, kv_partner), (cot, cot_t)))
    block = 384
    const = lambda s: pl.BlockSpec(s, lambda j: (0, 0))
    steps = ff // block
    out_blocks = [pl.BlockSpec((width, PAD), lambda j, o=o: (0, o)) for o in (3 * ff // PAD, 3 * ff // PAD + 1)]
    kv_full, attn_t, attn_b, log_total = call(
        functools.partial(attend_kernel, dims, qc, kc, oc),
        [sds((length, 2 * kc), bf16), sds(q_t.shape, f32), sds((span, qc), bf16), sds((8, q_t.shape[1]), f32)],
        [idx, q_t, kv_own, kv_partner],
        [pltpu.VMEM(q_t.shape, f32), pltpu.VMEM((8, q_t.shape[1]), f32)],
        flops=4 * span * length * qc,
    )
    res = call(
        functools.partial(out_kernel, dims),
        [sds((span, part), bf16)] * n,
        [idx, attn_b, ffn_w, ffn_w],
        grid=(1,),
        in_specs=[pl.BlockSpec(memory_space=pltpu.SMEM), const((span, qc))] + out_blocks,
        out_specs=[const((span, part))] * n,
        flops=2 * span * width * qc,
    )
    attn_mine = summed(res, "tensor").astype(bf16)
    attn_parts = gathered(attn_mine, "tensor")

    hgrad = call(
        hidden_grad_kernel,
        [sds((span, ff), f32)],
        [cot, ffn_w],
        grid=(steps,),
        in_specs=[const((span, width)), pl.BlockSpec((width, block), lambda j: (0, 2 * steps + j))],
        out_specs=[pl.BlockSpec((span, block), lambda j: (0, j))],
        flops=2 * span * width * ff,
    )[0]
    res = call(
        functools.partial(ffn_kernel, dims, own),
        [sds((span, width), f32), sds((span, width), bf16), sds((span, 3 * ff), bf16)]
        + [sds((span, part), bf16)] * n,
        [idx, base, gains] + attn_parts + [ffn_w, ffn_w, hgrad],
        [pltpu.VMEM((span, width), f32)],
        grid=(steps,),
        in_specs=[pl.BlockSpec(memory_space=pltpu.SMEM)]
        + [const((span, width)), const((8, width))]
        + [const((span, part))] * n
        + [pl.BlockSpec((width, block), lambda j, o=o: (0, o + j)) for o in (0, steps)]
        + [pl.BlockSpec((span, block), lambda j: (0, j))],
        out_specs=[const((span, width)), const((span, width)), const((span, 3 * ff))]
        + [const((span, part))] * n,
        flops=8 * span * width * ff,
    )
    middle, normed_two, big = res[:3]
    grad_got = [shift(res[3 + k], "tensor", k) for k in range(1, n)]
    grad_mine = sum([g.astype(f32) for g in grad_got], res[3].astype(f32)).astype(bf16)
    grad_parts = gathered(grad_mine, "tensor")

    ffn_grad = call(
        ffn_grad_kernel,
        [sds((width, 3 * ff), bf16)],
        [normed_two, cot_t, big],
        [pltpu.VMEM((width, span), bf16)],
        grid=(3,),
        in_specs=[const((span, width)), const((width, span)), pl.BlockSpec((span, ff), lambda j: (0, j))],
        out_specs=[pl.BlockSpec((width, ff), lambda j: (0, j))],
        flops=6 * span * width * ff,
    )[0]
    ffn_sum = lax.psum_scatter(ffn_grad, ("dp", "z", "core"), scatter_dimension=0, tiled=True).astype(f32)

    down_parts = call(
        functools.partial(down_kernel, dims),
        [sds((span, part), bf16)] * n,
        [idx, big, ffn_w],
        grid=(1,),
        in_specs=[
            pl.BlockSpec(memory_space=pltpu.SMEM),
            pl.BlockSpec((span, ff), lambda j: (0, 2)),
            pl.BlockSpec((width, ff), lambda j: (0, 2)),
        ],
        out_specs=[const((span, part))] * n,
        flops=2 * span * width * ff,
    )
    grad_parts, down_parts = lax.optimization_barrier((grad_parts, down_parts))

    mine, mid_rel, gain_two, q_gb, gq_grad, kv_keep, kv_send = call(
        functools.partial(attend_back_kernel, dims, own, qc, kc, oc),
        [
            sds((span, part), f32),
            sds((width, span), bf16),
            sds((8, width), f32),
            sds((span, qc), bf16),
            sds((HD, 1), f32),
            sds((length // 2, 2 * kc), bf16),
            sds((length // 2, 2 * kc), bf16),
        ],
        [idx, middle, gains, cot] + grad_parts + [ffn_w, ffn_w, attn_t, q_t, raw_t, kv_full, log_total, head_gains, cosine, sine],
        [
            pltpu.VMEM((span, width), bf16),
            pltpu.VMEM((width, span), bf16),
            pltpu.VMEM(q_t.shape, f32),
            pltpu.VMEM(q_t.shape, bf16),
            pltpu.VMEM((8, q_t.shape[1]), f32),
            pltpu.VMEM((span, width), f32),
            pltpu.VMEM(q_t.shape, f32),
            pltpu.VMEM((kc // HD * q_t.shape[1], HD), bf16),
            pltpu.VMEM((kc // HD * q_t.shape[1], HD), bf16),
        ],
        grid=(1,),
        in_specs=[pl.BlockSpec(memory_space=pltpu.SMEM), const((span, width)), const((8, width)), const((span, width))]
        + [const((span, part))] * n
        + out_blocks
        + [const(v.shape) for v in (attn_t, q_t, raw_t, kv_full, log_total, head_gains, cosine, sine)],
        out_specs=[
            const((span, part)),
            const((width, span)),
            const((8, width)),
            const((span, qc)),
            const((HD, 1)),
            const((length // 2, 2 * kc)),
            const((length // 2, 2 * kc)),
        ],
        flops=10 * span * length * qc,
    )
    kv_pieces = core_sum(kv_keep, kv_send, nz)
    kv_parts = [kv_pieces[0]] + [shift(kv_pieces[k], "z", k) for k in range(1, nz)]
    kv_parts[1], down_parts = lax.optimization_barrier((kv_parts[1], down_parts))
    me_t = idx[3]
    middle_mine = lax.dynamic_slice_in_dim(middle, me_t * part, part, 1)
    block_output = (middle_mine + summed(down_parts, "tensor")).astype(bf16)

    res = call(
        functools.partial(input_grad_kernel, dims, qc, kc),
        [sds((span, qkv), bf16), sds((8, width), f32), sds((HD, 1), f32)]
        + [sds((span + 16, part), bf16)] * n,
        [idx] + kv_parts + [raw_t, head_gains, cosine, sine, q_gb, w, base, gains],
        [pltpu.VMEM((span, width), f32)],
        flops=2 * span * width * qkv,
    )
    qkv_gb, gain_one, gk_grad = res[:3]
    norm_parts = res[3:]
    keep, send = call(
        functools.partial(attn_grad_kernel, dims, own, qc, kc, oc),
        [sds((width // 2, aw), bf16)] * 2,
        [idx, one_rel, mid_rel, qkv_gb, attn_b, gain_one, gain_two, gq_grad, gk_grad],
        [pltpu.VMEM((width, PAD), bf16), pltpu.VMEM((width, PAD), bf16)],
        flops=2 * span * width * (qkv + oc),
    )
    (keep, send), block_output = lax.optimization_barrier(((keep, send), block_output))
    attn_pieces = core_sum(keep, send, nx)
    attn_got = [shift(attn_pieces[k], "dp", k) for k in range(1, nx)]
    attn_got[0], norm_parts = lax.optimization_barrier((attn_got[0], norm_parts))
    attn_x = sum([v.astype(f32) for v in attn_got], attn_pieces[0].astype(f32)).astype(bf16)
    norm_mine = summed(norm_parts, "tensor")
    along = (norm_mine[span] + norm_mine[span + 1])[:, None] * (1.0 / width)
    base_f = base.astype(f32)
    scale_one = lax.rsqrt(jnp.mean(base_f * base_f, axis=1, keepdims=True) + EPS)
    unit_mine = block_input.reshape(span, part).astype(f32) * scale_one
    gain_mine = lax.dynamic_slice_in_dim(gains, me_t * part, part, 1)[0:1]
    input_grad = (mine + scale_one * (norm_mine[:span] * gain_mine - unit_mine * along)).astype(bf16)

    attn_sum = row_sum(attn_x, "z")
    small = attn_sum[:, qkv + oc :]
    small_all = sum(gathered(small, "tensor"))
    count = 2 * HD // own
    head_sum = (small_all[:, 4 : 4 + count] + small_all[:, 4 + count : 4 + 2 * count]).T.reshape(-1)
    return (
        block_output.reshape(span, seq_local, part),
        input_grad.reshape(span, seq_local, part),
        small_all[:, 0] + small_all[:, 1],
        small[:, 2] + small[:, 3],
        head_sum[:HD],
        head_sum[HD:],
        attn_sum[:, :qc],
        attn_sum[:, qc : qc + kc],
        attn_sum[:, qc + kc : qkv],
        attn_sum[:, qkv : qkv + oc],
        ffn_sum[:, :ff],
        ffn_sum[:, ff : 2 * ff],
        ffn_sum[:, 2 * ff :],
    )


def solution(mesh):
    dp, seq, tensor = (mesh.shape[a] for a in ("dp", "seq", "tensor"))
    grid = Mesh(
        np.asarray(mesh.devices).reshape(dp, seq // 2, 2, tensor), ("dp", "z", "core", "tensor")
    )
    tokens = P(("z", "core"), "dp", "tensor")
    rows = P(("dp", "z", "core"))
    weight = P(("dp", "z", "core"), "tensor")
    return jax.shard_map(
        body,
        mesh=grid,
        in_specs=(tokens, rows, rows, P(), P()) + (weight,) * 7 + (tokens,),
        out_specs=(tokens, tokens, rows, rows, P(), P()) + (weight,) * 7,
        check_vma=False,
    )
```

```python
import functools

import numpy as np
import jax
import jax.numpy as jnp
from jax import lax
from jax.experimental import pallas as pl
from jax.experimental.pallas import tpu as pltpu
from jax.sharding import Mesh, PartitionSpec as P

HD = 64
HALF = HD // 2
EPS = 1e-05
ROPE_BASE = 1000000.0
SCALE = HD ** (-0.5)
PAD = 128
bf16 = jnp.bfloat16
f32 = jnp.float32
NN = (((1,), (0,)), ((), ()))
NT = (((1,), (1,)), ((), ()))


def dot(a, b, dims=NN):
    return lax.dot_general(a, b, dims, preferred_element_type=f32)


def rot_index(a, k, n):
    return lax.rem(a + k, n)


def ds(start, size):
    return pl.ds(pl.multiple_of(start * size, size), size)


def shift(x, axis, k):
    n = lax.axis_size(axis)
    return lax.ppermute(x, axis, [(i, (i + k) % n) for i in range(n)])


def gathered(x, axis):
    return [x] + [shift(x, axis, k) for k in range(1, lax.axis_size(axis))]


def summed(pieces, axis):
    total = pieces[0].astype(f32)
    for k in range(1, lax.axis_size(axis)):
        total = total + shift(pieces[k], axis, k).astype(f32)
    return total


def call(kernel, outs, ins, scratch=(), grid=None, in_specs=None, out_specs=None, flops=0):
    vm = pl.BlockSpec(memory_space=pltpu.VMEM)
    nbytes = sum(x.size * x.dtype.itemsize for x in list(ins) + list(outs))
    kwargs = {} if grid is None else {"grid": grid}
    return pl.pallas_call(
        kernel,
        out_shape=outs,
        in_specs=in_specs or [pl.BlockSpec(memory_space=pltpu.SMEM) if x.dtype == jnp.int32 else vm for x in ins],
        out_specs=out_specs or [vm] * len(outs),
        scratch_shapes=list(scratch),
        cost_estimate=pl.CostEstimate(flops=flops, bytes_accessed=nbytes, transcendentals=0),
        **kwargs,
    )(*ins)


def sds(shape, dtype):
    return jax.ShapeDtypeStruct(shape, dtype)


def store_relative(dims, idx, dst, src, own):
    nx, nz, nc, _ = dims
    x, z, c = idx[0], idx[1], idx[2]
    at = 0
    for other in range(nc):
        core = c if other == 0 else 1 - c
        for xr in range(nx):
            for zr in range(nz):
                row = (rot_index(x, xr, nx) * nz + rot_index(z, zr, nz)) * nc + core
                dst[at * own : (at + 1) * own, :] = src[ds(row, own), :]
                at += 1


def assemble(idx, n, pieces, dst, first=0):
    part = dst.shape[1] // n
    for k in range(n):
        dst[:, ds(rot_index(idx[3], n - k, n), part)] = pieces[k][:, first : first + part]


def cot_kernel(dims, idx, *refs):
    n = dims[3]
    pieces, (full, turned) = refs[:n], refs[n:]
    assemble(idx, n, pieces, full, full.shape[1] // n)
    turned[...] = full[...].T


def head_columns(ref):
    turned = jnp.broadcast_to(ref[...].astype(f32), (8, 2 * HD)).T
    return turned[:HD, :1], turned[HD:, :1]


def to_groups(dst, rows):
    span = rows.shape[1]
    group = dst.shape[1] // span
    for h in range(rows.shape[0] // HD):
        g, at = h // group, h % group
        dst[g * HD : (g + 1) * HD, at * span : (at + 1) * span] = rows[h * HD : (h + 1) * HD]


def from_groups(x, span):
    group = x.shape[1] // span
    return jnp.concatenate(
        [
            x[h // group * HD : (h // group + 1) * HD, h % group * span : (h % group + 1) * span]
            for h in range(x.shape[0] // HD * group)
        ],
        axis=0,
    )


def turn_heads(raw, gain, cosine, sine, heads):
    outs = []
    for h in range(heads):
        v = raw[h * HD : (h + 1) * HD]
        v = v * lax.rsqrt(jnp.mean(v * v, axis=0, keepdims=True) + EPS) * gain
        a, b = v[:HALF], v[HALF:]
        outs += [a * cosine - b * sine, b * cosine + a * sine]
    return jnp.concatenate(outs, axis=0)


def turn_heads_back(raw, grad, gain, cosine, sine, heads):
    outs, gain_grad = [], jnp.zeros((HD, 1), f32)
    for h in range(heads):
        v = raw[h * HD : (h + 1) * HD]
        g = grad[h * HD : (h + 1) * HD]
        ga, gb = g[:HALF], g[HALF:]
        g = jnp.concatenate([ga * cosine + gb * sine, gb * cosine - ga * sine], axis=0)
        r = lax.rsqrt(jnp.mean(v * v, axis=0, keepdims=True) + EPS)
        n = v * r
        gain_grad = gain_grad + jnp.sum(g * n, axis=1, keepdims=True)
        g = g * gain
        outs.append(r * (g - n * jnp.mean(g * n, axis=0, keepdims=True)))
    return jnp.concatenate(outs, axis=0), gain_grad


def qkv_kernel(dims, own, qc, kc, oc, idx, *refs):
    nx, nz, nc, n = dims
    pieces = refs[:n]
    w_parts = refs[n : n + 2 * nx]
    head_gains, cosine, sine = refs[n + 2 * nx : n + 2 * nx + 3]
    w, base, gains, q_t, raw_t, kv, rel, turned = refs[n + 2 * nx + 3 :]
    gq, gk = head_columns(head_gains)
    assemble(idx, n, pieces, base)
    for other in range(nc):
        core = idx[2] if other == 0 else 1 - idx[2]
        for zr in range(nz):
            for xr in range(nx):
                row = (rot_index(idx[0], nx - xr, nx) * nz + rot_index(idx[1], nz - zr, nz)) * nc + core
                w[ds(row, own), :] = w_parts[other * nx + xr][zr * own : (zr + 1) * own, :]
    qkv = qc + 2 * kc
    gains[...] = w[:, qkv:].astype(f32).T[:8]
    b = base[...].astype(f32)
    normed = b * lax.rsqrt(jnp.mean(b * b, axis=1, keepdims=True) + EPS) * gains[0:1, :]
    normed = normed.astype(bf16)
    raw = dot(normed, w[:, :qkv])
    turned[...] = normed.T
    store_relative(dims, idx, rel, turned, own)
    kv[:, kc:] = raw[:, qc + kc :].astype(bf16)
    rt = raw[:, : qc + kc].T
    raw_t[...] = rt
    co, si = cosine[...], sine[...]
    q = (turn_heads(rt[:qc], gq, co, si, qc // HD) * SCALE).astype(bf16)
    to_groups(q_t, q)
    kv[:, :kc] = turn_heads(rt[qc:], gk, co, si, kc // HD).T.astype(bf16)


def attend_kernel(dims, qc, kc, oc, idx, q_t, *refs):
    nx, nz, nc, n = dims
    kv_parts = refs[: nz * nc]
    kv, attn_t, attn_b, log_total, acc, tot = refs[nz * nc :]
    span = attn_b.shape[0]
    group = qc // kc
    me = idx[1] * nc + idx[2]
    for other in range(nc):
        core = idx[2] if other == 0 else 1 - idx[2]
        for zr in range(nz):
            block = rot_index(idx[1], nz - zr, nz) * nc + core
            kv[ds(block, span), :] = kv_parts[other * nz + zr][...]
    acc[...] = jnp.zeros_like(acc)
    tot[...] = jnp.zeros_like(tot)
    keys_at = lax.broadcasted_iota(jnp.int32, (span, span), 0)
    query_at = lax.broadcasted_iota(jnp.int32, (span, span), 1)
    ahead = keys_at - query_at
    ahead = jnp.concatenate([ahead] * group, axis=1)

    def step(j, carry):
        vt = kv[ds(j, span), kc:].T
        allowed = ahead <= (me - j) * span
        for g in range(kc // HD):
            rows = slice(g * HD, (g + 1) * HD)
            s = dot(kv[ds(j, span), rows], q_t[rows, :])
            e = jnp.where(allowed, jnp.exp(s), 0.0)
            tot[g : g + 1, :] += jnp.sum(e, axis=0, keepdims=True)
            acc[rows, :] += dot(vt[rows], e.astype(bf16))
        return carry

    lax.fori_loop(0, me + 1, step, 0)
    for g in range(kc // HD):
        rows = slice(g * HD, (g + 1) * HD)
        attn_t[rows, :] = acc[rows, :] / tot[g : g + 1, :]
    log_total[...] = jnp.log(jnp.maximum(tot[...], 1e-30))
    attn = from_groups(attn_t[...], span).T.astype(bf16)
    attn_b[...] = attn


def out_kernel(dims, idx, attn_b, w_low, w_high, *pieces):
    n = dims[3]
    attn = attn_b[...]
    part = w_low.shape[0] // n
    for k in range(n):
        rows = ds(rot_index(idx[3], k, n), part)
        out = dot(attn[:, :PAD], w_low[rows, :], NT) + dot(attn[:, PAD:], w_high[rows, :], NT)
        pieces[k][...] = out.astype(bf16)


def hidden_grad_kernel(cot, wd, out):
    out[...] = dot(cot[...], wd[...])


def ffn_kernel(dims, own, idx, base, gains, *refs):
    n = dims[3]
    sums = refs[:n]
    wg, wu, hgrad = refs[n : n + 3]
    middle, normed, big = refs[n + 3 : n + 6]
    pieces = refs[n + 6 : n + 6 + n]
    acc = refs[n + 6 + n]
    j = pl.program_id(0)
    part = sums[0].shape[1]

    @pl.when(j == 0)
    def _():
        for k in range(n):
            at = ds(rot_index(idx[3], n - k, n), part)
            middle[:, at] = base[:, at].astype(f32) + sums[k][...].astype(f32)
        m = middle[...]
        v = m * lax.rsqrt(jnp.mean(m * m, axis=1, keepdims=True) + EPS) * gains[1:2, :]
        v = v.astype(bf16)
        normed[...] = v
        acc[...] = jnp.zeros_like(acc)

    v = normed[...]
    block = wg.shape[1]
    ff = big.shape[1] // 3
    gate = dot(v, wg[...])
    up = dot(v, wu[...])
    hg = hgrad[...]
    sig = 1.0 / (1.0 + jnp.exp(-gate))
    act = gate * sig
    hidden = (act * up).astype(bf16)
    gate_gb = (hg * up * (sig + act * (1.0 - sig))).astype(bf16)
    up_gb = (hg * act).astype(bf16)
    big[:, pl.ds(pl.multiple_of(j * block, block), block)] = gate_gb
    big[:, pl.ds(pl.multiple_of(ff + j * block, PAD), block)] = up_gb
    big[:, pl.ds(pl.multiple_of(2 * ff + j * block, PAD), block)] = hidden
    acc[...] += dot(gate_gb, wg[...], NT) + dot(up_gb, wu[...], NT)

    @pl.when(j == pl.num_programs(0) - 1)
    def _():
        for k in range(n):
            pieces[k][...] = acc[:, ds(rot_index(idx[3], k, n), part)].astype(bf16)


def down_kernel(dims, idx, hidden, wd, *refs):
    n = dims[3]
    part = wd.shape[0] // n
    for k in range(n):
        rows = ds(rot_index(idx[3], k, n), part)
        refs[k][...] = dot(hidden[...], wd[rows, :], NT).astype(bf16)


def ffn_grad_kernel(normed, cot_t, big, out, turned):
    j = pl.program_id(0)

    @pl.when(j == 0)
    def _():
        turned[...] = normed[...].T

    @pl.when(j < 2)
    def _():
        out[...] = dot(turned[...], big[...]).astype(bf16)

    @pl.when(j == 2)
    def _():
        out[...] = dot(cot_t[...], big[...]).astype(bf16)


def attend_back_kernel(dims, own, qc, kc, oc, idx, middle, gains, cot, *refs):
    nx, nz, nc, n = dims
    grads = refs[:n]
    w_low, w_high, attn_t, q_t, raw_t, kv, log_total, head_gains, cosine, sine = refs[n : n + 10]
    mine, mid, gain_two, q_gb, gq_grad, kv_keep, kv_send = refs[n + 10 : n + 17]
    full, dq, do_t, delta, mid_grad, do_f, q_n, do_n = refs[n + 17 :]
    span = mine.shape[0]
    group = qc // kc
    me = idx[1] * nc + idx[2]
    assemble(idx, n, grads, full)
    m = middle[...]
    r = lax.rsqrt(jnp.mean(m * m, axis=1, keepdims=True) + EPS)
    unit = m * r
    ng = full[...].astype(f32)
    gain_two[...] = jnp.broadcast_to(jnp.sum(ng * unit, axis=0, keepdims=True), gain_two.shape)
    gg = ng * gains[1:2, :]
    mg = cot[...].astype(f32) + r * (gg - unit * jnp.mean(gg * unit, axis=1, keepdims=True))
    mid_grad[...] = mg
    part = grads[0].shape[1]
    mine[...] = mid_grad[:, ds(idx[3], part)]
    mgb = mg.astype(bf16)
    mid[...] = mgb
    ag = jnp.concatenate([dot(mgb, w_low[...]), dot(mgb, w_high[...])], axis=1)
    to_groups(do_f, ag.T)
    prod = do_f[...] * attn_t[...]
    do_t[...] = do_f[...].astype(bf16)
    for g in range(kc // HD):
        rows = slice(g * HD, (g + 1) * HD)
        delta[g : g + 1, :] = jnp.sum(prod[rows], axis=0, keepdims=True)
        q_n[g * q_t.shape[1] : (g + 1) * q_t.shape[1], :] = q_t[rows, :].T
        do_n[g * q_t.shape[1] : (g + 1) * q_t.shape[1], :] = do_t[rows, :].T
    dq[...] = jnp.zeros_like(dq)
    keys_at = lax.broadcasted_iota(jnp.int32, (span, span), 0)
    query_at = lax.broadcasted_iota(jnp.int32, (span, span), 1)
    ahead = keys_at - query_at
    ahead = jnp.concatenate([ahead] * group, axis=1)
    for other, out in enumerate((kv_keep, kv_send)):
        core = idx[2] if other == 0 else 1 - idx[2]

        def step(zr, carry, out=out, core=core):
            j = rot_index(idx[1], zr, nz) * nc + core
            at = ds(zr, span)

            @pl.when(j > me)
            def _():
                out[at, :] = jnp.zeros((span, 2 * kc), bf16)

            @pl.when(j <= me)
            def _():
                kt = kv[ds(j, span), :kc].T
                allowed = ahead <= (me - j) * span
                wide = q_t.shape[1]
                for g in range(kc // HD):
                    rows = slice(g * HD, (g + 1) * HD)
                    s = dot(kv[ds(j, span), rows], q_t[rows, :])
                    p = jnp.where(allowed, jnp.exp(s - log_total[g : g + 1, :]), 0.0)
                    dp = dot(kv[ds(j, span), kc + g * HD : kc + (g + 1) * HD], do_t[rows, :])
                    sg = (p * (dp - delta[g : g + 1, :])).astype(bf16)
                    dq[rows, :] += dot(kt[rows], sg)
                    dk = dot(sg, q_n[g * wide : (g + 1) * wide, :])
                    dv = dot(p.astype(bf16), do_n[g * wide : (g + 1) * wide, :])
                    out[at, rows] = dk.astype(bf16)
                    out[at, kc + g * HD : kc + (g + 1) * HD] = dv.astype(bf16)

            return carry

        lax.fori_loop(0, nz, step, 0)
    raw_grad, gain_grad = turn_heads_back(
        raw_t[:qc, :], from_groups(dq[...], span) * SCALE, head_columns(head_gains)[0], cosine[...], sine[...], qc // HD
    )
    gq_grad[...] = gain_grad
    q_gb[...] = raw_grad.T.astype(bf16)


def input_grad_kernel(dims, qc, kc, idx, *refs):
    n, nz = dims[3], dims[1]
    kv_parts = refs[:nz]
    raw_t, head_gains, cosine, sine, q_gb, w, base, gains = refs[nz : nz + 8]
    qkv_gb, gain_one, gk_grad = refs[nz + 8 : nz + 11]
    pieces = refs[nz + 11 : nz + 11 + n]
    acc = refs[nz + 11 + n]
    total = kv_parts[0][...].astype(f32)
    for k in range(1, nz):
        total = total + kv_parts[k][...].astype(f32)
    raw_grad, gain_grad = turn_heads_back(
        raw_t[qc:, :], total[:, :kc].T, head_columns(head_gains)[1], cosine[...], sine[...], kc // HD
    )
    gk_grad[...] = gain_grad
    qkv_gb[:, :qc] = q_gb[...]
    qkv_gb[:, qc : qc + kc] = raw_grad.T.astype(bf16)
    qkv_gb[:, qc + kc :] = total[:, kc:].astype(bf16)
    ng = dot(qkv_gb[...], w[:, : qc + 2 * kc], NT)
    acc[...] = ng
    b = base[...].astype(f32)
    unit = b * lax.rsqrt(jnp.mean(b * b, axis=1, keepdims=True) + EPS)
    prod = ng * unit
    gain_one[...] = jnp.broadcast_to(jnp.sum(prod, axis=0, keepdims=True), gain_one.shape)
    along = jnp.sum(prod * gains[0:1, :], axis=1, keepdims=True)
    along = jnp.broadcast_to(along, (along.shape[0], PAD)).T[:16]
    high = along.astype(bf16)
    low = (along - high.astype(f32)).astype(bf16)
    row = lax.broadcasted_iota(jnp.int32, along.shape, 0)
    tail = jnp.where(row == 0, high.astype(f32), low.astype(f32)).astype(bf16)
    part = acc.shape[1] // n
    for k in range(n):
        pieces[k][: along.shape[1], :] = acc[:, ds(rot_index(idx[3], k, n), part)].astype(bf16)
        pieces[k][along.shape[1] :, :] = tail


def attn_grad_kernel(dims, own, qc, kc, oc, idx, one_rel, out_rel, qkv_gb, gain_one, gain_two, gq_grad, gk_grad, keep, send, extra, extra_rel):
    half = keep.shape[0]
    qkv = qc + 2 * kc
    width = one_rel.shape[0]

    def halves(v):
        high = v.astype(bf16).astype(f32)
        return high, v - high

    rows = lax.broadcasted_iota(jnp.int32, (PAD, width), 0)
    lines = jnp.zeros((PAD, width), f32)
    values = halves(gain_one[0:1, :]) + halves(gain_two[0:1, :])
    for i, v in enumerate(values):
        lines = lines + jnp.where(rows == i, v, 0.0)
    cols = lines.T
    heads = jnp.concatenate([gq_grad[...], gk_grad[...]], axis=0)
    high, low = halves(heads)
    lane = lax.broadcasted_iota(jnp.int32, (own, PAD), 1)
    tile = jnp.zeros((own, PAD), f32)
    count = 2 * HD // own
    for i in range(count):
        at = slice(i * own, (i + 1) * own)
        tile = tile + jnp.where(lane == 4 + i, high[at], 0.0)
        tile = tile + jnp.where(lane == 4 + count + i, low[at], 0.0)
    for i in range(width // own):
        extra[i * own : (i + 1) * own, :] = (cols[i * own : (i + 1) * own] + tile).astype(bf16)
    store_relative(dims, idx, extra_rel, extra, own)
    a = dot(one_rel[...], qkv_gb[...]).astype(bf16)
    for out, at in ((keep, slice(0, half)), (send, slice(half, 2 * half))):
        out[:, :qkv] = a[at]
        out[:, qkv : qkv + oc] = out_rel[at, :]
        out[:, qkv + oc :] = extra_rel[at, :]


def sum_kernel(cuts, *refs):
    outs = refs[len(refs) - len(cuts) + 1 :]
    ins = refs[: len(refs) - len(cuts) + 1]
    for out, first, last in zip(outs, cuts[:-1], cuts[1:]):
        total = ins[0][:, first:last].astype(f32)
        for v in ins[1:]:
            total = total + v[:, first:last].astype(f32)
        out[...] = total


def pack_kernel(q, k, v, o, g, u, d, gain_one, gain_two, x, c, attn, ffn, both, square):
    at = 0
    for w in (q, k, v):
        attn[:, at : at + w.shape[1]] = w[...]
        at += w.shape[1]
    own = q.shape[0]
    square[...] = jnp.zeros_like(square)
    square[0:1, :own] = gain_one[...].astype(f32)
    square[1:2, :own] = gain_two[...].astype(f32)
    attn[:, at:] = square[...].T[:own].astype(bf16)
    at = 0
    for w in (g, u, d, o):
        ffn[:, at : at + w.shape[1]] = w[...]
        at += w.shape[1]
    part = x.shape[1]
    both[:, :part] = x[...]
    both[:, part:] = c[...]


def out_grad_kernel(dims, own, idx, mid, attn_b, out, turned, rel):
    turned[...] = mid[...].T
    store_relative(dims, idx, rel, turned, own)
    out[...] = dot(rel[...], attn_b[...]).astype(bf16)


def core_sum(keep, send, n):
    got = shift(send, "core", 1)
    step = keep.shape[0] // n
    return [
        (keep[k * step : (k + 1) * step].astype(f32) + got[k * step : (k + 1) * step].astype(f32)).astype(bf16)
        for k in range(n)
    ]


def row_sum(x, axis):
    step = x.shape[0] // lax.axis_size(axis)
    return summed([x[k * step : (k + 1) * step] for k in range(lax.axis_size(axis))], axis)


def after(values, others):
    return lax.optimization_barrier((list(values), others))[0]


def body(
    block_input,
    attn_gain,
    ffn_gain,
    query_gain,
    key_gain,
    query_weight,
    key_weight,
    value_weight,
    out_weight,
    gate_weight,
    up_weight,
    down_weight,
    cotangent,
):
    span, seq_local, part = block_input.shape
    axes = ("dp", "z", "core", "tensor")
    dims = tuple(lax.axis_size(a) for a in axes)
    nx, nz, nc, n = dims
    idx = jnp.stack([lax.axis_index(a) for a in axes]).astype(jnp.int32)
    width = part * n
    own = query_weight.shape[0]
    qc, kc, oc, ff = (w.shape[1] for w in (query_weight, key_weight, out_weight, gate_weight))
    qkv = qc + 2 * kc
    aw = qkv + oc + PAD

    attn_local, ffn_local, both = call(
        pack_kernel,
        [sds((own, qkv + PAD), bf16), sds((own, 3 * ff + oc), bf16), sds((span, 2 * part), bf16)],
        [query_weight, key_weight, value_weight, out_weight, gate_weight, up_weight, down_weight]
        + [attn_gain[None, :], ffn_gain[None, :], block_input.reshape(span, part), cotangent.reshape(span, part)],
        [pltpu.VMEM((PAD, PAD), f32)],
    )
    ffn_w = lax.all_gather(ffn_local, ("dp", "z", "core"), axis=0, tiled=True)
    by_z = jnp.concatenate(gathered(attn_local, "z"), axis=0)
    both_parts = gathered(both, "tensor")
    my_first = (idx[1] * nc + idx[2]) * span
    positions = (my_first + jnp.arange(span, dtype=jnp.int32)).astype(f32)
    frequency = jnp.power(ROPE_BASE, -2.0 * jnp.arange(HALF, dtype=f32) / HD)
    angle = frequency[:, None] * positions[None, :]
    cosine, sine = jnp.cos(angle), jnp.sin(angle)
    head_gains = jnp.concatenate([query_gain, key_gain])[None, :]
    dp_parts = gathered(by_z, "dp")
    dp_parts, both_parts, cosine, sine, head_gains = lax.optimization_barrier(
        (dp_parts, both_parts, cosine, sine, head_gains)
    )
    dp_partner = [shift(v, "core", 1) for v in dp_parts]
    cot, cot_t = call(
        functools.partial(cot_kernel, dims),
        [sds((span, width), bf16), sds((width, span), bf16)],
        [idx] + both_parts,
    )

    w, base, gains, q_t, raw_t, kv, one_rel = call(
        functools.partial(qkv_kernel, dims, own, qc, kc, oc),
        [
            sds((width, qkv + PAD), bf16),
            sds((span, width), bf16),
            sds((8, width), f32),
            sds((kc, qc // kc * span), bf16),
            sds((qc + kc, span), f32),
            sds((span, 2 * kc), bf16),
            sds((width, span), bf16),
        ],
        [idx] + both_parts + dp_parts + dp_partner + [head_gains, cosine, sine],
        [pltpu.VMEM((width, span), bf16)],
        flops=2 * span * width * qkv,
    )
    kv_own = gathered(kv, "z")
    kv_partner = [shift(v, "core", 1) for v in kv_own]

    length = span * nz * nc
    (kv_own, kv_partner), (cot, cot_t) = lax.optimization_barrier(((kv_own, kv_partner), (cot, cot_t)))
    block = 384
    const = lambda s: pl.BlockSpec(s, lambda j: (0, 0))
    steps = ff // block
    out_blocks = [pl.BlockSpec((width, PAD), lambda j, o=o: (0, o)) for o in (3 * ff // PAD, 3 * ff // PAD + 1)]
    kv_full, attn_t, attn_b, log_total = call(
        functools.partial(attend_kernel, dims, qc, kc, oc),
        [sds((length, 2 * kc), bf16), sds(q_t.shape, f32), sds((span, qc), bf16), sds((8, q_t.shape[1]), f32)],
        [idx, q_t] + kv_own + kv_partner,
        [pltpu.VMEM(q_t.shape, f32), pltpu.VMEM((8, q_t.shape[1]), f32)],
        flops=4 * span * length * qc,
    )
    res = call(
        functools.partial(out_kernel, dims),
        [sds((span, part), bf16)] * n,
        [idx, attn_b, ffn_w, ffn_w],
        grid=(1,),
        in_specs=[pl.BlockSpec(memory_space=pltpu.SMEM), const((span, qc))] + out_blocks,
        out_specs=[const((span, part))] * n,
        flops=2 * span * width * qc,
    )
    attn_mine = summed(res, "tensor").astype(bf16)
    attn_parts = gathered(attn_mine, "tensor")

    hgrad = call(
        hidden_grad_kernel,
        [sds((span, ff), f32)],
        [cot, ffn_w],
        grid=(steps,),
        in_specs=[const((span, width)), pl.BlockSpec((width, block), lambda j: (0, 2 * steps + j))],
        out_specs=[pl.BlockSpec((span, block), lambda j: (0, j))],
        flops=2 * span * width * ff,
    )[0]
    res = call(
        functools.partial(ffn_kernel, dims, own),
        [sds((span, width), f32), sds((span, width), bf16), sds((span, 3 * ff), bf16)]
        + [sds((span, part), bf16)] * n,
        [idx, base, gains] + attn_parts + [ffn_w, ffn_w, hgrad],
        [pltpu.VMEM((span, width), f32)],
        grid=(steps,),
        in_specs=[pl.BlockSpec(memory_space=pltpu.SMEM)]
        + [const((span, width)), const((8, width))]
        + [const((span, part))] * n
        + [pl.BlockSpec((width, block), lambda j, o=o: (0, o + j)) for o in (0, steps)]
        + [pl.BlockSpec((span, block), lambda j: (0, j))],
        out_specs=[const((span, width)), const((span, width)), const((span, 3 * ff))]
        + [const((span, part))] * n,
        flops=8 * span * width * ff,
    )
    middle, normed_two, big = res[:3]
    grad_got = [shift(res[3 + k], "tensor", k) for k in range(1, n)]
    part_zero = res[3]

    ffn_grad = call(
        ffn_grad_kernel,
        [sds((width, 3 * ff), bf16)],
        [normed_two, cot_t, big],
        [pltpu.VMEM((width, span), bf16)],
        grid=(3,),
        in_specs=[const((span, width)), const((width, span)), pl.BlockSpec((span, ff), lambda j: (0, j))],
        out_specs=[pl.BlockSpec((width, ff), lambda j: (0, j))],
        flops=6 * span * width * ff,
    )[0]
    grad_got, ffn_grad = lax.optimization_barrier((grad_got, ffn_grad))
    grad_mine = sum([g.astype(f32) for g in grad_got], part_zero.astype(f32)).astype(bf16)
    grad_parts = gathered(grad_mine, "tensor")
    ffn_sum = lax.psum_scatter(ffn_grad, ("dp", "z", "core"), scatter_dimension=0, tiled=True)

    down_parts = call(
        functools.partial(down_kernel, dims),
        [sds((span, part), bf16)] * n,
        [idx, big, ffn_w],
        grid=(1,),
        in_specs=[
            pl.BlockSpec(memory_space=pltpu.SMEM),
            pl.BlockSpec((span, ff), lambda j: (0, 2)),
            pl.BlockSpec((width, ff), lambda j: (0, 2)),
        ],
        out_specs=[const((span, part))] * n,
        flops=2 * span * width * ff,
    )
    grad_parts, down_parts = lax.optimization_barrier((grad_parts, down_parts))

    mine, mid, gain_two, q_gb, gq_grad, kv_keep, kv_send = call(
        functools.partial(attend_back_kernel, dims, own, qc, kc, oc),
        [
            sds((span, part), f32),
            sds((span, width), bf16),
            sds((8, width), f32),
            sds((span, qc), bf16),
            sds((HD, 1), f32),
            sds((length // 2, 2 * kc), bf16),
            sds((length // 2, 2 * kc), bf16),
        ],
        [idx, middle, gains, cot] + grad_parts + [ffn_w, ffn_w, attn_t, q_t, raw_t, kv_full, log_total, head_gains, cosine, sine],
        [
            pltpu.VMEM((span, width), bf16),
            pltpu.VMEM(q_t.shape, f32),
            pltpu.VMEM(q_t.shape, bf16),
            pltpu.VMEM((8, q_t.shape[1]), f32),
            pltpu.VMEM((span, width), f32),
            pltpu.VMEM(q_t.shape, f32),
            pltpu.VMEM((kc // HD * q_t.shape[1], HD), bf16),
            pltpu.VMEM((kc // HD * q_t.shape[1], HD), bf16),
        ],
        grid=(1,),
        in_specs=[pl.BlockSpec(memory_space=pltpu.SMEM), const((span, width)), const((8, width)), const((span, width))]
        + [const((span, part))] * n
        + out_blocks
        + [const(v.shape) for v in (attn_t, q_t, raw_t, kv_full, log_total, head_gains, cosine, sine)],
        out_specs=[
            const((span, part)),
            const((span, width)),
            const((8, width)),
            const((span, qc)),
            const((HD, 1)),
            const((length // 2, 2 * kc)),
            const((length // 2, 2 * kc)),
        ],
        flops=10 * span * length * qc,
    )
    kv_pieces = core_sum(kv_keep, kv_send, nz)
    kv_parts = [kv_pieces[0]] + [shift(kv_pieces[k], "z", k) for k in range(1, nz)]
    kv_parts[1], down_parts = lax.optimization_barrier((kv_parts[1], down_parts))
    out_rel = call(
        functools.partial(out_grad_kernel, dims, own),
        [sds((width, oc), bf16)],
        [idx, mid, attn_b],
        [pltpu.VMEM((width, span), bf16)] * 2,
        flops=2 * span * width * oc,
    )[0]
    kv_parts[2], out_rel = lax.optimization_barrier((kv_parts[2], out_rel))
    me_t = idx[3]
    middle_mine = lax.dynamic_slice_in_dim(middle, me_t * part, part, 1)
    down_got = [down_parts[0]] + [shift(down_parts[k], "tensor", k) for k in range(1, n)]

    res = call(
        functools.partial(input_grad_kernel, dims, qc, kc),
        [sds((span, qkv), bf16), sds((8, width), f32), sds((HD, 1), f32)]
        + [sds((span + 16, part), bf16)] * n,
        [idx] + kv_parts + [raw_t, head_gains, cosine, sine, q_gb, w, base, gains],
        [pltpu.VMEM((span, width), f32)],
        flops=2 * span * width * qkv,
    )
    qkv_gb, gain_one, gk_grad = res[:3]
    norm_parts = res[3:]
    keep, send = call(
        functools.partial(attn_grad_kernel, dims, own, qc, kc, oc),
        [sds((width // 2, aw), bf16)] * 2,
        [idx, one_rel, out_rel, qkv_gb, gain_one, gain_two, gq_grad, gk_grad],
        [pltpu.VMEM((width, PAD), bf16), pltpu.VMEM((width, PAD), bf16)],
        flops=2 * span * width * (qkv + oc),
    )
    (keep, send), down_got = lax.optimization_barrier(((keep, send), down_got))
    attn_pieces = core_sum(keep, send, nx)
    attn_got = [shift(attn_pieces[k], "dp", k) for k in range(1, nx)]
    attn_got[0], norm_parts = lax.optimization_barrier((attn_got[0], norm_parts))
    attn_x = sum([v.astype(f32) for v in attn_got], attn_pieces[0].astype(f32)).astype(bf16)
    norm_got = [norm_parts[0]] + [shift(norm_parts[k], "tensor", k) for k in range(1, n)]
    attn_x, norm_got = lax.optimization_barrier((attn_x, norm_got))
    z_parts = [attn_x[:own]] + [shift(attn_x[k * own : (k + 1) * own], "z", k) for k in range(1, nz)]
    wgrads = call(
        functools.partial(sum_kernel, (0, qc, qc + kc, qkv, qkv + oc, aw)),
        [sds((own, v), f32) for v in (qc, kc, kc, oc, PAD)],
        z_parts,
    )
    small = wgrads[4]
    block_output = (middle_mine + sum([v.astype(f32) for v in down_got[1:]], down_got[0].astype(f32))).astype(bf16)
    norm_mine = sum([v.astype(f32) for v in norm_got[1:]], norm_got[0].astype(f32))
    along = (norm_mine[span] + norm_mine[span + 1])[:, None] * (1.0 / width)
    base_f = base.astype(f32)
    scale_one = lax.rsqrt(jnp.mean(base_f * base_f, axis=1, keepdims=True) + EPS)
    unit_mine = block_input.reshape(span, part).astype(f32) * scale_one
    gain_mine = lax.dynamic_slice_in_dim(gains, me_t * part, part, 1)[0:1]
    input_grad = (mine + scale_one * (norm_mine[:span] * gain_mine - unit_mine * along)).astype(bf16)

    fgrads = call(
        functools.partial(sum_kernel, (0, ff, 2 * ff, 3 * ff)),
        [sds((own, ff), f32)] * 3,
        [ffn_sum],
    )
    small_all = sum(gathered(small, "tensor"))
    count = 2 * HD // own
    head_sum = (small_all[:, 4 : 4 + count] + small_all[:, 4 + count : 4 + 2 * count]).T.reshape(-1)
    return (
        block_output.reshape(span, seq_local, part),
        input_grad.reshape(span, seq_local, part),
        small_all[:, 0] + small_all[:, 1],
        small[:, 2] + small[:, 3],
        head_sum[:HD],
        head_sum[HD:],
        *wgrads[:4],
        *fgrads,
    )


def solution(mesh):
    dp, seq, tensor = (mesh.shape[a] for a in ("dp", "seq", "tensor"))
    grid = Mesh(
        np.asarray(mesh.devices).reshape(dp, seq // 2, 2, tensor), ("dp", "z", "core", "tensor")
    )
    tokens = P(("z", "core"), "dp", "tensor")
    rows = P(("dp", "z", "core"))
    weight = P(("dp", "z", "core"), "tensor")
    return jax.shard_map(
        body,
        mesh=grid,
        in_specs=(tokens, rows, rows, P(), P()) + (weight,) * 7 + (tokens,),
        out_specs=(tokens, tokens, rows, rows, P(), P()) + (weight,) * 7,
        check_vma=False,
    )
```

```python
import functools

import numpy as np
import jax
import jax.numpy as jnp
from jax import lax
from jax.experimental import pallas as pl
from jax.experimental.pallas import tpu as pltpu
from jax.sharding import Mesh, PartitionSpec as P

HD = 64
HALF = HD // 2
EPS = 1e-05
ROPE_BASE = 1000000.0
SCALE = HD ** (-0.5)
PAD = 128
bf16 = jnp.bfloat16
f32 = jnp.float32
NN = (((1,), (0,)), ((), ()))
NT = (((1,), (1,)), ((), ()))


def dot(a, b, dims=NN):
    return lax.dot_general(a, b, dims, preferred_element_type=f32)


def rot_index(a, k, n):
    return lax.rem(a + k, n)


def ds(start, size):
    return pl.ds(pl.multiple_of(start * size, size), size)


def shift(x, axis, k):
    n = lax.axis_size(axis)
    return lax.ppermute(x, axis, [(i, (i + k) % n) for i in range(n)])


def gathered(x, axis):
    return [x] + [shift(x, axis, k) for k in range(1, lax.axis_size(axis))]


def summed(pieces, axis):
    total = pieces[0].astype(f32)
    for k in range(1, lax.axis_size(axis)):
        total = total + shift(pieces[k], axis, k).astype(f32)
    return total


def call(kernel, outs, ins, scratch=(), grid=None, in_specs=None, out_specs=None, flops=0):
    vm = pl.BlockSpec(memory_space=pltpu.VMEM)
    nbytes = sum(x.size * x.dtype.itemsize for x in list(ins) + list(outs))
    kwargs = {} if grid is None else {"grid": grid}
    return pl.pallas_call(
        kernel,
        out_shape=outs,
        in_specs=in_specs or [pl.BlockSpec(memory_space=pltpu.SMEM) if x.dtype == jnp.int32 else vm for x in ins],
        out_specs=out_specs or [vm] * len(outs),
        scratch_shapes=list(scratch),
        cost_estimate=pl.CostEstimate(flops=flops, bytes_accessed=nbytes, transcendentals=0),
        **kwargs,
    )(*ins)


def sds(shape, dtype):
    return jax.ShapeDtypeStruct(shape, dtype)


def store_relative(dims, idx, dst, src, own):
    nx, nz, nc, _ = dims
    half = nx * nz
    for other in range(nc):
        core = idx[2] if other == 0 else 1 - idx[2]

        def step(i, carry, other=other, core=core):
            row = (rot_index(idx[0], i // nz, nx) * nz + rot_index(idx[1], i % nz, nz)) * nc + core
            dst[ds(other * half + i, own), :] = src[ds(row, own), :]
            return carry

        lax.fori_loop(0, half, step, 0)


def assemble(idx, n, pieces, dst, first=0):
    part = dst.shape[1] // n
    for k in range(n):
        dst[:, ds(rot_index(idx[3], n - k, n), part)] = pieces[k][:, first : first + part]


def cot_kernel(dims, own, idx, *refs):
    n = dims[3]
    pieces, (full, cot_t, turned) = refs[:n], refs[n:]
    assemble(idx, n, pieces, full, full.shape[1] // n)
    turned[...] = full[...].T
    by_core(dims, idx, cot_t, turned, own)


def head_columns(ref):
    turned = jnp.broadcast_to(ref[...].astype(f32), (8, 2 * HD)).T
    return turned[:HD, :1], turned[HD:, :1]


def to_groups(dst, rows):
    span = rows.shape[1]
    group = dst.shape[1] // span
    for h in range(rows.shape[0] // HD):
        g, at = h // group, h % group
        dst[g * HD : (g + 1) * HD, at * span : (at + 1) * span] = rows[h * HD : (h + 1) * HD]


def from_groups(x, span):
    group = x.shape[1] // span
    return jnp.concatenate(
        [
            x[h // group * HD : (h // group + 1) * HD, h % group * span : (h % group + 1) * span]
            for h in range(x.shape[0] // HD * group)
        ],
        axis=0,
    )


def turn_heads(raw, gain, cosine, sine, heads):
    outs = []
    for h in range(heads):
        v = raw[h * HD : (h + 1) * HD]
        v = v * lax.rsqrt(jnp.mean(v * v, axis=0, keepdims=True) + EPS) * gain
        a, b = v[:HALF], v[HALF:]
        outs += [a * cosine - b * sine, b * cosine + a * sine]
    return jnp.concatenate(outs, axis=0)


def turn_heads_back(raw, grad, gain, cosine, sine, heads):
    outs, gain_grad = [], jnp.zeros((HD, 1), f32)
    for h in range(heads):
        v = raw[h * HD : (h + 1) * HD]
        g = grad[h * HD : (h + 1) * HD]
        ga, gb = g[:HALF], g[HALF:]
        g = jnp.concatenate([ga * cosine + gb * sine, gb * cosine - ga * sine], axis=0)
        r = lax.rsqrt(jnp.mean(v * v, axis=0, keepdims=True) + EPS)
        n = v * r
        gain_grad = gain_grad + jnp.sum(g * n, axis=1, keepdims=True)
        g = g * gain
        outs.append(r * (g - n * jnp.mean(g * n, axis=0, keepdims=True)))
    return jnp.concatenate(outs, axis=0), gain_grad


def qkv_kernel(dims, own, qc, kc, oc, idx, *refs):
    nx, nz, nc, n = dims
    pieces = refs[:n]
    w_parts = refs[n : n + 2 * nx]
    head_gains, cosine, sine = refs[n + 2 * nx : n + 2 * nx + 3]
    w, base, gains, q_t, raw_t, kv, rel, turned = refs[n + 2 * nx + 3 :]
    gq, gk = head_columns(head_gains)
    assemble(idx, n, pieces, base)
    for other in range(nc):
        core = idx[2] if other == 0 else 1 - idx[2]
        for xr in range(nx):
            src = w_parts[other * nx + xr]

            def step(zr, carry, src=src, xr=xr, core=core):
                row = (rot_index(idx[0], nx - xr, nx) * nz + rot_index(idx[1], nz - zr, nz)) * nc + core
                w[ds(row, own), :] = src[ds(zr, own), :]
                return carry

            lax.fori_loop(0, nz, step, 0)
    qkv = qc + 2 * kc
    gains[...] = w[:, qkv:].astype(f32).T[:8]
    b = base[...].astype(f32)
    normed = b * lax.rsqrt(jnp.mean(b * b, axis=1, keepdims=True) + EPS) * gains[0:1, :]
    normed = normed.astype(bf16)
    raw = dot(normed, w[:, :qkv])
    turned[...] = normed.T
    store_relative(dims, idx, rel, turned, own)
    kv[:, kc:] = raw[:, qc + kc :].astype(bf16)
    rt = raw[:, : qc + kc].T
    raw_t[...] = rt
    co, si = cosine[...], sine[...]
    q = (turn_heads(rt[:qc], gq, co, si, qc // HD) * SCALE).astype(bf16)
    to_groups(q_t, q)
    kv[:, :kc] = turn_heads(rt[qc:], gk, co, si, kc // HD).T.astype(bf16)


def attend_kernel(dims, qc, kc, oc, idx, q_t, *refs):
    nx, nz, nc, n = dims
    kv_parts = refs[: nz * nc]
    kv, attn_t, attn_b, log_total, acc, tot = refs[nz * nc :]
    span = attn_b.shape[0]
    group = qc // kc
    me = idx[1] * nc + idx[2]
    for other in range(nc):
        core = idx[2] if other == 0 else 1 - idx[2]
        for zr in range(nz):
            block = rot_index(idx[1], nz - zr, nz) * nc + core
            kv[ds(block, span), :] = kv_parts[other * nz + zr][...]
    acc[...] = jnp.zeros_like(acc)
    tot[...] = jnp.zeros_like(tot)
    keys_at = lax.broadcasted_iota(jnp.int32, (span, span), 0)
    query_at = lax.broadcasted_iota(jnp.int32, (span, span), 1)
    ahead = keys_at - query_at
    ahead = jnp.concatenate([ahead] * group, axis=1)

    def step(j, carry):
        vt = kv[ds(j, span), kc:].T
        allowed = ahead <= (me - j) * span
        for g in range(kc // HD):
            rows = slice(g * HD, (g + 1) * HD)
            s = dot(kv[ds(j, span), rows], q_t[rows, :])
            e = jnp.where(allowed, jnp.exp(s), 0.0)
            tot[g : g + 1, :] += jnp.sum(e, axis=0, keepdims=True)
            acc[rows, :] += dot(vt[rows], e.astype(bf16))
        return carry

    lax.fori_loop(0, me + 1, step, 0)
    for g in range(kc // HD):
        rows = slice(g * HD, (g + 1) * HD)
        attn_t[rows, :] = acc[rows, :] / tot[g : g + 1, :]
    log_total[...] = jnp.log(jnp.maximum(tot[...], 1e-30))
    attn = from_groups(attn_t[...], span).T.astype(bf16)
    attn_b[...] = attn


def out_kernel(dims, idx, attn_b, w_low, w_high, *pieces):
    n = dims[3]
    attn = attn_b[...]
    part = w_low.shape[0] // n
    for k in range(n):
        rows = ds(rot_index(idx[3], k, n), part)
        out = dot(attn[:, :PAD], w_low[rows, :], NT) + dot(attn[:, PAD:], w_high[rows, :], NT)
        pieces[k][...] = out.astype(bf16)


def hidden_grad_kernel(cot, wd, out):
    out[...] = dot(cot[...], wd[...])


def ffn_kernel(dims, own, idx, base, gains, *refs):
    n = dims[3]
    sums = refs[:n]
    wg, wu, hgrad = refs[n : n + 3]
    middle, normed, big = refs[n + 3 : n + 6]
    pieces = refs[n + 6 : n + 6 + n]
    acc = refs[n + 6 + n]
    j = pl.program_id(0)
    part = sums[0].shape[1]

    @pl.when(j == 0)
    def _():
        for k in range(n):
            at = ds(rot_index(idx[3], n - k, n), part)
            middle[:, at] = base[:, at].astype(f32) + sums[k][...].astype(f32)
        m = middle[...]
        v = m * lax.rsqrt(jnp.mean(m * m, axis=1, keepdims=True) + EPS) * gains[1:2, :]
        v = v.astype(bf16)
        normed[...] = v
        acc[...] = jnp.zeros_like(acc)

    v = normed[...]
    block = wg.shape[1]
    ff = big.shape[1] // 3
    gate = dot(v, wg[...])
    up = dot(v, wu[...])
    hg = hgrad[...]
    sig = 1.0 / (1.0 + jnp.exp(-gate))
    act = gate * sig
    hidden = (act * up).astype(bf16)
    gate_gb = (hg * up * (sig + act * (1.0 - sig))).astype(bf16)
    up_gb = (hg * act).astype(bf16)
    big[:, pl.ds(pl.multiple_of(j * block, block), block)] = gate_gb
    big[:, pl.ds(pl.multiple_of(ff + j * block, PAD), block)] = up_gb
    big[:, pl.ds(pl.multiple_of(2 * ff + j * block, PAD), block)] = hidden
    acc[...] += dot(gate_gb, wg[...], NT) + dot(up_gb, wu[...], NT)

    @pl.when(j == pl.num_programs(0) - 1)
    def _():
        for k in range(n):
            pieces[k][...] = acc[:, ds(rot_index(idx[3], k, n), part)].astype(bf16)


def down_kernel(dims, idx, hidden, wd, *refs):
    n = dims[3]
    part = wd.shape[0] // n
    for k in range(n):
        rows = ds(rot_index(idx[3], k, n), part)
        refs[k][...] = dot(hidden[...], wd[rows, :], NT).astype(bf16)


def by_core(dims, idx, dst, src, own):
    nx, nz, nc, _ = dims
    half = nx * nz
    for other in range(nc):
        core = idx[2] if other == 0 else 1 - idx[2]

        def step(i, carry, other=other, core=core):
            dst[ds(other * half + i, own), :] = src[ds(i * nc + core, own), :]
            return carry

        lax.fori_loop(0, half, step, 0)


def ffn_grad_kernel(dims, own, idx, normed, cot_t, big, keep, send, turned, left):
    j = pl.program_id(0)
    half = keep.shape[0]

    @pl.when(j == 0)
    def _():
        turned[...] = normed[...].T
        by_core(dims, idx, left, turned, own)

    @pl.when(j == 2)
    def _():
        left[...] = cot_t[...]

    keep[...] = dot(left[:half, :], big[...]).astype(bf16)
    send[...] = dot(left[half:, :], big[...]).astype(bf16)


def attend_back_kernel(dims, own, qc, kc, oc, idx, middle, gains, cot, *refs):
    nx, nz, nc, n = dims
    grads = refs[:n]
    w_low, w_high, attn_t, q_t, raw_t, kv, log_total, head_gains, cosine, sine = refs[n : n + 10]
    mine, mid, gain_two, q_gb, gq_grad, kv_keep, kv_send = refs[n + 10 : n + 17]
    full, dq, do_t, delta, mid_grad, do_f, q_n, do_n, out = refs[n + 17 :]
    span = mine.shape[0]
    group = qc // kc
    me = idx[1] * nc + idx[2]
    assemble(idx, n, grads, full)
    m = middle[...]
    r = lax.rsqrt(jnp.mean(m * m, axis=1, keepdims=True) + EPS)
    unit = m * r
    ng = full[...].astype(f32)
    gain_two[...] = jnp.broadcast_to(jnp.sum(ng * unit, axis=0, keepdims=True), gain_two.shape)
    gg = ng * gains[1:2, :]
    mg = cot[...].astype(f32) + r * (gg - unit * jnp.mean(gg * unit, axis=1, keepdims=True))
    mid_grad[...] = mg
    part = grads[0].shape[1]
    mine[...] = mid_grad[:, ds(idx[3], part)]
    mgb = mg.astype(bf16)
    mid[...] = mgb
    ag = jnp.concatenate([dot(mgb, w_low[...]), dot(mgb, w_high[...])], axis=1)
    to_groups(do_f, ag.T)
    prod = do_f[...] * attn_t[...]
    do_t[...] = do_f[...].astype(bf16)
    for g in range(kc // HD):
        rows = slice(g * HD, (g + 1) * HD)
        delta[g : g + 1, :] = jnp.sum(prod[rows], axis=0, keepdims=True)
        q_n[g * q_t.shape[1] : (g + 1) * q_t.shape[1], :] = q_t[rows, :].T
        do_n[g * q_t.shape[1] : (g + 1) * q_t.shape[1], :] = do_t[rows, :].T
    dq[...] = jnp.zeros_like(dq)
    keys_at = lax.broadcasted_iota(jnp.int32, (span, span), 0)
    query_at = lax.broadcasted_iota(jnp.int32, (span, span), 1)
    ahead = keys_at - query_at
    ahead = jnp.concatenate([ahead] * group, axis=1)
    def step(t, carry):
        other = t // nz
        j = rot_index(idx[1], t % nz, nz) * nc + lax.rem(idx[2] + other, nc)
        at = ds(t, span)

        @pl.when(j > me)
        def _():
            out[at, :] = jnp.zeros((span, 2 * kc), bf16)

        @pl.when(j <= me)
        def _():
            kt = kv[ds(j, span), :kc].T
            allowed = ahead <= (me - j) * span
            wide = q_t.shape[1]
            for g in range(kc // HD):
                rows = slice(g * HD, (g + 1) * HD)
                s = dot(kv[ds(j, span), rows], q_t[rows, :])
                p = jnp.where(allowed, jnp.exp(s - log_total[g : g + 1, :]), 0.0)
                dp = dot(kv[ds(j, span), kc + g * HD : kc + (g + 1) * HD], do_t[rows, :])
                sg = (p * (dp - delta[g : g + 1, :])).astype(bf16)
                dq[rows, :] += dot(kt[rows], sg)
                dk = dot(sg, q_n[g * wide : (g + 1) * wide, :])
                dv = dot(p.astype(bf16), do_n[g * wide : (g + 1) * wide, :])
                out[at, rows] = dk.astype(bf16)
                out[at, kc + g * HD : kc + (g + 1) * HD] = dv.astype(bf16)

        return carry

    lax.fori_loop(0, nz * nc, step, 0)
    kv_keep[...] = out[: nz * span, :]
    kv_send[...] = out[nz * span :, :]
    raw_grad, gain_grad = turn_heads_back(
        raw_t[:qc, :], from_groups(dq[...], span) * SCALE, head_columns(head_gains)[0], cosine[...], sine[...], qc // HD
    )
    gq_grad[...] = gain_grad
    q_gb[...] = raw_grad.T.astype(bf16)


def input_grad_kernel(dims, qc, kc, idx, *refs):
    n, nz = dims[3], dims[1]
    kv_parts = refs[:nz]
    raw_t, head_gains, cosine, sine, q_gb, w, base, gains = refs[nz : nz + 8]
    qkv_gb, gain_one, gk_grad = refs[nz + 8 : nz + 11]
    pieces = refs[nz + 11 : nz + 11 + n]
    acc = refs[nz + 11 + n]
    total = kv_parts[0][...].astype(f32)
    for k in range(1, nz):
        total = total + kv_parts[k][...].astype(f32)
    raw_grad, gain_grad = turn_heads_back(
        raw_t[qc:, :], total[:, :kc].T, head_columns(head_gains)[1], cosine[...], sine[...], kc // HD
    )
    gk_grad[...] = gain_grad
    qkv_gb[:, :qc] = q_gb[...]
    qkv_gb[:, qc : qc + kc] = raw_grad.T.astype(bf16)
    qkv_gb[:, qc + kc :] = total[:, kc:].astype(bf16)
    ng = dot(qkv_gb[...], w[:, : qc + 2 * kc], NT)
    acc[...] = ng
    b = base[...].astype(f32)
    unit = b * lax.rsqrt(jnp.mean(b * b, axis=1, keepdims=True) + EPS)
    prod = ng * unit
    gain_one[...] = jnp.broadcast_to(jnp.sum(prod, axis=0, keepdims=True), gain_one.shape)
    along = jnp.sum(prod * gains[0:1, :], axis=1, keepdims=True)
    along = jnp.broadcast_to(along, (along.shape[0], PAD)).T[:16]
    high = along.astype(bf16)
    low = (along - high.astype(f32)).astype(bf16)
    row = lax.broadcasted_iota(jnp.int32, along.shape, 0)
    tail = jnp.where(row == 0, high.astype(f32), low.astype(f32)).astype(bf16)
    part = acc.shape[1] // n
    for k in range(n):
        pieces[k][: along.shape[1], :] = acc[:, ds(rot_index(idx[3], k, n), part)].astype(bf16)
        pieces[k][along.shape[1] :, :] = tail


def attn_grad_kernel(dims, own, qc, kc, oc, idx, one_rel, out_rel, qkv_gb, gain_one, gain_two, gq_grad, gk_grad, keep, send, extra, extra_rel, lined, spread):
    half = keep.shape[0]
    qkv = qc + 2 * kc
    width = one_rel.shape[0]

    def halves(v):
        high = v.astype(bf16).astype(f32)
        return high, v - high

    rows = lax.broadcasted_iota(jnp.int32, (PAD, width), 0)
    lines = jnp.zeros((PAD, width), f32)
    values = halves(gain_one[0:1, :]) + halves(gain_two[0:1, :])
    for i, v in enumerate(values):
        lines = lines + jnp.where(rows == i, v, 0.0)
    cols = lines.T
    heads = jnp.concatenate([gq_grad[...], gk_grad[...]], axis=0)
    high, low = halves(heads)
    lane = lax.broadcasted_iota(jnp.int32, (own, PAD), 1)
    tile = jnp.zeros((own, PAD), f32)
    count = 2 * HD // own
    for i in range(count):
        at = slice(i * own, (i + 1) * own)
        tile = tile + jnp.where(lane == 4 + i, high[at], 0.0)
        tile = tile + jnp.where(lane == 4 + count + i, low[at], 0.0)
    lined[...] = cols
    spread[...] = tile

    def step(i, carry):
        extra[ds(i, own), :] = (lined[ds(i, own), :] + spread[...]).astype(bf16)
        return carry

    lax.fori_loop(0, width // own, step, 0)
    store_relative(dims, idx, extra_rel, extra, own)
    a = dot(one_rel[...], qkv_gb[...]).astype(bf16)
    for out, at in ((keep, slice(0, half)), (send, slice(half, 2 * half))):
        out[:, :qkv] = a[at]
        out[:, qkv : qkv + oc] = out_rel[at, :]
        out[:, qkv + oc :] = extra_rel[at, :]


def sum_kernel(cuts, *refs):
    outs = refs[len(refs) - len(cuts) + 1 :]
    ins = refs[: len(refs) - len(cuts) + 1]
    for out, first, last in zip(outs, cuts[:-1], cuts[1:]):
        total = ins[0][:, first:last].astype(f32)
        for v in ins[1:]:
            total = total + v[:, first:last].astype(f32)
        out[...] = total


def pack_kernel(q, k, v, o, g, u, d, gain_one, gain_two, x, c, attn, ffn, both, square):
    at = 0
    for w in (q, k, v):
        attn[:, at : at + w.shape[1]] = w[...]
        at += w.shape[1]
    own = q.shape[0]
    square[...] = jnp.zeros_like(square)
    square[0:1, :own] = gain_one[...].astype(f32)
    square[1:2, :own] = gain_two[...].astype(f32)
    attn[:, at:] = square[...].T[:own].astype(bf16)
    at = 0
    for w in (g, u, d, o):
        ffn[:, at : at + w.shape[1]] = w[...]
        at += w.shape[1]
    part = x.shape[1]
    both[:, :part] = x[...]
    both[:, part:] = c[...]


def out_grad_kernel(dims, own, idx, mid, attn_b, out, turned, rel):
    turned[...] = mid[...].T
    store_relative(dims, idx, rel, turned, own)
    out[...] = dot(rel[...], attn_b[...]).astype(bf16)


def core_sum(keep, send, n):
    got = shift(send, "core", 1)
    step = keep.shape[0] // n
    return [
        (keep[k * step : (k + 1) * step].astype(f32) + got[k * step : (k + 1) * step].astype(f32)).astype(bf16)
        for k in range(n)
    ]


def row_sum(x, axis):
    step = x.shape[0] // lax.axis_size(axis)
    return summed([x[k * step : (k + 1) * step] for k in range(lax.axis_size(axis))], axis)


def after(values, others):
    return lax.optimization_barrier((list(values), others))[0]


def body(
    block_input,
    attn_gain,
    ffn_gain,
    query_gain,
    key_gain,
    query_weight,
    key_weight,
    value_weight,
    out_weight,
    gate_weight,
    up_weight,
    down_weight,
    cotangent,
):
    span, seq_local, part = block_input.shape
    axes = ("dp", "z", "core", "tensor")
    dims = tuple(lax.axis_size(a) for a in axes)
    nx, nz, nc, n = dims
    idx = jnp.stack([lax.axis_index(a) for a in axes]).astype(jnp.int32)
    width = part * n
    own = query_weight.shape[0]
    qc, kc, oc, ff = (w.shape[1] for w in (query_weight, key_weight, out_weight, gate_weight))
    qkv = qc + 2 * kc
    aw = qkv + oc + PAD

    attn_local, ffn_local, both = call(
        pack_kernel,
        [sds((own, qkv + PAD), bf16), sds((own, 3 * ff + oc), bf16), sds((span, 2 * part), bf16)],
        [query_weight, key_weight, value_weight, out_weight, gate_weight, up_weight, down_weight]
        + [attn_gain[None, :], ffn_gain[None, :], block_input.reshape(span, part), cotangent.reshape(span, part)],
        [pltpu.VMEM((PAD, PAD), f32)],
    )
    ffn_w = lax.all_gather(ffn_local, ("dp", "z", "core"), axis=0, tiled=True)
    by_z = jnp.concatenate(gathered(attn_local, "z"), axis=0)
    both_parts = gathered(both, "tensor")
    my_first = (idx[1] * nc + idx[2]) * span
    positions = (my_first + jnp.arange(span, dtype=jnp.int32)).astype(f32)
    frequency = jnp.power(ROPE_BASE, -2.0 * jnp.arange(HALF, dtype=f32) / HD)
    angle = frequency[:, None] * positions[None, :]
    cosine, sine = jnp.cos(angle), jnp.sin(angle)
    head_gains = jnp.concatenate([query_gain, key_gain])[None, :]
    dp_parts = gathered(by_z, "dp")
    dp_parts, both_parts, cosine, sine, head_gains = lax.optimization_barrier(
        (dp_parts, both_parts, cosine, sine, head_gains)
    )
    dp_partner = [shift(v, "core", 1) for v in dp_parts]
    cot, cot_t = call(
        functools.partial(cot_kernel, dims, own),
        [sds((span, width), bf16), sds((width, span), bf16)],
        [idx] + both_parts,
        [pltpu.VMEM((width, span), bf16)],
    )

    w, base, gains, q_t, raw_t, kv, one_rel = call(
        functools.partial(qkv_kernel, dims, own, qc, kc, oc),
        [
            sds((width, qkv + PAD), bf16),
            sds((span, width), bf16),
            sds((8, width), f32),
            sds((kc, qc // kc * span), bf16),
            sds((qc + kc, span), f32),
            sds((span, 2 * kc), bf16),
            sds((width, span), bf16),
        ],
        [idx] + both_parts + dp_parts + dp_partner + [head_gains, cosine, sine],
        [pltpu.VMEM((width, span), bf16)],
        flops=2 * span * width * qkv,
    )
    kv_own = gathered(kv, "z")
    kv_partner = [shift(v, "core", 1) for v in kv_own]

    length = span * nz * nc
    (kv_own, kv_partner), (cot, cot_t) = lax.optimization_barrier(((kv_own, kv_partner), (cot, cot_t)))
    block = 384
    const = lambda s: pl.BlockSpec(s, lambda j: (0, 0))
    steps = ff // block
    out_blocks = [pl.BlockSpec((width, PAD), lambda j, o=o: (0, o)) for o in (3 * ff // PAD, 3 * ff // PAD + 1)]
    kv_full, attn_t, attn_b, log_total = call(
        functools.partial(attend_kernel, dims, qc, kc, oc),
        [sds((length, 2 * kc), bf16), sds(q_t.shape, f32), sds((span, qc), bf16), sds((8, q_t.shape[1]), f32)],
        [idx, q_t] + kv_own + kv_partner,
        [pltpu.VMEM(q_t.shape, f32), pltpu.VMEM((8, q_t.shape[1]), f32)],
        flops=4 * span * length * qc,
    )
    res = call(
        functools.partial(out_kernel, dims),
        [sds((span, part), bf16)] * n,
        [idx, attn_b, ffn_w, ffn_w],
        grid=(1,),
        in_specs=[pl.BlockSpec(memory_space=pltpu.SMEM), const((span, qc))] + out_blocks,
        out_specs=[const((span, part))] * n,
        flops=2 * span * width * qc,
    )
    attn_mine = summed(res, "tensor").astype(bf16)
    attn_parts = gathered(attn_mine, "tensor")

    hgrad = call(
        hidden_grad_kernel,
        [sds((span, ff), f32)],
        [cot, ffn_w],
        grid=(steps,),
        in_specs=[const((span, width)), pl.BlockSpec((width, block), lambda j: (0, 2 * steps + j))],
        out_specs=[pl.BlockSpec((span, block), lambda j: (0, j))],
        flops=2 * span * width * ff,
    )[0]
    res = call(
        functools.partial(ffn_kernel, dims, own),
        [sds((span, width), f32), sds((span, width), bf16), sds((span, 3 * ff), bf16)]
        + [sds((span, part), bf16)] * n,
        [idx, base, gains] + attn_parts + [ffn_w, ffn_w, hgrad],
        [pltpu.VMEM((span, width), f32)],
        grid=(steps,),
        in_specs=[pl.BlockSpec(memory_space=pltpu.SMEM)]
        + [const((span, width)), const((8, width))]
        + [const((span, part))] * n
        + [pl.BlockSpec((width, block), lambda j, o=o: (0, o + j)) for o in (0, steps)]
        + [pl.BlockSpec((span, block), lambda j: (0, j))],
        out_specs=[const((span, width)), const((span, width)), const((span, 3 * ff))]
        + [const((span, part))] * n,
        flops=8 * span * width * ff,
    )
    middle, normed_two, big = res[:3]
    grad_got = [shift(res[3 + k], "tensor", k) for k in range(1, n)]
    part_zero = res[3]

    ffn_keep, ffn_send = call(
        functools.partial(ffn_grad_kernel, dims, own),
        [sds((width // nc, 3 * ff), bf16)] * 2,
        [idx, normed_two, cot_t, big],
        [pltpu.VMEM((width, span), bf16)] * 2,
        grid=(3,),
        in_specs=[pl.BlockSpec(memory_space=pltpu.SMEM), const((span, width)), const((width, span))]
        + [pl.BlockSpec((span, ff), lambda j: (0, j))],
        out_specs=[pl.BlockSpec((width // nc, ff), lambda j: (0, j))] * 2,
        flops=6 * span * width * ff,
    )
    grad_got, (ffn_keep, ffn_send) = lax.optimization_barrier((grad_got, (ffn_keep, ffn_send)))
    grad_mine = sum([g.astype(f32) for g in grad_got], part_zero.astype(f32)).astype(bf16)
    grad_parts = gathered(grad_mine, "tensor")
    down_parts = call(
        functools.partial(down_kernel, dims),
        [sds((span, part), bf16)] * n,
        [idx, big, ffn_w],
        grid=(1,),
        in_specs=[
            pl.BlockSpec(memory_space=pltpu.SMEM),
            pl.BlockSpec((span, ff), lambda j: (0, 2)),
            pl.BlockSpec((width, ff), lambda j: (0, 2)),
        ],
        out_specs=[const((span, part))] * n,
        flops=2 * span * width * ff,
    )
    ffn_got = shift(ffn_send, "core", 1)
    grad_parts, ffn_got, down_parts = lax.optimization_barrier((grad_parts, ffn_got, down_parts))
    ffn_half = (ffn_keep.astype(f32) + ffn_got.astype(f32)).astype(bf16)
    ffn_x = lax.psum_scatter(ffn_half, "dp", scatter_dimension=0, tiled=True)

    mine, mid, gain_two, q_gb, gq_grad, kv_keep, kv_send = call(
        functools.partial(attend_back_kernel, dims, own, qc, kc, oc),
        [
            sds((span, part), f32),
            sds((span, width), bf16),
            sds((8, width), f32),
            sds((span, qc), bf16),
            sds((HD, 1), f32),
            sds((length // 2, 2 * kc), bf16),
            sds((length // 2, 2 * kc), bf16),
        ],
        [idx, middle, gains, cot] + grad_parts + [ffn_w, ffn_w, attn_t, q_t, raw_t, kv_full, log_total, head_gains, cosine, sine],
        [
            pltpu.VMEM((span, width), bf16),
            pltpu.VMEM(q_t.shape, f32),
            pltpu.VMEM(q_t.shape, bf16),
            pltpu.VMEM((8, q_t.shape[1]), f32),
            pltpu.VMEM((span, width), f32),
            pltpu.VMEM(q_t.shape, f32),
            pltpu.VMEM((kc // HD * q_t.shape[1], HD), bf16),
            pltpu.VMEM((kc // HD * q_t.shape[1], HD), bf16),
            pltpu.VMEM((length, 2 * kc), bf16),
        ],
        grid=(1,),
        in_specs=[pl.BlockSpec(memory_space=pltpu.SMEM), const((span, width)), const((8, width)), const((span, width))]
        + [const((span, part))] * n
        + out_blocks
        + [const(v.shape) for v in (attn_t, q_t, raw_t, kv_full, log_total, head_gains, cosine, sine)],
        out_specs=[
            const((span, part)),
            const((span, width)),
            const((8, width)),
            const((span, qc)),
            const((HD, 1)),
            const((length // 2, 2 * kc)),
            const((length // 2, 2 * kc)),
        ],
        flops=10 * span * length * qc,
    )
    kv_pieces = core_sum(kv_keep, kv_send, nz)
    kv_parts = [kv_pieces[0]] + [shift(kv_pieces[k], "z", k) for k in range(1, nz)]
    kv_parts[1], down_parts = lax.optimization_barrier((kv_parts[1], down_parts))
    out_rel = call(
        functools.partial(out_grad_kernel, dims, own),
        [sds((width, oc), bf16)],
        [idx, mid, attn_b],
        [pltpu.VMEM((width, span), bf16)] * 2,
        flops=2 * span * width * oc,
    )[0]
    kv_parts[2], out_rel = lax.optimization_barrier((kv_parts[2], out_rel))
    me_t = idx[3]
    middle_mine = lax.dynamic_slice_in_dim(middle, me_t * part, part, 1)
    down_got = [down_parts[0]] + [shift(down_parts[k], "tensor", k) for k in range(1, n)]

    res = call(
        functools.partial(input_grad_kernel, dims, qc, kc),
        [sds((span, qkv), bf16), sds((8, width), f32), sds((HD, 1), f32)]
        + [sds((span + 16, part), bf16)] * n,
        [idx] + kv_parts + [raw_t, head_gains, cosine, sine, q_gb, w, base, gains],
        [pltpu.VMEM((span, width), f32)],
        flops=2 * span * width * qkv,
    )
    qkv_gb, gain_one, gk_grad = res[:3]
    norm_parts = res[3:]
    keep, send = call(
        functools.partial(attn_grad_kernel, dims, own, qc, kc, oc),
        [sds((width // 2, aw), bf16)] * 2,
        [idx, one_rel, out_rel, qkv_gb, gain_one, gain_two, gq_grad, gk_grad],
        [pltpu.VMEM((width, PAD), bf16)] * 2 + [pltpu.VMEM((width, PAD), f32), pltpu.VMEM((own, PAD), f32)],
        flops=2 * span * width * (qkv + oc),
    )
    (keep, send), down_got = lax.optimization_barrier(((keep, send), down_got))
    attn_pieces = core_sum(keep, send, nx)
    attn_got = [shift(attn_pieces[k], "dp", k) for k in range(1, nx)]
    attn_got[0], norm_parts, ffn_x = lax.optimization_barrier((attn_got[0], norm_parts, ffn_x))
    ffn_sum = lax.psum_scatter(ffn_x, "z", scatter_dimension=0, tiled=True)
    attn_x = sum([v.astype(f32) for v in attn_got], attn_pieces[0].astype(f32)).astype(bf16)
    norm_got = [norm_parts[0]] + [shift(norm_parts[k], "tensor", k) for k in range(1, n)]
    attn_x, norm_got = lax.optimization_barrier((attn_x, norm_got))
    z_parts = [attn_x[:own]] + [shift(attn_x[k * own : (k + 1) * own], "z", k) for k in range(1, nz)]
    wgrads = call(
        functools.partial(sum_kernel, (0, qc, qc + kc, qkv, qkv + oc, aw)),
        [sds((own, v), f32) for v in (qc, kc, kc, oc, PAD)],
        z_parts,
    )
    small = wgrads[4]
    block_output = (middle_mine + sum([v.astype(f32) for v in down_got[1:]], down_got[0].astype(f32))).astype(bf16)
    norm_mine = sum([v.astype(f32) for v in norm_got[1:]], norm_got[0].astype(f32))
    along = (norm_mine[span] + norm_mine[span + 1])[:, None] * (1.0 / width)
    base_f = base.astype(f32)
    scale_one = lax.rsqrt(jnp.mean(base_f * base_f, axis=1, keepdims=True) + EPS)
    unit_mine = block_input.reshape(span, part).astype(f32) * scale_one
    gain_mine = lax.dynamic_slice_in_dim(gains, me_t * part, part, 1)[0:1]
    input_grad = (mine + scale_one * (norm_mine[:span] * gain_mine - unit_mine * along)).astype(bf16)

    fgrads = call(
        functools.partial(sum_kernel, (0, ff, 2 * ff, 3 * ff)),
        [sds((own, ff), f32)] * 3,
        [ffn_sum],
    )
    small_all = sum(gathered(small, "tensor"))
    count = 2 * HD // own
    head_sum = (small_all[:, 4 : 4 + count] + small_all[:, 4 + count : 4 + 2 * count]).T.reshape(-1)
    return (
        block_output.reshape(span, seq_local, part),
        input_grad.reshape(span, seq_local, part),
        small_all[:, 0] + small_all[:, 1],
        small[:, 2] + small[:, 3],
        head_sum[:HD],
        head_sum[HD:],
        *wgrads[:4],
        *fgrads,
    )


def solution(mesh):
    dp, seq, tensor = (mesh.shape[a] for a in ("dp", "seq", "tensor"))
    grid = Mesh(
        np.asarray(mesh.devices).reshape(dp, seq // 2, 2, tensor), ("dp", "z", "core", "tensor")
    )
    tokens = P(("z", "core"), "dp", "tensor")
    rows = P(("dp", "z", "core"))
    weight = P(("dp", "z", "core"), "tensor")
    return jax.shard_map(
        body,
        mesh=grid,
        in_specs=(tokens, rows, rows, P(), P()) + (weight,) * 7 + (tokens,),
        out_specs=(tokens, tokens, rows, rows, P(), P()) + (weight,) * 7,
        check_vma=False,
    )
```

```python
import functools

import numpy as np
import jax
import jax.numpy as jnp
from jax import lax
from jax.experimental import pallas as pl
from jax.experimental.pallas import tpu as pltpu
from jax.sharding import Mesh, PartitionSpec as P

HD = 64
HALF = HD // 2
EPS = 1e-05
ROPE_BASE = 1000000.0
SCALE = HD ** (-0.5)
PAD = 128
bf16 = jnp.bfloat16
f32 = jnp.float32
NN = (((1,), (0,)), ((), ()))
NT = (((1,), (1,)), ((), ()))


def dot(a, b, dims=NN):
    return lax.dot_general(a, b, dims, preferred_element_type=f32)


def rot_index(a, k, n):
    return lax.rem(a + k, n)


def ds(start, size):
    return pl.ds(pl.multiple_of(start * size, size), size)


def shift(x, axis, k):
    n = lax.axis_size(axis)
    return lax.ppermute(x, axis, [(i, (i + k) % n) for i in range(n)])


def gathered(x, axis):
    return [x] + [shift(x, axis, k) for k in range(1, lax.axis_size(axis))]


def summed(pieces, axis):
    total = pieces[0].astype(f32)
    for k in range(1, lax.axis_size(axis)):
        total = total + shift(pieces[k], axis, k).astype(f32)
    return total


def call(kernel, outs, ins, scratch=(), grid=None, in_specs=None, out_specs=None, flops=0):
    vm = pl.BlockSpec(memory_space=pltpu.VMEM)
    nbytes = sum(x.size * x.dtype.itemsize for x in list(ins) + list(outs))
    kwargs = {} if grid is None else {"grid": grid}
    return pl.pallas_call(
        kernel,
        out_shape=outs,
        in_specs=in_specs or [pl.BlockSpec(memory_space=pltpu.SMEM) if x.dtype == jnp.int32 else vm for x in ins],
        out_specs=out_specs or [vm] * len(outs),
        scratch_shapes=list(scratch),
        cost_estimate=pl.CostEstimate(flops=flops, bytes_accessed=nbytes, transcendentals=0),
        **kwargs,
    )(*ins)


def sds(shape, dtype):
    return jax.ShapeDtypeStruct(shape, dtype)


def store_relative(dims, idx, dst, src, own):
    nx, nz, nc, _ = dims
    half = nx * nz
    for other in range(nc):
        core = idx[2] if other == 0 else 1 - idx[2]

        def step(i, carry, other=other, core=core):
            row = (rot_index(idx[0], i // nz, nx) * nz + rot_index(idx[1], i % nz, nz)) * nc + core
            dst[ds(other * half + i, own), :] = src[ds(row, own), :]
            return carry

        lax.fori_loop(0, half, step, 0)


def assemble(idx, n, pieces, dst, first=0):
    part = dst.shape[1] // n
    for k in range(n):
        dst[:, ds(rot_index(idx[3], n - k, n), part)] = pieces[k][:, first : first + part]


def cot_kernel(dims, own, idx, *refs):
    n = dims[3]
    pieces, (full,) = refs[:n], refs[n:]
    assemble(idx, n, pieces, full, full.shape[1] // n)


def head_columns(ref):
    turned = jnp.broadcast_to(ref[...].astype(f32), (8, 2 * HD)).T
    return turned[:HD, :1], turned[HD:, :1]


def to_groups(dst, rows):
    span = rows.shape[1]
    group = dst.shape[1] // span
    for h in range(rows.shape[0] // HD):
        g, at = h // group, h % group
        dst[g * HD : (g + 1) * HD, at * span : (at + 1) * span] = rows[h * HD : (h + 1) * HD]


def from_groups(x, span):
    group = x.shape[1] // span
    return jnp.concatenate(
        [
            x[h // group * HD : (h // group + 1) * HD, h % group * span : (h % group + 1) * span]
            for h in range(x.shape[0] // HD * group)
        ],
        axis=0,
    )


def turn_heads(raw, gain, cosine, sine, heads):
    outs = []
    for h in range(heads):
        v = raw[h * HD : (h + 1) * HD]
        v = v * lax.rsqrt(jnp.mean(v * v, axis=0, keepdims=True) + EPS) * gain
        a, b = v[:HALF], v[HALF:]
        outs += [a * cosine - b * sine, b * cosine + a * sine]
    return jnp.concatenate(outs, axis=0)


def turn_heads_back(raw, grad, gain, cosine, sine, heads):
    outs, gain_grad = [], jnp.zeros((HD, 1), f32)
    for h in range(heads):
        v = raw[h * HD : (h + 1) * HD]
        g = grad[h * HD : (h + 1) * HD]
        ga, gb = g[:HALF], g[HALF:]
        g = jnp.concatenate([ga * cosine + gb * sine, gb * cosine - ga * sine], axis=0)
        r = lax.rsqrt(jnp.mean(v * v, axis=0, keepdims=True) + EPS)
        n = v * r
        gain_grad = gain_grad + jnp.sum(g * n, axis=1, keepdims=True)
        g = g * gain
        outs.append(r * (g - n * jnp.mean(g * n, axis=0, keepdims=True)))
    return jnp.concatenate(outs, axis=0), gain_grad


def qkv_kernel(dims, own, qc, kc, oc, idx, *refs):
    nx, nz, nc, n = dims
    pieces = refs[:n]
    w_parts = refs[n : n + 2 * nx]
    head_gains, cosine, sine = refs[n + 2 * nx : n + 2 * nx + 3]
    w, base, gains, q_t, raw_t, kv, rel, turned = refs[n + 2 * nx + 3 :]
    gq, gk = head_columns(head_gains)
    assemble(idx, n, pieces, base)
    for other in range(nc):
        core = idx[2] if other == 0 else 1 - idx[2]
        for xr in range(nx):
            src = w_parts[other * nx + xr]

            def step(zr, carry, src=src, xr=xr, core=core):
                row = (rot_index(idx[0], nx - xr, nx) * nz + rot_index(idx[1], nz - zr, nz)) * nc + core
                w[ds(row, own), :] = src[ds(zr, own), :]
                return carry

            lax.fori_loop(0, nz, step, 0)
    qkv = qc + 2 * kc
    gains[...] = w[:, qkv:].astype(f32).T[:8]
    b = base[...].astype(f32)
    normed = b * lax.rsqrt(jnp.mean(b * b, axis=1, keepdims=True) + EPS) * gains[0:1, :]
    normed = normed.astype(bf16)
    raw = dot(normed, w[:, :qkv])
    turned[...] = normed.T
    store_relative(dims, idx, rel, turned, own)
    kv[:, kc:] = raw[:, qc + kc :].astype(bf16)
    rt = raw[:, : qc + kc].T
    raw_t[...] = rt
    co, si = cosine[...], sine[...]
    q = (turn_heads(rt[:qc], gq, co, si, qc // HD) * SCALE).astype(bf16)
    to_groups(q_t, q)
    kv[:, :kc] = turn_heads(rt[qc:], gk, co, si, kc // HD).T.astype(bf16)


def attend_kernel(dims, qc, kc, oc, idx, q_t, *refs):
    nx, nz, nc, n = dims
    kv_parts = refs[: nz * nc]
    kv, attn_t, attn_b, log_total, acc, tot = refs[nz * nc :]
    span = attn_b.shape[0]
    group = qc // kc
    me = idx[1] * nc + idx[2]
    for other in range(nc):
        core = idx[2] if other == 0 else 1 - idx[2]
        for zr in range(nz):
            block = rot_index(idx[1], nz - zr, nz) * nc + core
            kv[ds(block, span), :] = kv_parts[other * nz + zr][...]
    acc[...] = jnp.zeros_like(acc)
    tot[...] = jnp.zeros_like(tot)
    keys_at = lax.broadcasted_iota(jnp.int32, (span, span), 0)
    query_at = lax.broadcasted_iota(jnp.int32, (span, span), 1)
    ahead = keys_at - query_at
    ahead = jnp.concatenate([ahead] * group, axis=1)

    def step(j, carry):
        vt = kv[ds(j, span), kc:].T
        allowed = ahead <= (me - j) * span
        for g in range(kc // HD):
            rows = slice(g * HD, (g + 1) * HD)
            s = dot(kv[ds(j, span), rows], q_t[rows, :])
            e = jnp.where(allowed, jnp.exp(s), 0.0)
            tot[g : g + 1, :] += jnp.sum(e, axis=0, keepdims=True)
            acc[rows, :] += dot(vt[rows], e.astype(bf16))
        return carry

    lax.fori_loop(0, me + 1, step, 0)
    for g in range(kc // HD):
        rows = slice(g * HD, (g + 1) * HD)
        attn_t[rows, :] = acc[rows, :] / tot[g : g + 1, :]
    log_total[...] = jnp.log(jnp.maximum(tot[...], 1e-30))
    attn = from_groups(attn_t[...], span).T.astype(bf16)
    attn_b[...] = attn


def out_kernel(dims, idx, attn_b, w_low, w_high, *pieces):
    n = dims[3]
    attn = attn_b[...]
    part = w_low.shape[0] // n
    for k in range(n):
        rows = ds(rot_index(idx[3], k, n), part)
        out = dot(attn[:, :PAD], w_low[rows, :], NT) + dot(attn[:, PAD:], w_high[rows, :], NT)
        pieces[k][...] = out.astype(bf16)


def hidden_grad_kernel(cot, wd, out):
    out[...] = dot(cot[...], wd[...])


def ffn_kernel(dims, own, idx, base, gains, *refs):
    n = dims[3]
    sums = refs[:n]
    wg, wu, hgrad = refs[n : n + 3]
    middle, normed, big = refs[n + 3 : n + 6]
    pieces = refs[n + 6 : n + 6 + n]
    acc = refs[n + 6 + n]
    j = pl.program_id(0)
    part = sums[0].shape[1]

    @pl.when(j == 0)
    def _():
        for k in range(n):
            at = ds(rot_index(idx[3], n - k, n), part)
            middle[:, at] = base[:, at].astype(f32) + sums[k][...].astype(f32)
        m = middle[...]
        v = m * lax.rsqrt(jnp.mean(m * m, axis=1, keepdims=True) + EPS) * gains[1:2, :]
        v = v.astype(bf16)
        normed[...] = v
        acc[...] = jnp.zeros_like(acc)

    v = normed[...]
    block = wg.shape[1]
    ff = big.shape[1] // 3
    gate = dot(v, wg[...])
    up = dot(v, wu[...])
    hg = hgrad[...]
    sig = 1.0 / (1.0 + jnp.exp(-gate))
    act = gate * sig
    hidden = (act * up).astype(bf16)
    gate_gb = (hg * up * (sig + act * (1.0 - sig))).astype(bf16)
    up_gb = (hg * act).astype(bf16)
    big[:, pl.ds(pl.multiple_of(j * block, block), block)] = gate_gb
    big[:, pl.ds(pl.multiple_of(ff + j * block, PAD), block)] = up_gb
    big[:, pl.ds(pl.multiple_of(2 * ff + j * block, PAD), block)] = hidden
    acc[...] += dot(gate_gb, wg[...], NT) + dot(up_gb, wu[...], NT)

    @pl.when(j == pl.num_programs(0) - 1)
    def _():
        for k in range(n):
            pieces[k][...] = acc[:, ds(rot_index(idx[3], k, n), part)].astype(bf16)


def down_kernel(dims, idx, hidden, wd, *refs):
    n = dims[3]
    part = wd.shape[0] // n
    for k in range(n):
        rows = ds(rot_index(idx[3], k, n), part)
        refs[k][...] = dot(hidden[...], wd[rows, :], NT).astype(bf16)


def rows_kernel(dims, own, idx, mine, partner, out, turned):
    nx, nz, nc, _ = dims
    span = mine.shape[0]
    for k, src in enumerate((mine, partner)):
        turned[...] = src[...].T

        def step(i, carry, k=k):
            out[ds(i, own), k * span : (k + 1) * span] = turned[ds(i * nc + idx[2], own), :]
            return carry

        lax.fori_loop(0, nx * nz, step, 0)


def ffn_grad_kernel(normed_rows, cot_rows, big, partner_big, out, left):
    j = pl.program_id(0)

    @pl.when(j == 0)
    def _():
        left[...] = normed_rows[...]

    @pl.when(j == 2)
    def _():
        left[...] = cot_rows[...]

    span = big.shape[0]
    out[...] = (dot(left[:, :span], big[...]) + dot(left[:, span:], partner_big[...])).astype(bf16)


def attend_back_kernel(dims, own, qc, kc, oc, idx, middle, gains, cot, *refs):
    nx, nz, nc, n = dims
    grads = refs[:n]
    w_low, w_high, attn_t, q_t, raw_t, kv, log_total, head_gains, cosine, sine = refs[n : n + 10]
    mine, mid, gain_two, q_gb, gq_grad, kv_keep, kv_send = refs[n + 10 : n + 17]
    full, dq, do_t, delta, mid_grad, do_f, q_n, do_n, out = refs[n + 17 :]
    span = mine.shape[0]
    group = qc // kc
    me = idx[1] * nc + idx[2]
    assemble(idx, n, grads, full)
    m = middle[...]
    r = lax.rsqrt(jnp.mean(m * m, axis=1, keepdims=True) + EPS)
    unit = m * r
    ng = full[...].astype(f32)
    gain_two[...] = jnp.broadcast_to(jnp.sum(ng * unit, axis=0, keepdims=True), gain_two.shape)
    gg = ng * gains[1:2, :]
    mg = cot[...].astype(f32) + r * (gg - unit * jnp.mean(gg * unit, axis=1, keepdims=True))
    mid_grad[...] = mg
    part = grads[0].shape[1]
    mine[...] = mid_grad[:, ds(idx[3], part)]
    mgb = mg.astype(bf16)
    mid[...] = mgb
    ag = jnp.concatenate([dot(mgb, w_low[...]), dot(mgb, w_high[...])], axis=1)
    to_groups(do_f, ag.T)
    prod = do_f[...] * attn_t[...]
    do_t[...] = do_f[...].astype(bf16)
    for g in range(kc // HD):
        rows = slice(g * HD, (g + 1) * HD)
        delta[g : g + 1, :] = jnp.sum(prod[rows], axis=0, keepdims=True)
        q_n[g * q_t.shape[1] : (g + 1) * q_t.shape[1], :] = q_t[rows, :].T
        do_n[g * q_t.shape[1] : (g + 1) * q_t.shape[1], :] = do_t[rows, :].T
    dq[...] = jnp.zeros_like(dq)
    keys_at = lax.broadcasted_iota(jnp.int32, (span, span), 0)
    query_at = lax.broadcasted_iota(jnp.int32, (span, span), 1)
    ahead = keys_at - query_at
    ahead = jnp.concatenate([ahead] * group, axis=1)
    def step(t, carry):
        other = t // nz
        j = rot_index(idx[1], t % nz, nz) * nc + lax.rem(idx[2] + other, nc)
        at = ds(t, span)

        @pl.when(j > me)
        def _():
            out[at, :] = jnp.zeros((span, 2 * kc), bf16)

        @pl.when(j <= me)
        def _():
            kt = kv[ds(j, span), :kc].T
            allowed = ahead <= (me - j) * span
            wide = q_t.shape[1]
            for g in range(kc // HD):
                rows = slice(g * HD, (g + 1) * HD)
                s = dot(kv[ds(j, span), rows], q_t[rows, :])
                p = jnp.where(allowed, jnp.exp(s - log_total[g : g + 1, :]), 0.0)
                dp = dot(kv[ds(j, span), kc + g * HD : kc + (g + 1) * HD], do_t[rows, :])
                sg = (p * (dp - delta[g : g + 1, :])).astype(bf16)
                dq[rows, :] += dot(kt[rows], sg)
                dk = dot(sg, q_n[g * wide : (g + 1) * wide, :])
                dv = dot(p.astype(bf16), do_n[g * wide : (g + 1) * wide, :])
                out[at, rows] = dk.astype(bf16)
                out[at, kc + g * HD : kc + (g + 1) * HD] = dv.astype(bf16)

        return carry

    lax.fori_loop(0, nz * nc, step, 0)
    kv_keep[...] = out[: nz * span, :]
    kv_send[...] = out[nz * span :, :]
    raw_grad, gain_grad = turn_heads_back(
        raw_t[:qc, :], from_groups(dq[...], span) * SCALE, head_columns(head_gains)[0], cosine[...], sine[...], qc // HD
    )
    gq_grad[...] = gain_grad
    q_gb[...] = raw_grad.T.astype(bf16)


def input_grad_kernel(dims, qc, kc, idx, *refs):
    n, nz = dims[3], dims[1]
    kv_parts = refs[:nz]
    raw_t, head_gains, cosine, sine, q_gb, w, base, gains = refs[nz : nz + 8]
    qkv_gb, gain_one, gk_grad = refs[nz + 8 : nz + 11]
    pieces = refs[nz + 11 : nz + 11 + n]
    acc = refs[nz + 11 + n]
    total = kv_parts[0][...].astype(f32)
    for k in range(1, nz):
        total = total + kv_parts[k][...].astype(f32)
    raw_grad, gain_grad = turn_heads_back(
        raw_t[qc:, :], total[:, :kc].T, head_columns(head_gains)[1], cosine[...], sine[...], kc // HD
    )
    gk_grad[...] = gain_grad
    qkv_gb[:, :qc] = q_gb[...]
    qkv_gb[:, qc : qc + kc] = raw_grad.T.astype(bf16)
    qkv_gb[:, qc + kc :] = total[:, kc:].astype(bf16)
    ng = dot(qkv_gb[...], w[:, : qc + 2 * kc], NT)
    acc[...] = ng
    b = base[...].astype(f32)
    unit = b * lax.rsqrt(jnp.mean(b * b, axis=1, keepdims=True) + EPS)
    prod = ng * unit
    gain_one[...] = jnp.broadcast_to(jnp.sum(prod, axis=0, keepdims=True), gain_one.shape)
    along = jnp.sum(prod * gains[0:1, :], axis=1, keepdims=True)
    along = jnp.broadcast_to(along, (along.shape[0], PAD)).T[:16]
    high = along.astype(bf16)
    low = (along - high.astype(f32)).astype(bf16)
    row = lax.broadcasted_iota(jnp.int32, along.shape, 0)
    tail = jnp.where(row == 0, high.astype(f32), low.astype(f32)).astype(bf16)
    part = acc.shape[1] // n
    for k in range(n):
        pieces[k][: along.shape[1], :] = acc[:, ds(rot_index(idx[3], k, n), part)].astype(bf16)
        pieces[k][along.shape[1] :, :] = tail


def attn_grad_kernel(dims, own, qc, kc, oc, idx, one_rel, out_rel, qkv_gb, gain_one, gain_two, gq_grad, gk_grad, keep, send, extra, extra_rel, lined, spread):
    half = keep.shape[0]
    qkv = qc + 2 * kc
    width = one_rel.shape[0]

    def halves(v):
        high = v.astype(bf16).astype(f32)
        return high, v - high

    rows = lax.broadcasted_iota(jnp.int32, (PAD, width), 0)
    lines = jnp.zeros((PAD, width), f32)
    values = halves(gain_one[0:1, :]) + halves(gain_two[0:1, :])
    for i, v in enumerate(values):
        lines = lines + jnp.where(rows == i, v, 0.0)
    cols = lines.T
    heads = jnp.concatenate([gq_grad[...], gk_grad[...]], axis=0)
    high, low = halves(heads)
    lane = lax.broadcasted_iota(jnp.int32, (own, PAD), 1)
    tile = jnp.zeros((own, PAD), f32)
    count = 2 * HD // own
    for i in range(count):
        at = slice(i * own, (i + 1) * own)
        tile = tile + jnp.where(lane == 4 + i, high[at], 0.0)
        tile = tile + jnp.where(lane == 4 + count + i, low[at], 0.0)
    lined[...] = cols
    spread[...] = tile

    def step(i, carry):
        extra[ds(i, own), :] = (lined[ds(i, own), :] + spread[...]).astype(bf16)
        return carry

    lax.fori_loop(0, width // own, step, 0)
    store_relative(dims, idx, extra_rel, extra, own)
    a = dot(one_rel[...], qkv_gb[...]).astype(bf16)
    for out, at in ((keep, slice(0, half)), (send, slice(half, 2 * half))):
        out[:, :qkv] = a[at]
        out[:, qkv : qkv + oc] = out_rel[at, :]
        out[:, qkv + oc :] = extra_rel[at, :]


def sum_kernel(cuts, *refs):
    outs = refs[len(refs) - len(cuts) + 1 :]
    ins = refs[: len(refs) - len(cuts) + 1]
    for out, first, last in zip(outs, cuts[:-1], cuts[1:]):
        total = ins[0][:, first:last].astype(f32)
        for v in ins[1:]:
            total = total + v[:, first:last].astype(f32)
        out[...] = total


def pack_kernel(q, k, v, o, g, u, d, gain_one, gain_two, x, c, attn, ffn, both, square):
    at = 0
    for w in (q, k, v):
        attn[:, at : at + w.shape[1]] = w[...]
        at += w.shape[1]
    own = q.shape[0]
    square[...] = jnp.zeros_like(square)
    square[0:1, :own] = gain_one[...].astype(f32)
    square[1:2, :own] = gain_two[...].astype(f32)
    attn[:, at:] = square[...].T[:own].astype(bf16)
    at = 0
    for w in (g, u, d, o):
        ffn[:, at : at + w.shape[1]] = w[...]
        at += w.shape[1]
    part = x.shape[1]
    both[:, :part] = x[...]
    both[:, part:] = c[...]


def out_grad_kernel(dims, own, idx, mid, attn_b, out, turned, rel):
    turned[...] = mid[...].T
    store_relative(dims, idx, rel, turned, own)
    out[...] = dot(rel[...], attn_b[...]).astype(bf16)


def core_sum(keep, send, n):
    got = shift(send, "core", 1)
    step = keep.shape[0] // n
    return [
        (keep[k * step : (k + 1) * step].astype(f32) + got[k * step : (k + 1) * step].astype(f32)).astype(bf16)
        for k in range(n)
    ]


def row_sum(x, axis):
    step = x.shape[0] // lax.axis_size(axis)
    return summed([x[k * step : (k + 1) * step] for k in range(lax.axis_size(axis))], axis)


def after(values, others):
    return lax.optimization_barrier((list(values), others))[0]


def body(
    block_input,
    attn_gain,
    ffn_gain,
    query_gain,
    key_gain,
    query_weight,
    key_weight,
    value_weight,
    out_weight,
    gate_weight,
    up_weight,
    down_weight,
    cotangent,
):
    span, seq_local, part = block_input.shape
    axes = ("dp", "z", "core", "tensor")
    dims = tuple(lax.axis_size(a) for a in axes)
    nx, nz, nc, n = dims
    idx = jnp.stack([lax.axis_index(a) for a in axes]).astype(jnp.int32)
    width = part * n
    own = query_weight.shape[0]
    qc, kc, oc, ff = (w.shape[1] for w in (query_weight, key_weight, out_weight, gate_weight))
    qkv = qc + 2 * kc
    aw = qkv + oc + PAD

    attn_local, ffn_local, both = call(
        pack_kernel,
        [sds((own, qkv + PAD), bf16), sds((own, 3 * ff + oc), bf16), sds((span, 2 * part), bf16)],
        [query_weight, key_weight, value_weight, out_weight, gate_weight, up_weight, down_weight]
        + [attn_gain[None, :], ffn_gain[None, :], block_input.reshape(span, part), cotangent.reshape(span, part)],
        [pltpu.VMEM((PAD, PAD), f32)],
    )
    ffn_w = lax.all_gather(ffn_local, ("dp", "z", "core"), axis=0, tiled=True)
    by_z = jnp.concatenate(gathered(attn_local, "z"), axis=0)
    both_parts = gathered(both, "tensor")
    my_first = (idx[1] * nc + idx[2]) * span
    positions = (my_first + jnp.arange(span, dtype=jnp.int32)).astype(f32)
    frequency = jnp.power(ROPE_BASE, -2.0 * jnp.arange(HALF, dtype=f32) / HD)
    angle = frequency[:, None] * positions[None, :]
    cosine, sine = jnp.cos(angle), jnp.sin(angle)
    head_gains = jnp.concatenate([query_gain, key_gain])[None, :]
    dp_parts = gathered(by_z, "dp")
    dp_parts, both_parts, cosine, sine, head_gains = lax.optimization_barrier(
        (dp_parts, both_parts, cosine, sine, head_gains)
    )
    dp_partner = [shift(v, "core", 1) for v in dp_parts]
    cot = call(
        functools.partial(cot_kernel, dims, own),
        [sds((span, width), bf16)],
        [idx] + both_parts,
    )[0]

    def core_rows(x):
        return call(
            functools.partial(rows_kernel, dims, own),
            [sds((width // nc, nc * span), bf16)],
            [idx, x, shift(x, "core", 1)],
            [pltpu.VMEM((width, span), bf16)],
        )[0]

    cot_rows = core_rows(cot)

    w, base, gains, q_t, raw_t, kv, one_rel = call(
        functools.partial(qkv_kernel, dims, own, qc, kc, oc),
        [
            sds((width, qkv + PAD), bf16),
            sds((span, width), bf16),
            sds((8, width), f32),
            sds((kc, qc // kc * span), bf16),
            sds((qc + kc, span), f32),
            sds((span, 2 * kc), bf16),
            sds((width, span), bf16),
        ],
        [idx] + both_parts + dp_parts + dp_partner + [head_gains, cosine, sine],
        [pltpu.VMEM((width, span), bf16)],
        flops=2 * span * width * qkv,
    )
    kv_own = gathered(kv, "z")
    kv_partner = [shift(v, "core", 1) for v in kv_own]

    length = span * nz * nc
    block = 384
    const = lambda s: pl.BlockSpec(s, lambda j: (0, 0))
    steps = ff // block
    out_blocks = [pl.BlockSpec((width, PAD), lambda j, o=o: (0, o)) for o in (3 * ff // PAD, 3 * ff // PAD + 1)]
    kv_full, attn_t, attn_b, log_total = call(
        functools.partial(attend_kernel, dims, qc, kc, oc),
        [sds((length, 2 * kc), bf16), sds(q_t.shape, f32), sds((span, qc), bf16), sds((8, q_t.shape[1]), f32)],
        [idx, q_t] + kv_own + kv_partner,
        [pltpu.VMEM(q_t.shape, f32), pltpu.VMEM((8, q_t.shape[1]), f32)],
        flops=4 * span * length * qc,
    )
    res = call(
        functools.partial(out_kernel, dims),
        [sds((span, part), bf16)] * n,
        [idx, attn_b, ffn_w, ffn_w],
        grid=(1,),
        in_specs=[pl.BlockSpec(memory_space=pltpu.SMEM), const((span, qc))] + out_blocks,
        out_specs=[const((span, part))] * n,
        flops=2 * span * width * qc,
    )
    attn_mine = summed(res, "tensor").astype(bf16)
    attn_parts = gathered(attn_mine, "tensor")
    attn_parts, cot_rows = lax.optimization_barrier((attn_parts, cot_rows))

    hgrad = call(
        hidden_grad_kernel,
        [sds((span, ff), f32)],
        [cot, ffn_w],
        grid=(steps,),
        in_specs=[const((span, width)), pl.BlockSpec((width, block), lambda j: (0, 2 * steps + j))],
        out_specs=[pl.BlockSpec((span, block), lambda j: (0, j))],
        flops=2 * span * width * ff,
    )[0]
    res = call(
        functools.partial(ffn_kernel, dims, own),
        [sds((span, width), f32), sds((span, width), bf16), sds((span, 3 * ff), bf16)]
        + [sds((span, part), bf16)] * n,
        [idx, base, gains] + attn_parts + [ffn_w, ffn_w, hgrad],
        [pltpu.VMEM((span, width), f32)],
        grid=(steps,),
        in_specs=[pl.BlockSpec(memory_space=pltpu.SMEM)]
        + [const((span, width)), const((8, width))]
        + [const((span, part))] * n
        + [pl.BlockSpec((width, block), lambda j, o=o: (0, o + j)) for o in (0, steps)]
        + [pl.BlockSpec((span, block), lambda j: (0, j))],
        out_specs=[const((span, width)), const((span, width)), const((span, 3 * ff))]
        + [const((span, part))] * n,
        flops=8 * span * width * ff,
    )
    middle, normed_two, big = res[:3]
    grad_got = [shift(res[3 + k], "tensor", k) for k in range(1, n)]
    part_zero = res[3]

    ffn_half = call(
        ffn_grad_kernel,
        [sds((width // nc, 3 * ff), bf16)],
        [core_rows(normed_two), cot_rows, big, shift(big, "core", 1)],
        [pltpu.VMEM((width // nc, nc * span), bf16)],
        grid=(3,),
        in_specs=[const((width // nc, nc * span))] * 2 + [pl.BlockSpec((span, ff), lambda j: (0, j))] * 2,
        out_specs=[pl.BlockSpec((width // nc, ff), lambda j: (0, j))],
        flops=6 * span * width * ff,
    )[0]
    grad_got, ffn_half = lax.optimization_barrier((grad_got, ffn_half))
    grad_mine = sum([g.astype(f32) for g in grad_got], part_zero.astype(f32)).astype(bf16)
    grad_parts = gathered(grad_mine, "tensor")
    down_parts = call(
        functools.partial(down_kernel, dims),
        [sds((span, part), bf16)] * n,
        [idx, big, ffn_w],
        grid=(1,),
        in_specs=[
            pl.BlockSpec(memory_space=pltpu.SMEM),
            pl.BlockSpec((span, ff), lambda j: (0, 2)),
            pl.BlockSpec((width, ff), lambda j: (0, 2)),
        ],
        out_specs=[const((span, part))] * n,
        flops=2 * span * width * ff,
    )
    grad_parts, down_parts = lax.optimization_barrier((grad_parts, down_parts))
    ffn_sum = lax.psum_scatter(ffn_half, ("dp", "z"), scatter_dimension=0, tiled=True)

    mine, mid, gain_two, q_gb, gq_grad, kv_keep, kv_send = call(
        functools.partial(attend_back_kernel, dims, own, qc, kc, oc),
        [
            sds((span, part), f32),
            sds((span, width), bf16),
            sds((8, width), f32),
            sds((span, qc), bf16),
            sds((HD, 1), f32),
            sds((length // 2, 2 * kc), bf16),
            sds((length // 2, 2 * kc), bf16),
        ],
        [idx, middle, gains, cot] + grad_parts + [ffn_w, ffn_w, attn_t, q_t, raw_t, kv_full, log_total, head_gains, cosine, sine],
        [
            pltpu.VMEM((span, width), bf16),
            pltpu.VMEM(q_t.shape, f32),
            pltpu.VMEM(q_t.shape, bf16),
            pltpu.VMEM((8, q_t.shape[1]), f32),
            pltpu.VMEM((span, width), f32),
            pltpu.VMEM(q_t.shape, f32),
            pltpu.VMEM((kc // HD * q_t.shape[1], HD), bf16),
            pltpu.VMEM((kc // HD * q_t.shape[1], HD), bf16),
            pltpu.VMEM((length, 2 * kc), bf16),
        ],
        grid=(1,),
        in_specs=[pl.BlockSpec(memory_space=pltpu.SMEM), const((span, width)), const((8, width)), const((span, width))]
        + [const((span, part))] * n
        + out_blocks
        + [const(v.shape) for v in (attn_t, q_t, raw_t, kv_full, log_total, head_gains, cosine, sine)],
        out_specs=[
            const((span, part)),
            const((span, width)),
            const((8, width)),
            const((span, qc)),
            const((HD, 1)),
            const((length // 2, 2 * kc)),
            const((length // 2, 2 * kc)),
        ],
        flops=10 * span * length * qc,
    )
    kv_pieces = core_sum(kv_keep, kv_send, nz)
    kv_parts = [kv_pieces[0]] + [shift(kv_pieces[k], "z", k) for k in range(1, nz)]
    kv_parts[1], down_parts = lax.optimization_barrier((kv_parts[1], down_parts))
    out_rel = call(
        functools.partial(out_grad_kernel, dims, own),
        [sds((width, oc), bf16)],
        [idx, mid, attn_b],
        [pltpu.VMEM((width, span), bf16)] * 2,
        flops=2 * span * width * oc,
    )[0]
    kv_parts[2], out_rel = lax.optimization_barrier((kv_parts[2], out_rel))
    me_t = idx[3]
    middle_mine = lax.dynamic_slice_in_dim(middle, me_t * part, part, 1)
    down_got = [down_parts[0]] + [shift(down_parts[k], "tensor", k) for k in range(1, n)]

    res = call(
        functools.partial(input_grad_kernel, dims, qc, kc),
        [sds((span, qkv), bf16), sds((8, width), f32), sds((HD, 1), f32)]
        + [sds((span + 16, part), bf16)] * n,
        [idx] + kv_parts + [raw_t, head_gains, cosine, sine, q_gb, w, base, gains],
        [pltpu.VMEM((span, width), f32)],
        flops=2 * span * width * qkv,
    )
    qkv_gb, gain_one, gk_grad = res[:3]
    norm_parts = res[3:]
    keep, send = call(
        functools.partial(attn_grad_kernel, dims, own, qc, kc, oc),
        [sds((width // 2, aw), bf16)] * 2,
        [idx, one_rel, out_rel, qkv_gb, gain_one, gain_two, gq_grad, gk_grad],
        [pltpu.VMEM((width, PAD), bf16)] * 2 + [pltpu.VMEM((width, PAD), f32), pltpu.VMEM((own, PAD), f32)],
        flops=2 * span * width * (qkv + oc),
    )
    (keep, send), down_got = lax.optimization_barrier(((keep, send), down_got))
    attn_pieces = core_sum(keep, send, nx)
    attn_got = [shift(attn_pieces[k], "dp", k) for k in range(1, nx)]
    attn_got[0], norm_parts = lax.optimization_barrier((attn_got[0], norm_parts))
    attn_x = sum([v.astype(f32) for v in attn_got], attn_pieces[0].astype(f32)).astype(bf16)
    norm_got = [norm_parts[0]] + [shift(norm_parts[k], "tensor", k) for k in range(1, n)]
    attn_x, norm_got = lax.optimization_barrier((attn_x, norm_got))
    z_parts = [attn_x[:own]] + [shift(attn_x[k * own : (k + 1) * own], "z", k) for k in range(1, nz)]
    wgrads = call(
        functools.partial(sum_kernel, (0, qc, qc + kc, qkv, qkv + oc, aw)),
        [sds((own, v), f32) for v in (qc, kc, kc, oc, PAD)],
        z_parts,
    )
    small = wgrads[4]
    block_output = (middle_mine + sum([v.astype(f32) for v in down_got[1:]], down_got[0].astype(f32))).astype(bf16)
    norm_mine = sum([v.astype(f32) for v in norm_got[1:]], norm_got[0].astype(f32))
    along = (norm_mine[span] + norm_mine[span + 1])[:, None] * (1.0 / width)
    base_f = base.astype(f32)
    scale_one = lax.rsqrt(jnp.mean(base_f * base_f, axis=1, keepdims=True) + EPS)
    unit_mine = block_input.reshape(span, part).astype(f32) * scale_one
    gain_mine = lax.dynamic_slice_in_dim(gains, me_t * part, part, 1)[0:1]
    input_grad = (mine + scale_one * (norm_mine[:span] * gain_mine - unit_mine * along)).astype(bf16)

    fgrads = call(
        functools.partial(sum_kernel, (0, ff, 2 * ff, 3 * ff)),
        [sds((own, ff), f32)] * 3,
        [ffn_sum],
    )
    small_all = sum(gathered(small, "tensor"))
    count = 2 * HD // own
    head_sum = (small_all[:, 4 : 4 + count] + small_all[:, 4 + count : 4 + 2 * count]).T.reshape(-1)
    return (
        block_output.reshape(span, seq_local, part),
        input_grad.reshape(span, seq_local, part),
        small_all[:, 0] + small_all[:, 1],
        small[:, 2] + small[:, 3],
        head_sum[:HD],
        head_sum[HD:],
        *wgrads[:4],
        *fgrads,
    )


def solution(mesh):
    dp, seq, tensor = (mesh.shape[a] for a in ("dp", "seq", "tensor"))
    grid = Mesh(
        np.asarray(mesh.devices).reshape(dp, seq // 2, 2, tensor), ("dp", "z", "core", "tensor")
    )
    tokens = P(("z", "core"), "dp", "tensor")
    rows = P(("dp", "z", "core"))
    weight = P(("dp", "z", "core"), "tensor")
    return jax.shard_map(
        body,
        mesh=grid,
        in_specs=(tokens, rows, rows, P(), P()) + (weight,) * 7 + (tokens,),
        out_specs=(tokens, tokens, rows, rows, P(), P()) + (weight,) * 7,
        check_vma=False,
    )
```

```python
import functools

import numpy as np
import jax
import jax.numpy as jnp
from jax import lax
from jax.experimental import pallas as pl
from jax.experimental.pallas import tpu as pltpu
from jax.sharding import Mesh, PartitionSpec as P

HD = 64
HALF = HD // 2
EPS = 1e-05
ROPE_BASE = 1000000.0
SCALE = HD ** (-0.5)
PAD = 128
bf16 = jnp.bfloat16
f32 = jnp.float32
NN = (((1,), (0,)), ((), ()))
NT = (((1,), (1,)), ((), ()))


def dot(a, b, dims=NN):
    return lax.dot_general(a, b, dims, preferred_element_type=f32)


def rot_index(a, k, n):
    return lax.rem(a + k, n)


def ds(start, size):
    if isinstance(start, int):
        return pl.ds(start * size, size)
    return pl.ds(pl.multiple_of(start * size, size), size)


def shift(x, axis, k):
    n = lax.axis_size(axis)
    return lax.ppermute(x, axis, [(i, (i + k) % n) for i in range(n)])


def gathered(x, axis):
    return [x] + [shift(x, axis, k) for k in range(1, lax.axis_size(axis))]


def summed(pieces, axis):
    total = pieces[0].astype(f32)
    for k in range(1, lax.axis_size(axis)):
        total = total + shift(pieces[k], axis, k).astype(f32)
    return total


def call(kernel, outs, ins, scratch=(), grid=None, in_specs=None, out_specs=None, flops=0):
    vm = pl.BlockSpec(memory_space=pltpu.VMEM)
    nbytes = sum(x.size * x.dtype.itemsize for x in list(ins) + list(outs))
    kwargs = {} if grid is None else {"grid": grid}
    return pl.pallas_call(
        kernel,
        out_shape=outs,
        in_specs=in_specs or [pl.BlockSpec(memory_space=pltpu.SMEM) if x.dtype == jnp.int32 else vm for x in ins],
        out_specs=out_specs or [vm] * len(outs),
        scratch_shapes=list(scratch),
        cost_estimate=pl.CostEstimate(flops=flops, bytes_accessed=nbytes, transcendentals=0),
        **kwargs,
    )(*ins)


def sds(shape, dtype):
    return jax.ShapeDtypeStruct(shape, dtype)


def store_relative(dims, idx, dst, src, own):
    nx, nz, nc, _ = dims
    half = nx * nz
    for other in range(nc):
        core = idx[2] if other == 0 else 1 - idx[2]

        def step(i, carry, other=other, core=core):
            row = (rot_index(idx[0], i // nz, nx) * nz + rot_index(idx[1], i % nz, nz)) * nc + core
            dst[ds(other * half + i, own), :] = src[ds(row, own), :]
            return carry

        for i in range(half):
            step(i, 0)


def assemble(idx, n, pieces, dst, first=0):
    part = dst.shape[1] // n
    for k in range(n):
        dst[:, ds(rot_index(idx[3], n - k, n), part)] = pieces[k][:, first : first + part]


def cot_kernel(dims, own, idx, *refs):
    n = dims[3]
    pieces, (full,) = refs[:n], refs[n:]
    assemble(idx, n, pieces, full, full.shape[1] // n)


def head_columns(ref):
    turned = jnp.broadcast_to(ref[...].astype(f32), (8, 2 * HD)).T
    return turned[:HD, :1], turned[HD:, :1]


def to_groups(dst, rows):
    span = rows.shape[1]
    group = dst.shape[1] // span
    for h in range(rows.shape[0] // HD):
        g, at = h // group, h % group
        dst[g * HD : (g + 1) * HD, at * span : (at + 1) * span] = rows[h * HD : (h + 1) * HD]


def from_groups(x, span):
    group = x.shape[1] // span
    return jnp.concatenate(
        [
            x[h // group * HD : (h // group + 1) * HD, h % group * span : (h % group + 1) * span]
            for h in range(x.shape[0] // HD * group)
        ],
        axis=0,
    )


def turn_heads(raw, gain, cosine, sine, heads):
    outs = []
    for h in range(heads):
        v = raw[h * HD : (h + 1) * HD]
        v = v * lax.rsqrt(jnp.mean(v * v, axis=0, keepdims=True) + EPS) * gain
        a, b = v[:HALF], v[HALF:]
        outs += [a * cosine - b * sine, b * cosine + a * sine]
    return jnp.concatenate(outs, axis=0)


def turn_heads_back(raw, grad, gain, cosine, sine, heads):
    outs, gain_grad = [], jnp.zeros((HD, 1), f32)
    for h in range(heads):
        v = raw[h * HD : (h + 1) * HD]
        g = grad[h * HD : (h + 1) * HD]
        ga, gb = g[:HALF], g[HALF:]
        g = jnp.concatenate([ga * cosine + gb * sine, gb * cosine - ga * sine], axis=0)
        r = lax.rsqrt(jnp.mean(v * v, axis=0, keepdims=True) + EPS)
        n = v * r
        gain_grad = gain_grad + jnp.sum(g * n, axis=1, keepdims=True)
        g = g * gain
        outs.append(r * (g - n * jnp.mean(g * n, axis=0, keepdims=True)))
    return jnp.concatenate(outs, axis=0), gain_grad


def qkv_kernel(dims, own, qc, kc, oc, idx, *refs):
    nx, nz, nc, n = dims
    pieces = refs[:n]
    w_parts = refs[n : n + 2 * nx]
    head_gains, cosine, sine = refs[n + 2 * nx : n + 2 * nx + 3]
    w, base, gains, q_t, raw_t, kv, rel, turned = refs[n + 2 * nx + 3 :]
    gq, gk = head_columns(head_gains)
    assemble(idx, n, pieces, base)
    for other in range(nc):
        core = idx[2] if other == 0 else 1 - idx[2]
        for xr in range(nx):
            src = w_parts[other * nx + xr]

            def step(zr, carry, src=src, xr=xr, core=core):
                row = (rot_index(idx[0], nx - xr, nx) * nz + rot_index(idx[1], nz - zr, nz)) * nc + core
                w[ds(row, own), :] = src[ds(zr, own), :]
                return carry

            for zr in range(nz):
                step(zr, 0)
    qkv = qc + 2 * kc
    gains[...] = w[:, qkv:].astype(f32).T[:8]
    b = base[...].astype(f32)
    normed = b * lax.rsqrt(jnp.mean(b * b, axis=1, keepdims=True) + EPS) * gains[0:1, :]
    normed = normed.astype(bf16)
    raw = dot(normed, w[:, :qkv])
    turned[...] = normed.T
    store_relative(dims, idx, rel, turned, own)
    kv[:, kc:] = raw[:, qc + kc :].astype(bf16)
    rt = raw[:, : qc + kc].T
    raw_t[...] = rt
    co, si = cosine[...], sine[...]
    q = (turn_heads(rt[:qc], gq, co, si, qc // HD) * SCALE).astype(bf16)
    to_groups(q_t, q)
    kv[:, :kc] = turn_heads(rt[qc:], gk, co, si, kc // HD).T.astype(bf16)


def attend_kernel(dims, qc, kc, oc, idx, q_t, *refs):
    nx, nz, nc, n = dims
    kv_parts = refs[: nz * nc]
    kv, attn_t, attn_b, log_total, acc, tot = refs[nz * nc :]
    span = attn_b.shape[0]
    group = qc // kc
    me = idx[1] * nc + idx[2]
    for other in range(nc):
        core = idx[2] if other == 0 else 1 - idx[2]
        for zr in range(nz):
            block = rot_index(idx[1], nz - zr, nz) * nc + core
            kv[ds(block, span), :] = kv_parts[other * nz + zr][...]
    acc[...] = jnp.zeros_like(acc)
    tot[...] = jnp.zeros_like(tot)
    keys_at = lax.broadcasted_iota(jnp.int32, (span, span), 0)
    query_at = lax.broadcasted_iota(jnp.int32, (span, span), 1)
    ahead = keys_at - query_at
    ahead = jnp.concatenate([ahead] * group, axis=1)

    def step(j, carry):
        vt = kv[ds(j, span), kc:].T
        allowed = ahead <= (me - j) * span
        for g in range(kc // HD):
            rows = slice(g * HD, (g + 1) * HD)
            s = dot(kv[ds(j, span), rows], q_t[rows, :])
            e = jnp.where(allowed, jnp.exp(s), 0.0)
            tot[g : g + 1, :] += jnp.sum(e, axis=0, keepdims=True)
            acc[rows, :] += dot(vt[rows], e.astype(bf16))
        return carry

    lax.fori_loop(0, me + 1, step, 0)
    for g in range(kc // HD):
        rows = slice(g * HD, (g + 1) * HD)
        attn_t[rows, :] = acc[rows, :] / tot[g : g + 1, :]
    log_total[...] = jnp.log(jnp.maximum(tot[...], 1e-30))
    attn = from_groups(attn_t[...], span).T.astype(bf16)
    attn_b[...] = attn


def out_kernel(dims, idx, attn_b, w_low, w_high, *pieces):
    n = dims[3]
    attn = attn_b[...]
    part = w_low.shape[0] // n
    for k in range(n):
        rows = ds(rot_index(idx[3], k, n), part)
        out = dot(attn[:, :PAD], w_low[rows, :], NT) + dot(attn[:, PAD:], w_high[rows, :], NT)
        pieces[k][...] = out.astype(bf16)


def hidden_grad_kernel(cot, wd, out):
    out[...] = dot(cot[...], wd[...])


def ffn_kernel(dims, own, idx, base, gains, *refs):
    n = dims[3]
    sums = refs[:n]
    wg, wu, hgrad = refs[n : n + 3]
    middle, normed, big = refs[n + 3 : n + 6]
    pieces = refs[n + 6 : n + 6 + n]
    acc = refs[n + 6 + n]
    j = pl.program_id(0)
    part = sums[0].shape[1]

    @pl.when(j == 0)
    def _():
        for k in range(n):
            at = ds(rot_index(idx[3], n - k, n), part)
            middle[:, at] = base[:, at].astype(f32) + sums[k][...].astype(f32)
        m = middle[...]
        v = m * lax.rsqrt(jnp.mean(m * m, axis=1, keepdims=True) + EPS) * gains[1:2, :]
        v = v.astype(bf16)
        normed[...] = v
        acc[...] = jnp.zeros_like(acc)

    v = normed[...]
    block = wg.shape[1]
    ff = big.shape[1] // 3
    gate = dot(v, wg[...])
    up = dot(v, wu[...])
    hg = hgrad[...]
    sig = 1.0 / (1.0 + jnp.exp(-gate))
    act = gate * sig
    hidden = (act * up).astype(bf16)
    gate_gb = (hg * up * (sig + act * (1.0 - sig))).astype(bf16)
    up_gb = (hg * act).astype(bf16)
    big[:, pl.ds(pl.multiple_of(j * block, block), block)] = gate_gb
    big[:, pl.ds(pl.multiple_of(ff + j * block, PAD), block)] = up_gb
    big[:, pl.ds(pl.multiple_of(2 * ff + j * block, PAD), block)] = hidden
    acc[...] += dot(gate_gb, wg[...], NT) + dot(up_gb, wu[...], NT)

    @pl.when(j == pl.num_programs(0) - 1)
    def _():
        for k in range(n):
            pieces[k][...] = acc[:, ds(rot_index(idx[3], k, n), part)].astype(bf16)


def down_kernel(dims, idx, hidden, wd, *refs):
    n = dims[3]
    part = wd.shape[0] // n
    for k in range(n):
        rows = ds(rot_index(idx[3], k, n), part)
        refs[k][...] = dot(hidden[...], wd[rows, :], NT).astype(bf16)


def rows_kernel(dims, own, idx, mine, partner, out, turned):
    nx, nz, nc, _ = dims
    span = mine.shape[0]
    for k, src in enumerate((mine, partner)):
        turned[...] = src[...].T

        def step(i, carry, k=k):
            out[ds(i, own), k * span : (k + 1) * span] = turned[ds(i * nc + idx[2], own), :]
            return carry

        for i in range(nx * nz):
            step(i, 0)


def ffn_grad_kernel(normed_rows, cot_rows, big, partner_big, out, left):
    j = pl.program_id(0)

    @pl.when(j == 0)
    def _():
        left[...] = normed_rows[...]

    @pl.when(j == 2)
    def _():
        left[...] = cot_rows[...]

    span = big.shape[0]
    out[...] = (dot(left[:, :span], big[...]) + dot(left[:, span:], partner_big[...])).astype(bf16)


def attend_back_kernel(dims, own, qc, kc, oc, idx, middle, gains, cot, *refs):
    nx, nz, nc, n = dims
    grads = refs[:n]
    w_low, w_high, attn_t, q_t, raw_t, kv, log_total, head_gains, cosine, sine = refs[n : n + 10]
    mine, mid, gain_two, q_gb, gq_grad, kv_keep, kv_send = refs[n + 10 : n + 17]
    full, dq, do_t, delta, mid_grad, do_f, q_n, do_n, out = refs[n + 17 :]
    span = mine.shape[0]
    group = qc // kc
    me = idx[1] * nc + idx[2]
    assemble(idx, n, grads, full)
    m = middle[...]
    r = lax.rsqrt(jnp.mean(m * m, axis=1, keepdims=True) + EPS)
    unit = m * r
    ng = full[...].astype(f32)
    gain_two[...] = jnp.broadcast_to(jnp.sum(ng * unit, axis=0, keepdims=True), gain_two.shape)
    gg = ng * gains[1:2, :]
    mg = cot[...].astype(f32) + r * (gg - unit * jnp.mean(gg * unit, axis=1, keepdims=True))
    mid_grad[...] = mg
    part = grads[0].shape[1]
    mine[...] = mid_grad[:, ds(idx[3], part)]
    mgb = mg.astype(bf16)
    mid[...] = mgb
    ag = jnp.concatenate([dot(mgb, w_low[...]), dot(mgb, w_high[...])], axis=1)
    to_groups(do_f, ag.T)
    prod = do_f[...] * attn_t[...]
    do_t[...] = do_f[...].astype(bf16)
    for g in range(kc // HD):
        rows = slice(g * HD, (g + 1) * HD)
        delta[g : g + 1, :] = jnp.sum(prod[rows], axis=0, keepdims=True)
        q_n[g * q_t.shape[1] : (g + 1) * q_t.shape[1], :] = q_t[rows, :].T
        do_n[g * q_t.shape[1] : (g + 1) * q_t.shape[1], :] = do_t[rows, :].T
    dq[...] = jnp.zeros_like(dq)
    keys_at = lax.broadcasted_iota(jnp.int32, (span, span), 0)
    query_at = lax.broadcasted_iota(jnp.int32, (span, span), 1)
    ahead = keys_at - query_at
    ahead = jnp.concatenate([ahead] * group, axis=1)
    def step(t, carry):
        other = t // nz
        j = rot_index(idx[1], t % nz, nz) * nc + lax.rem(idx[2] + other, nc)
        at = ds(t, span)

        @pl.when(j > me)
        def _():
            out[at, :] = jnp.zeros((span, 2 * kc), bf16)

        @pl.when(j <= me)
        def _():
            kt = kv[ds(j, span), :kc].T
            allowed = ahead <= (me - j) * span
            wide = q_t.shape[1]
            for g in range(kc // HD):
                rows = slice(g * HD, (g + 1) * HD)
                s = dot(kv[ds(j, span), rows], q_t[rows, :])
                p = jnp.where(allowed, jnp.exp(s - log_total[g : g + 1, :]), 0.0)
                dp = dot(kv[ds(j, span), kc + g * HD : kc + (g + 1) * HD], do_t[rows, :])
                sg = (p * (dp - delta[g : g + 1, :])).astype(bf16)
                dq[rows, :] += dot(kt[rows], sg)
                dk = dot(sg, q_n[g * wide : (g + 1) * wide, :])
                dv = dot(p.astype(bf16), do_n[g * wide : (g + 1) * wide, :])
                out[at, rows] = dk.astype(bf16)
                out[at, kc + g * HD : kc + (g + 1) * HD] = dv.astype(bf16)

        return carry

    lax.fori_loop(0, nz * nc, step, 0)
    kv_keep[...] = out[: nz * span, :]
    kv_send[...] = out[nz * span :, :]
    raw_grad, gain_grad = turn_heads_back(
        raw_t[:qc, :], from_groups(dq[...], span) * SCALE, head_columns(head_gains)[0], cosine[...], sine[...], qc // HD
    )
    gq_grad[...] = gain_grad
    q_gb[...] = raw_grad.T.astype(bf16)


def input_grad_kernel(dims, qc, kc, idx, *refs):
    n, nz = dims[3], dims[1]
    kv_parts = refs[:nz]
    raw_t, head_gains, cosine, sine, q_gb, w, base, gains = refs[nz : nz + 8]
    qkv_gb, gain_one, gk_grad = refs[nz + 8 : nz + 11]
    pieces = refs[nz + 11 : nz + 11 + n]
    acc = refs[nz + 11 + n]
    total = kv_parts[0][...].astype(f32)
    for k in range(1, nz):
        total = total + kv_parts[k][...].astype(f32)
    raw_grad, gain_grad = turn_heads_back(
        raw_t[qc:, :], total[:, :kc].T, head_columns(head_gains)[1], cosine[...], sine[...], kc // HD
    )
    gk_grad[...] = gain_grad
    qkv_gb[:, :qc] = q_gb[...]
    qkv_gb[:, qc : qc + kc] = raw_grad.T.astype(bf16)
    qkv_gb[:, qc + kc :] = total[:, kc:].astype(bf16)
    ng = dot(qkv_gb[...], w[:, : qc + 2 * kc], NT)
    acc[...] = ng
    b = base[...].astype(f32)
    unit = b * lax.rsqrt(jnp.mean(b * b, axis=1, keepdims=True) + EPS)
    prod = ng * unit
    gain_one[...] = jnp.broadcast_to(jnp.sum(prod, axis=0, keepdims=True), gain_one.shape)
    along = jnp.sum(prod * gains[0:1, :], axis=1, keepdims=True)
    along = jnp.broadcast_to(along, (along.shape[0], PAD)).T[:16]
    high = along.astype(bf16)
    low = (along - high.astype(f32)).astype(bf16)
    row = lax.broadcasted_iota(jnp.int32, along.shape, 0)
    tail = jnp.where(row == 0, high.astype(f32), low.astype(f32)).astype(bf16)
    part = acc.shape[1] // n
    for k in range(n):
        pieces[k][: along.shape[1], :] = acc[:, ds(rot_index(idx[3], k, n), part)].astype(bf16)
        pieces[k][along.shape[1] :, :] = tail


def attn_grad_kernel(dims, own, qc, kc, oc, idx, one_rel, out_rel, qkv_gb, gain_one, gain_two, gq_grad, gk_grad, keep, send, extra, extra_rel, lined, spread):
    half = keep.shape[0]
    qkv = qc + 2 * kc
    width = one_rel.shape[0]

    def halves(v):
        high = v.astype(bf16).astype(f32)
        return high, v - high

    rows = lax.broadcasted_iota(jnp.int32, (PAD, width), 0)
    lines = jnp.zeros((PAD, width), f32)
    values = halves(gain_one[0:1, :]) + halves(gain_two[0:1, :])
    for i, v in enumerate(values):
        lines = lines + jnp.where(rows == i, v, 0.0)
    cols = lines.T
    heads = jnp.concatenate([gq_grad[...], gk_grad[...]], axis=0)
    high, low = halves(heads)
    lane = lax.broadcasted_iota(jnp.int32, (own, PAD), 1)
    tile = jnp.zeros((own, PAD), f32)
    count = 2 * HD // own
    for i in range(count):
        at = slice(i * own, (i + 1) * own)
        tile = tile + jnp.where(lane == 4 + i, high[at], 0.0)
        tile = tile + jnp.where(lane == 4 + count + i, low[at], 0.0)
    lined[...] = cols
    spread[...] = tile

    def step(i, carry):
        extra[ds(i, own), :] = (lined[ds(i, own), :] + spread[...]).astype(bf16)
        return carry

    for i in range(width // own):
        step(i, 0)
    store_relative(dims, idx, extra_rel, extra, own)
    a = dot(one_rel[...], qkv_gb[...]).astype(bf16)
    for out, at in ((keep, slice(0, half)), (send, slice(half, 2 * half))):
        out[:, :qkv] = a[at]
        out[:, qkv : qkv + oc] = out_rel[at, :]
        out[:, qkv + oc :] = extra_rel[at, :]


def sum_kernel(cuts, *refs):
    outs = refs[len(refs) - len(cuts) + 1 :]
    ins = refs[: len(refs) - len(cuts) + 1]
    for out, first, last in zip(outs, cuts[:-1], cuts[1:]):
        total = ins[0][:, first:last].astype(f32)
        for v in ins[1:]:
            total = total + v[:, first:last].astype(f32)
        out[...] = total


def pack_kernel(q, k, v, o, g, u, d, gain_one, gain_two, x, c, attn, ffn, both, square):
    at = 0
    for w in (q, k, v):
        attn[:, at : at + w.shape[1]] = w[...]
        at += w.shape[1]
    own = q.shape[0]
    square[...] = jnp.zeros_like(square)
    square[0:1, :own] = gain_one[...].astype(f32)
    square[1:2, :own] = gain_two[...].astype(f32)
    attn[:, at:] = square[...].T[:own].astype(bf16)
    at = 0
    for w in (g, u, d, o):
        ffn[:, at : at + w.shape[1]] = w[...]
        at += w.shape[1]
    part = x.shape[1]
    both[:, :part] = x[...]
    both[:, part:] = c[...]


def out_grad_kernel(dims, own, idx, mid, attn_b, out, turned, rel):
    turned[...] = mid[...].T
    store_relative(dims, idx, rel, turned, own)
    out[...] = dot(rel[...], attn_b[...]).astype(bf16)


def core_sum(keep, send, n):
    got = shift(send, "core", 1)
    step = keep.shape[0] // n
    return [
        (keep[k * step : (k + 1) * step].astype(f32) + got[k * step : (k + 1) * step].astype(f32)).astype(bf16)
        for k in range(n)
    ]


def row_sum(x, axis):
    step = x.shape[0] // lax.axis_size(axis)
    return summed([x[k * step : (k + 1) * step] for k in range(lax.axis_size(axis))], axis)


def after(values, others):
    return lax.optimization_barrier((list(values), others))[0]


def body(
    block_input,
    attn_gain,
    ffn_gain,
    query_gain,
    key_gain,
    query_weight,
    key_weight,
    value_weight,
    out_weight,
    gate_weight,
    up_weight,
    down_weight,
    cotangent,
):
    span, seq_local, part = block_input.shape
    axes = ("dp", "z", "core", "tensor")
    dims = tuple(lax.axis_size(a) for a in axes)
    nx, nz, nc, n = dims
    idx = jnp.stack([lax.axis_index(a) for a in axes]).astype(jnp.int32)
    width = part * n
    own = query_weight.shape[0]
    qc, kc, oc, ff = (w.shape[1] for w in (query_weight, key_weight, out_weight, gate_weight))
    qkv = qc + 2 * kc
    aw = qkv + oc + PAD

    attn_local, ffn_local, both = call(
        pack_kernel,
        [sds((own, qkv + PAD), bf16), sds((own, 3 * ff + oc), bf16), sds((span, 2 * part), bf16)],
        [query_weight, key_weight, value_weight, out_weight, gate_weight, up_weight, down_weight]
        + [attn_gain[None, :], ffn_gain[None, :], block_input.reshape(span, part), cotangent.reshape(span, part)],
        [pltpu.VMEM((PAD, PAD), f32)],
    )
    ffn_w = lax.all_gather(ffn_local, ("dp", "z", "core"), axis=0, tiled=True)
    by_z = jnp.concatenate(gathered(attn_local, "z"), axis=0)
    both_parts = gathered(both, "tensor")
    my_first = (idx[1] * nc + idx[2]) * span
    positions = (my_first + jnp.arange(span, dtype=jnp.int32)).astype(f32)
    frequency = jnp.power(ROPE_BASE, -2.0 * jnp.arange(HALF, dtype=f32) / HD)
    angle = frequency[:, None] * positions[None, :]
    cosine, sine = jnp.cos(angle), jnp.sin(angle)
    head_gains = jnp.concatenate([query_gain, key_gain])[None, :]
    dp_parts = gathered(by_z, "dp")
    dp_parts, both_parts, cosine, sine, head_gains = lax.optimization_barrier(
        (dp_parts, both_parts, cosine, sine, head_gains)
    )
    dp_partner = [shift(v, "core", 1) for v in dp_parts]
    cot = call(
        functools.partial(cot_kernel, dims, own),
        [sds((span, width), bf16)],
        [idx] + both_parts,
    )[0]

    def core_rows(x):
        return call(
            functools.partial(rows_kernel, dims, own),
            [sds((width // nc, nc * span), bf16)],
            [idx, x, shift(x, "core", 1)],
            [pltpu.VMEM((width, span), bf16)],
        )[0]

    cot_rows = core_rows(cot)

    w, base, gains, q_t, raw_t, kv, one_rel = call(
        functools.partial(qkv_kernel, dims, own, qc, kc, oc),
        [
            sds((width, qkv + PAD), bf16),
            sds((span, width), bf16),
            sds((8, width), f32),
            sds((kc, qc // kc * span), bf16),
            sds((qc + kc, span), f32),
            sds((span, 2 * kc), bf16),
            sds((width, span), bf16),
        ],
        [idx] + both_parts + dp_parts + dp_partner + [head_gains, cosine, sine],
        [pltpu.VMEM((width, span), bf16)],
        flops=2 * span * width * qkv,
    )
    kv_own = gathered(kv, "z")
    kv_partner = [shift(v, "core", 1) for v in kv_own]

    length = span * nz * nc
    block = 384
    const = lambda s: pl.BlockSpec(s, lambda j: (0, 0))
    steps = ff // block
    out_blocks = [pl.BlockSpec((width, PAD), lambda j, o=o: (0, o)) for o in (3 * ff // PAD, 3 * ff // PAD + 1)]
    kv_full, attn_t, attn_b, log_total = call(
        functools.partial(attend_kernel, dims, qc, kc, oc),
        [sds((length, 2 * kc), bf16), sds(q_t.shape, f32), sds((span, qc), bf16), sds((8, q_t.shape[1]), f32)],
        [idx, q_t] + kv_own + kv_partner,
        [pltpu.VMEM(q_t.shape, f32), pltpu.VMEM((8, q_t.shape[1]), f32)],
        flops=4 * span * length * qc,
    )
    res = call(
        functools.partial(out_kernel, dims),
        [sds((span, part), bf16)] * n,
        [idx, attn_b, ffn_w, ffn_w],
        grid=(1,),
        in_specs=[pl.BlockSpec(memory_space=pltpu.SMEM), const((span, qc))] + out_blocks,
        out_specs=[const((span, part))] * n,
        flops=2 * span * width * qc,
    )
    attn_mine = summed(res, "tensor").astype(bf16)
    attn_parts = gathered(attn_mine, "tensor")
    attn_parts, cot_rows = lax.optimization_barrier((attn_parts, cot_rows))

    hgrad = call(
        hidden_grad_kernel,
        [sds((span, ff), f32)],
        [cot, ffn_w],
        grid=(steps,),
        in_specs=[const((span, width)), pl.BlockSpec((width, block), lambda j: (0, 2 * steps + j))],
        out_specs=[pl.BlockSpec((span, block), lambda j: (0, j))],
        flops=2 * span * width * ff,
    )[0]
    res = call(
        functools.partial(ffn_kernel, dims, own),
        [sds((span, width), f32), sds((span, width), bf16), sds((span, 3 * ff), bf16)]
        + [sds((span, part), bf16)] * n,
        [idx, base, gains] + attn_parts + [ffn_w, ffn_w, hgrad],
        [pltpu.VMEM((span, width), f32)],
        grid=(steps,),
        in_specs=[pl.BlockSpec(memory_space=pltpu.SMEM)]
        + [const((span, width)), const((8, width))]
        + [const((span, part))] * n
        + [pl.BlockSpec((width, block), lambda j, o=o: (0, o + j)) for o in (0, steps)]
        + [pl.BlockSpec((span, block), lambda j: (0, j))],
        out_specs=[const((span, width)), const((span, width)), const((span, 3 * ff))]
        + [const((span, part))] * n,
        flops=8 * span * width * ff,
    )
    middle, normed_two, big = res[:3]
    grad_got = [shift(res[3 + k], "tensor", k) for k in range(1, n)]
    part_zero = res[3]

    normed_rows = core_rows(normed_two)
    grad_got, normed_rows = lax.optimization_barrier((grad_got, normed_rows))
    ffn_half = call(
        ffn_grad_kernel,
        [sds((width // nc, 3 * ff), bf16)],
        [normed_rows, cot_rows, big, shift(big, "core", 1)],
        [pltpu.VMEM((width // nc, nc * span), bf16)],
        grid=(3,),
        in_specs=[const((width // nc, nc * span))] * 2 + [pl.BlockSpec((span, ff), lambda j: (0, j))] * 2,
        out_specs=[pl.BlockSpec((width // nc, ff), lambda j: (0, j))],
        flops=6 * span * width * ff,
    )[0]
    grad_mine = sum([g.astype(f32) for g in grad_got], part_zero.astype(f32)).astype(bf16)
    grad_parts = gathered(grad_mine, "tensor")
    down_parts = call(
        functools.partial(down_kernel, dims),
        [sds((span, part), bf16)] * n,
        [idx, big, ffn_w],
        grid=(1,),
        in_specs=[
            pl.BlockSpec(memory_space=pltpu.SMEM),
            pl.BlockSpec((span, ff), lambda j: (0, 2)),
            pl.BlockSpec((width, ff), lambda j: (0, 2)),
        ],
        out_specs=[const((span, part))] * n,
        flops=2 * span * width * ff,
    )
    grad_parts, ffn_half = lax.optimization_barrier((grad_parts, ffn_half))
    ffn_sum = lax.psum_scatter(ffn_half, ("dp", "z"), scatter_dimension=0, tiled=True)

    mine, mid, gain_two, q_gb, gq_grad, kv_keep, kv_send = call(
        functools.partial(attend_back_kernel, dims, own, qc, kc, oc),
        [
            sds((span, part), f32),
            sds((span, width), bf16),
            sds((8, width), f32),
            sds((span, qc), bf16),
            sds((HD, 1), f32),
            sds((length // 2, 2 * kc), bf16),
            sds((length // 2, 2 * kc), bf16),
        ],
        [idx, middle, gains, cot] + grad_parts + [ffn_w, ffn_w, attn_t, q_t, raw_t, kv_full, log_total, head_gains, cosine, sine],
        [
            pltpu.VMEM((span, width), bf16),
            pltpu.VMEM(q_t.shape, f32),
            pltpu.VMEM(q_t.shape, bf16),
            pltpu.VMEM((8, q_t.shape[1]), f32),
            pltpu.VMEM((span, width), f32),
            pltpu.VMEM(q_t.shape, f32),
            pltpu.VMEM((kc // HD * q_t.shape[1], HD), bf16),
            pltpu.VMEM((kc // HD * q_t.shape[1], HD), bf16),
            pltpu.VMEM((length, 2 * kc), bf16),
        ],
        grid=(1,),
        in_specs=[pl.BlockSpec(memory_space=pltpu.SMEM), const((span, width)), const((8, width)), const((span, width))]
        + [const((span, part))] * n
        + out_blocks
        + [const(v.shape) for v in (attn_t, q_t, raw_t, kv_full, log_total, head_gains, cosine, sine)],
        out_specs=[
            const((span, part)),
            const((span, width)),
            const((8, width)),
            const((span, qc)),
            const((HD, 1)),
            const((length // 2, 2 * kc)),
            const((length // 2, 2 * kc)),
        ],
        flops=10 * span * length * qc,
    )
    kv_pieces = core_sum(kv_keep, kv_send, nz)
    kv_parts = [kv_pieces[0]] + [shift(kv_pieces[k], "z", k) for k in range(1, nz)]
    kv_parts[1], down_parts = lax.optimization_barrier((kv_parts[1], down_parts))
    out_rel = call(
        functools.partial(out_grad_kernel, dims, own),
        [sds((width, oc), bf16)],
        [idx, mid, attn_b],
        [pltpu.VMEM((width, span), bf16)] * 2,
        flops=2 * span * width * oc,
    )[0]
    kv_parts[2], out_rel = lax.optimization_barrier((kv_parts[2], out_rel))
    me_t = idx[3]
    middle_mine = lax.dynamic_slice_in_dim(middle, me_t * part, part, 1)
    down_got = [down_parts[0]] + [shift(down_parts[k], "tensor", k) for k in range(1, n)]

    res = call(
        functools.partial(input_grad_kernel, dims, qc, kc),
        [sds((span, qkv), bf16), sds((8, width), f32), sds((HD, 1), f32)]
        + [sds((span + 16, part), bf16)] * n,
        [idx] + kv_parts + [raw_t, head_gains, cosine, sine, q_gb, w, base, gains],
        [pltpu.VMEM((span, width), f32)],
        flops=2 * span * width * qkv,
    )
    qkv_gb, gain_one, gk_grad = res[:3]
    norm_parts = res[3:]
    keep, send = call(
        functools.partial(attn_grad_kernel, dims, own, qc, kc, oc),
        [sds((width // 2, aw), bf16)] * 2,
        [idx, one_rel, out_rel, qkv_gb, gain_one, gain_two, gq_grad, gk_grad],
        [pltpu.VMEM((width, PAD), bf16)] * 2 + [pltpu.VMEM((width, PAD), f32), pltpu.VMEM((own, PAD), f32)],
        flops=2 * span * width * (qkv + oc),
    )
    (keep, send), down_got = lax.optimization_barrier(((keep, send), down_got))
    attn_pieces = core_sum(keep, send, nx)
    attn_got = [shift(attn_pieces[k], "dp", k) for k in range(1, nx)]
    attn_got[0], norm_parts = lax.optimization_barrier((attn_got[0], norm_parts))
    attn_x = sum([v.astype(f32) for v in attn_got], attn_pieces[0].astype(f32)).astype(bf16)
    norm_got = [norm_parts[0]] + [shift(norm_parts[k], "tensor", k) for k in range(1, n)]
    attn_x, norm_got = lax.optimization_barrier((attn_x, norm_got))
    z_parts = [attn_x[:own]] + [shift(attn_x[k * own : (k + 1) * own], "z", k) for k in range(1, nz)]
    wgrads = call(
        functools.partial(sum_kernel, (0, qc, qc + kc, qkv, qkv + oc, aw)),
        [sds((own, v), f32) for v in (qc, kc, kc, oc, PAD)],
        z_parts,
    )
    small = wgrads[4]
    block_output = (middle_mine + sum([v.astype(f32) for v in down_got[1:]], down_got[0].astype(f32))).astype(bf16)
    norm_mine = sum([v.astype(f32) for v in norm_got[1:]], norm_got[0].astype(f32))
    along = (norm_mine[span] + norm_mine[span + 1])[:, None] * (1.0 / width)
    base_f = base.astype(f32)
    scale_one = lax.rsqrt(jnp.mean(base_f * base_f, axis=1, keepdims=True) + EPS)
    unit_mine = block_input.reshape(span, part).astype(f32) * scale_one
    gain_mine = lax.dynamic_slice_in_dim(gains, me_t * part, part, 1)[0:1]
    input_grad = (mine + scale_one * (norm_mine[:span] * gain_mine - unit_mine * along)).astype(bf16)

    fgrads = call(
        functools.partial(sum_kernel, (0, ff, 2 * ff, 3 * ff)),
        [sds((own, ff), f32)] * 3,
        [ffn_sum],
    )
    small_all = sum(gathered(small, "tensor"))
    count = 2 * HD // own
    head_sum = (small_all[:, 4 : 4 + count] + small_all[:, 4 + count : 4 + 2 * count]).T.reshape(-1)
    return (
        block_output.reshape(span, seq_local, part),
        input_grad.reshape(span, seq_local, part),
        small_all[:, 0] + small_all[:, 1],
        small[:, 2] + small[:, 3],
        head_sum[:HD],
        head_sum[HD:],
        *wgrads[:4],
        *fgrads,
    )


def solution(mesh):
    dp, seq, tensor = (mesh.shape[a] for a in ("dp", "seq", "tensor"))
    grid = Mesh(
        np.asarray(mesh.devices).reshape(dp, seq // 2, 2, tensor), ("dp", "z", "core", "tensor")
    )
    tokens = P(("z", "core"), "dp", "tensor")
    rows = P(("dp", "z", "core"))
    weight = P(("dp", "z", "core"), "tensor")
    return jax.shard_map(
        body,
        mesh=grid,
        in_specs=(tokens, rows, rows, P(), P()) + (weight,) * 7 + (tokens,),
        out_specs=(tokens, tokens, rows, rows, P(), P()) + (weight,) * 7,
        check_vma=False,
    )
```

```python
import functools

import numpy as np
import jax
import jax.numpy as jnp
from jax import lax
from jax.experimental import pallas as pl
from jax.experimental.pallas import tpu as pltpu
from jax.sharding import Mesh, PartitionSpec as P

HD = 64
HALF = HD // 2
EPS = 1e-05
ROPE_BASE = 1000000.0
SCALE = HD ** (-0.5)
PAD = 128
bf16 = jnp.bfloat16
f32 = jnp.float32
NN = (((1,), (0,)), ((), ()))
NT = (((1,), (1,)), ((), ()))


def dot(a, b, dims=NN):
    return lax.dot_general(a, b, dims, preferred_element_type=f32)


def rot_index(a, k, n):
    return lax.rem(a + k, n)


def ds(start, size):
    return pl.ds(pl.multiple_of(start * size, size), size)


def shift(x, axis, k):
    n = lax.axis_size(axis)
    return lax.ppermute(x, axis, [(i, (i + k) % n) for i in range(n)])


def gathered(x, axis):
    return [x] + [shift(x, axis, k) for k in range(1, lax.axis_size(axis))]


def summed(pieces, axis):
    total = pieces[0].astype(f32)
    for k in range(1, lax.axis_size(axis)):
        total = total + shift(pieces[k], axis, k).astype(f32)
    return total


def call(kernel, outs, ins, scratch=(), grid=None, in_specs=None, out_specs=None, flops=0):
    vm = pl.BlockSpec(memory_space=pltpu.VMEM)
    nbytes = sum(x.size * x.dtype.itemsize for x in list(ins) + list(outs))
    kwargs = {} if grid is None else {"grid": grid}
    return pl.pallas_call(
        kernel,
        out_shape=outs,
        in_specs=in_specs or [pl.BlockSpec(memory_space=pltpu.SMEM) if x.dtype == jnp.int32 else vm for x in ins],
        out_specs=out_specs or [vm] * len(outs),
        scratch_shapes=list(scratch),
        cost_estimate=pl.CostEstimate(flops=flops, bytes_accessed=nbytes, transcendentals=0),
        **kwargs,
    )(*ins)


def sds(shape, dtype):
    return jax.ShapeDtypeStruct(shape, dtype)


def store_relative(dims, idx, dst, src, own):
    nx, nz, nc, _ = dims
    x, z, c = idx[0], idx[1], idx[2]
    at = 0
    for other in range(nc):
        core = c if other == 0 else 1 - c
        for zr in range(nz):
            for xr in range(nx):
                row = (rot_index(x, xr, nx) * nz + rot_index(z, zr, nz)) * nc + core
                dst[at * own : (at + 1) * own, :] = src[ds(row, own), :]
                at += 1


def assemble(idx, n, pieces, dst, first=0):
    part = dst.shape[1] // n
    for k in range(n):
        dst[:, ds(rot_index(idx[3], n - k, n), part)] = pieces[k][:, first : first + part]


def cot_kernel(dims, idx, *refs):
    n = dims[3]
    pieces, (full, turned) = refs[:n], refs[n:]
    assemble(idx, n, pieces, full, full.shape[1] // n)
    turned[...] = full[...].T


def head_columns(ref):
    turned = jnp.broadcast_to(ref[...].astype(f32), (8, 2 * HD)).T
    return turned[:HD, :1], turned[HD:, :1]


def to_groups(dst, rows):
    span = rows.shape[1]
    group = dst.shape[1] // span
    for h in range(rows.shape[0] // HD):
        g, at = h // group, h % group
        dst[g * HD : (g + 1) * HD, at * span : (at + 1) * span] = rows[h * HD : (h + 1) * HD]


def from_groups(x, span):
    group = x.shape[1] // span
    return jnp.concatenate(
        [
            x[h // group * HD : (h // group + 1) * HD, h % group * span : (h % group + 1) * span]
            for h in range(x.shape[0] // HD * group)
        ],
        axis=0,
    )


def turn_heads(raw, gain, cosine, sine, heads):
    outs = []
    for h in range(heads):
        v = raw[h * HD : (h + 1) * HD]
        v = v * lax.rsqrt(jnp.mean(v * v, axis=0, keepdims=True) + EPS) * gain
        a, b = v[:HALF], v[HALF:]
        outs += [a * cosine - b * sine, b * cosine + a * sine]
    return jnp.concatenate(outs, axis=0)


def turn_heads_back(raw, grad, gain, cosine, sine, heads):
    outs, gain_grad = [], jnp.zeros((HD, 1), f32)
    for h in range(heads):
        v = raw[h * HD : (h + 1) * HD]
        g = grad[h * HD : (h + 1) * HD]
        ga, gb = g[:HALF], g[HALF:]
        g = jnp.concatenate([ga * cosine + gb * sine, gb * cosine - ga * sine], axis=0)
        r = lax.rsqrt(jnp.mean(v * v, axis=0, keepdims=True) + EPS)
        n = v * r
        gain_grad = gain_grad + jnp.sum(g * n, axis=1, keepdims=True)
        g = g * gain
        outs.append(r * (g - n * jnp.mean(g * n, axis=0, keepdims=True)))
    return jnp.concatenate(outs, axis=0), gain_grad


def qkv_kernel(dims, own, qc, kc, oc, idx, *refs):
    nx, nz, nc, n = dims
    pieces = refs[:n]
    w_parts = refs[n : n + 2 * nx]
    head_gains, cosine, sine = refs[n + 2 * nx : n + 2 * nx + 3]
    w, base, gains, q_t, raw_t, kv, rel, turned = refs[n + 2 * nx + 3 :]
    gq, gk = head_columns(head_gains)
    assemble(idx, n, pieces, base)
    for other in range(nc):
        core = idx[2] if other == 0 else 1 - idx[2]
        for zr in range(nz):
            for xr in range(nx):
                row = (rot_index(idx[0], nx - xr, nx) * nz + rot_index(idx[1], nz - zr, nz)) * nc + core
                w[ds(row, own), :] = w_parts[other * nx + xr][zr * own : (zr + 1) * own, :]
    qkv = qc + 2 * kc
    gains[...] = w[:, qkv:].astype(f32).T[:8]
    b = base[...].astype(f32)
    normed = b * lax.rsqrt(jnp.mean(b * b, axis=1, keepdims=True) + EPS) * gains[0:1, :]
    normed = normed.astype(bf16)
    raw = dot(normed, w[:, :qkv])
    turned[...] = normed.T
    store_relative(dims, idx, rel, turned, own)
    kv[:, kc:] = raw[:, qc + kc :].astype(bf16)
    rt = raw[:, : qc + kc].T
    raw_t[...] = rt
    co, si = cosine[...], sine[...]
    q = (turn_heads(rt[:qc], gq, co, si, qc // HD) * SCALE).astype(bf16)
    to_groups(q_t, q)
    kv[:, :kc] = turn_heads(rt[qc:], gk, co, si, kc // HD).T.astype(bf16)


def attend_kernel(dims, qc, kc, oc, idx, q_t, *refs):
    nx, nz, nc, n = dims
    kv_parts = refs[: nz * nc]
    kv, attn_t, attn_b, log_total, acc, tot = refs[nz * nc :]
    span = attn_b.shape[0]
    group = qc // kc
    me = idx[1] * nc + idx[2]
    for other in range(nc):
        core = idx[2] if other == 0 else 1 - idx[2]
        for zr in range(nz):
            block = rot_index(idx[1], nz - zr, nz) * nc + core
            kv[ds(block, span), :] = kv_parts[other * nz + zr][...]
    acc[...] = jnp.zeros_like(acc)
    tot[...] = jnp.zeros_like(tot)
    keys_at = lax.broadcasted_iota(jnp.int32, (span, span), 0)
    query_at = lax.broadcasted_iota(jnp.int32, (span, span), 1)
    ahead = keys_at - query_at
    ahead = jnp.concatenate([ahead] * group, axis=1)

    def step(j, carry):
        vt = kv[ds(j, span), kc:].T
        allowed = ahead <= (me - j) * span
        for g in range(kc // HD):
            rows = slice(g * HD, (g + 1) * HD)
            s = dot(kv[ds(j, span), rows], q_t[rows, :])
            e = jnp.where(allowed, jnp.exp(s), 0.0)
            tot[g : g + 1, :] += jnp.sum(e, axis=0, keepdims=True)
            acc[rows, :] += dot(vt[rows], e.astype(bf16))
        return carry

    lax.fori_loop(0, me + 1, step, 0)
    for g in range(kc // HD):
        rows = slice(g * HD, (g + 1) * HD)
        attn_t[rows, :] = acc[rows, :] / tot[g : g + 1, :]
    log_total[...] = jnp.log(jnp.maximum(tot[...], 1e-30))
    attn = from_groups(attn_t[...], span).T.astype(bf16)
    attn_b[...] = attn


def out_kernel(dims, idx, attn_b, w_low, w_high, *pieces):
    n = dims[3]
    attn = attn_b[...]
    part = w_low.shape[0] // n
    for k in range(n):
        rows = ds(rot_index(idx[3], k, n), part)
        out = dot(attn[:, :PAD], w_low[rows, :], NT) + dot(attn[:, PAD:], w_high[rows, :], NT)
        pieces[k][...] = out.astype(bf16)


def hidden_grad_kernel(cot, wd, out):
    out[...] = dot(cot[...], wd[...])


def ffn_kernel(dims, own, idx, base, gains, *refs):
    n = dims[3]
    sums = refs[:n]
    wg, wu, hgrad = refs[n : n + 3]
    middle, normed, big = refs[n + 3 : n + 6]
    pieces = refs[n + 6 : n + 6 + n]
    acc = refs[n + 6 + n]
    j = pl.program_id(0)
    part = sums[0].shape[1]

    @pl.when(j == 0)
    def _():
        for k in range(n):
            at = ds(rot_index(idx[3], n - k, n), part)
            middle[:, at] = base[:, at].astype(f32) + sums[k][...].astype(f32)
        m = middle[...]
        v = m * lax.rsqrt(jnp.mean(m * m, axis=1, keepdims=True) + EPS) * gains[1:2, :]
        v = v.astype(bf16)
        normed[...] = v
        acc[...] = jnp.zeros_like(acc)

    v = normed[...]
    block = wg.shape[1]
    ff = big.shape[1] // 3
    gate = dot(v, wg[...])
    up = dot(v, wu[...])
    hg = hgrad[...]
    sig = 1.0 / (1.0 + jnp.exp(-gate))
    act = gate * sig
    hidden = (act * up).astype(bf16)
    gate_gb = (hg * up * (sig + act * (1.0 - sig))).astype(bf16)
    up_gb = (hg * act).astype(bf16)
    big[:, pl.ds(pl.multiple_of(j * block, block), block)] = gate_gb
    big[:, pl.ds(pl.multiple_of(ff + j * block, PAD), block)] = up_gb
    big[:, pl.ds(pl.multiple_of(2 * ff + j * block, PAD), block)] = hidden
    acc[...] += dot(gate_gb, wg[...], NT) + dot(up_gb, wu[...], NT)

    @pl.when(j == pl.num_programs(0) - 1)
    def _():
        for k in range(n):
            pieces[k][...] = acc[:, ds(rot_index(idx[3], k, n), part)].astype(bf16)


def down_kernel(dims, idx, hidden, wd, *refs):
    n = dims[3]
    part = wd.shape[0] // n
    for k in range(n):
        rows = ds(rot_index(idx[3], k, n), part)
        refs[k][...] = dot(hidden[...], wd[rows, :], NT).astype(bf16)


def ffn_grad_kernel(normed, cot_t, big, out, turned):
    j = pl.program_id(0)

    @pl.when(j == 0)
    def _():
        turned[...] = normed[...].T

    @pl.when(j < 2)
    def _():
        out[...] = dot(turned[...], big[...]).astype(bf16)

    @pl.when(j == 2)
    def _():
        out[...] = dot(cot_t[...], big[...]).astype(bf16)


def attend_back_kernel(dims, own, qc, kc, oc, idx, middle, gains, cot, *refs):
    nx, nz, nc, n = dims
    grads = refs[:n]
    w_low, w_high, attn_t, q_t, raw_t, kv, log_total, head_gains, cosine, sine = refs[n : n + 10]
    mine, mid, gain_two, q_gb, gq_grad, kv_keep, kv_send = refs[n + 10 : n + 17]
    full, dq, do_t, delta, mid_grad, do_f, q_n, do_n = refs[n + 17 :]
    span = mine.shape[0]
    group = qc // kc
    me = idx[1] * nc + idx[2]
    assemble(idx, n, grads, full)
    m = middle[...]
    r = lax.rsqrt(jnp.mean(m * m, axis=1, keepdims=True) + EPS)
    unit = m * r
    ng = full[...].astype(f32)
    gain_two[...] = jnp.broadcast_to(jnp.sum(ng * unit, axis=0, keepdims=True), gain_two.shape)
    gg = ng * gains[1:2, :]
    mg = cot[...].astype(f32) + r * (gg - unit * jnp.mean(gg * unit, axis=1, keepdims=True))
    mid_grad[...] = mg
    part = grads[0].shape[1]
    mine[...] = mid_grad[:, ds(idx[3], part)]
    mgb = mg.astype(bf16)
    mid[...] = mgb
    ag = jnp.concatenate([dot(mgb, w_low[...]), dot(mgb, w_high[...])], axis=1)
    to_groups(do_f, ag.T)
    prod = do_f[...] * attn_t[...]
    do_t[...] = do_f[...].astype(bf16)
    for g in range(kc // HD):
        rows = slice(g * HD, (g + 1) * HD)
        delta[g : g + 1, :] = jnp.sum(prod[rows], axis=0, keepdims=True)
        q_n[g * q_t.shape[1] : (g + 1) * q_t.shape[1], :] = q_t[rows, :].T
        do_n[g * q_t.shape[1] : (g + 1) * q_t.shape[1], :] = do_t[rows, :].T
    dq[...] = jnp.zeros_like(dq)
    keys_at = lax.broadcasted_iota(jnp.int32, (span, span), 0)
    query_at = lax.broadcasted_iota(jnp.int32, (span, span), 1)
    ahead = keys_at - query_at
    ahead = jnp.concatenate([ahead] * group, axis=1)
    for other, out in enumerate((kv_keep, kv_send)):
        core = idx[2] if other == 0 else 1 - idx[2]

        def step(zr, carry, out=out, core=core):
            j = rot_index(idx[1], zr, nz) * nc + core
            at = ds(zr, span)

            @pl.when(j > me)
            def _():
                out[at, :] = jnp.zeros((span, 2 * kc), bf16)

            @pl.when(j <= me)
            def _():
                kt = kv[ds(j, span), :kc].T
                allowed = ahead <= (me - j) * span
                wide = q_t.shape[1]
                for g in range(kc // HD):
                    rows = slice(g * HD, (g + 1) * HD)
                    s = dot(kv[ds(j, span), rows], q_t[rows, :])
                    p = jnp.where(allowed, jnp.exp(s - log_total[g : g + 1, :]), 0.0)
                    dp = dot(kv[ds(j, span), kc + g * HD : kc + (g + 1) * HD], do_t[rows, :])
                    sg = (p * (dp - delta[g : g + 1, :])).astype(bf16)
                    dq[rows, :] += dot(kt[rows], sg)
                    dk = dot(sg, q_n[g * wide : (g + 1) * wide, :])
                    dv = dot(p.astype(bf16), do_n[g * wide : (g + 1) * wide, :])
                    out[at, rows] = dk.astype(bf16)
                    out[at, kc + g * HD : kc + (g + 1) * HD] = dv.astype(bf16)

            return carry

        lax.fori_loop(0, nz, step, 0)
    raw_grad, gain_grad = turn_heads_back(
        raw_t[:qc, :], from_groups(dq[...], span) * SCALE, head_columns(head_gains)[0], cosine[...], sine[...], qc // HD
    )
    gq_grad[...] = gain_grad
    q_gb[...] = raw_grad.T.astype(bf16)


def input_grad_kernel(dims, qc, kc, idx, *refs):
    n, nz = dims[3], dims[1]
    kv_parts = refs[:nz]
    raw_t, head_gains, cosine, sine, q_gb, w, base, gains = refs[nz : nz + 8]
    qkv_gb, gain_one, gk_grad = refs[nz + 8 : nz + 11]
    pieces = refs[nz + 11 : nz + 11 + n]
    acc = refs[nz + 11 + n]
    total = kv_parts[0][...].astype(f32)
    for k in range(1, nz):
        total = total + kv_parts[k][...].astype(f32)
    raw_grad, gain_grad = turn_heads_back(
        raw_t[qc:, :], total[:, :kc].T, head_columns(head_gains)[1], cosine[...], sine[...], kc // HD
    )
    gk_grad[...] = gain_grad
    qkv_gb[:, :qc] = q_gb[...]
    qkv_gb[:, qc : qc + kc] = raw_grad.T.astype(bf16)
    qkv_gb[:, qc + kc :] = total[:, kc:].astype(bf16)
    ng = dot(qkv_gb[...], w[:, : qc + 2 * kc], NT)
    acc[...] = ng
    b = base[...].astype(f32)
    unit = b * lax.rsqrt(jnp.mean(b * b, axis=1, keepdims=True) + EPS)
    prod = ng * unit
    gain_one[...] = jnp.broadcast_to(jnp.sum(prod, axis=0, keepdims=True), gain_one.shape)
    along = jnp.sum(prod * gains[0:1, :], axis=1, keepdims=True)
    along = jnp.broadcast_to(along, (along.shape[0], PAD)).T[:16]
    high = along.astype(bf16)
    low = (along - high.astype(f32)).astype(bf16)
    row = lax.broadcasted_iota(jnp.int32, along.shape, 0)
    tail = jnp.where(row == 0, high.astype(f32), low.astype(f32)).astype(bf16)
    part = acc.shape[1] // n
    for k in range(n):
        pieces[k][: along.shape[1], :] = acc[:, ds(rot_index(idx[3], k, n), part)].astype(bf16)
        pieces[k][along.shape[1] :, :] = tail


def attn_grad_kernel(dims, own, qc, kc, oc, idx, one_rel, out_rel, qkv_gb, gain_one, gain_two, gq_grad, gk_grad, keep, send, extra, extra_rel):
    half = keep.shape[0]
    qkv = qc + 2 * kc
    width = one_rel.shape[0]

    def halves(v):
        high = v.astype(bf16).astype(f32)
        return high, v - high

    rows = lax.broadcasted_iota(jnp.int32, (PAD, width), 0)
    lines = jnp.zeros((PAD, width), f32)
    values = halves(gain_one[0:1, :]) + halves(gain_two[0:1, :])
    for i, v in enumerate(values):
        lines = lines + jnp.where(rows == i, v, 0.0)
    cols = lines.T
    heads = jnp.concatenate([gq_grad[...], gk_grad[...]], axis=0)
    high, low = halves(heads)
    lane = lax.broadcasted_iota(jnp.int32, (own, PAD), 1)
    tile = jnp.zeros((own, PAD), f32)
    count = 2 * HD // own
    for i in range(count):
        at = slice(i * own, (i + 1) * own)
        tile = tile + jnp.where(lane == 4 + i, high[at], 0.0)
        tile = tile + jnp.where(lane == 4 + count + i, low[at], 0.0)
    for i in range(width // own):
        extra[i * own : (i + 1) * own, :] = (cols[i * own : (i + 1) * own] + tile).astype(bf16)
    store_relative(dims, idx, extra_rel, extra, own)
    a = dot(one_rel[...], qkv_gb[...]).astype(bf16)
    for out, at in ((keep, slice(0, half)), (send, slice(half, 2 * half))):
        out[:, :qkv] = a[at]
        out[:, qkv : qkv + oc] = out_rel[at, :]
        out[:, qkv + oc :] = extra_rel[at, :]


def sum_kernel(cuts, *refs):
    outs = refs[len(refs) - len(cuts) + 1 :]
    ins = refs[: len(refs) - len(cuts) + 1]
    for out, first, last in zip(outs, cuts[:-1], cuts[1:]):
        total = ins[0][:, first:last].astype(f32)
        for v in ins[1:]:
            total = total + v[:, first:last].astype(f32)
        out[...] = total


def pack_kernel(q, k, v, o, g, u, d, gain_one, gain_two, x, c, attn, ffn, both, square):
    at = 0
    for w in (q, k, v):
        attn[:, at : at + w.shape[1]] = w[...]
        at += w.shape[1]
    own = q.shape[0]
    square[...] = jnp.zeros_like(square)
    square[0:1, :own] = gain_one[...].astype(f32)
    square[1:2, :own] = gain_two[...].astype(f32)
    attn[:, at:] = square[...].T[:own].astype(bf16)
    at = 0
    for w in (g, u, d, o):
        ffn[:, at : at + w.shape[1]] = w[...]
        at += w.shape[1]
    part = x.shape[1]
    both[:, :part] = x[...]
    both[:, part:] = c[...]


def out_grad_kernel(dims, own, idx, mid, attn_b, out, turned, rel):
    turned[...] = mid[...].T
    store_relative(dims, idx, rel, turned, own)
    out[...] = dot(rel[...], attn_b[...]).astype(bf16)


def core_sum(keep, send, n):
    got = shift(send, "core", 1)
    step = keep.shape[0] // n
    return [
        (keep[k * step : (k + 1) * step].astype(f32) + got[k * step : (k + 1) * step].astype(f32)).astype(bf16)
        for k in range(n)
    ]


def row_sum(x, axis):
    step = x.shape[0] // lax.axis_size(axis)
    return summed([x[k * step : (k + 1) * step] for k in range(lax.axis_size(axis))], axis)


def after(values, others):
    return lax.optimization_barrier((list(values), others))[0]


def body(
    block_input,
    attn_gain,
    ffn_gain,
    query_gain,
    key_gain,
    query_weight,
    key_weight,
    value_weight,
    out_weight,
    gate_weight,
    up_weight,
    down_weight,
    cotangent,
):
    span, seq_local, part = block_input.shape
    axes = ("dp", "z", "core", "tensor")
    dims = tuple(lax.axis_size(a) for a in axes)
    nx, nz, nc, n = dims
    idx = jnp.stack([lax.axis_index(a) for a in axes]).astype(jnp.int32)
    width = part * n
    own = query_weight.shape[0]
    qc, kc, oc, ff = (w.shape[1] for w in (query_weight, key_weight, out_weight, gate_weight))
    qkv = qc + 2 * kc
    aw = qkv + oc + PAD

    attn_local, ffn_local, both = call(
        pack_kernel,
        [sds((own, qkv + PAD), bf16), sds((own, 3 * ff + oc), bf16), sds((span, 2 * part), bf16)],
        [query_weight, key_weight, value_weight, out_weight, gate_weight, up_weight, down_weight]
        + [attn_gain[None, :], ffn_gain[None, :], block_input.reshape(span, part), cotangent.reshape(span, part)],
        [pltpu.VMEM((PAD, PAD), f32)],
    )
    ffn_w = lax.all_gather(ffn_local, ("dp", "z", "core"), axis=0, tiled=True)
    by_z = jnp.concatenate(gathered(attn_local, "z"), axis=0)
    both_parts = gathered(both, "tensor")
    my_first = (idx[1] * nc + idx[2]) * span
    positions = (my_first + jnp.arange(span, dtype=jnp.int32)).astype(f32)
    frequency = jnp.power(ROPE_BASE, -2.0 * jnp.arange(HALF, dtype=f32) / HD)
    angle = frequency[:, None] * positions[None, :]
    cosine, sine = jnp.cos(angle), jnp.sin(angle)
    head_gains = jnp.concatenate([query_gain, key_gain])[None, :]
    dp_parts = gathered(by_z, "dp")
    dp_parts, both_parts, cosine, sine, head_gains = lax.optimization_barrier(
        (dp_parts, both_parts, cosine, sine, head_gains)
    )
    dp_partner = [shift(v, "core", 1) for v in dp_parts]
    cot, cot_t = call(
        functools.partial(cot_kernel, dims),
        [sds((span, width), bf16), sds((width, span), bf16)],
        [idx] + both_parts,
    )

    w, base, gains, q_t, raw_t, kv, one_rel = call(
        functools.partial(qkv_kernel, dims, own, qc, kc, oc),
        [
            sds((width, qkv + PAD), bf16),
            sds((span, width), bf16),
            sds((8, width), f32),
            sds((kc, qc // kc * span), bf16),
            sds((qc + kc, span), f32),
            sds((span, 2 * kc), bf16),
            sds((width, span), bf16),
        ],
        [idx] + both_parts + dp_parts + dp_partner + [head_gains, cosine, sine],
        [pltpu.VMEM((width, span), bf16)],
        flops=2 * span * width * qkv,
    )
    kv_own = gathered(kv, "z")
    kv_partner = [shift(v, "core", 1) for v in kv_own]

    length = span * nz * nc
    (kv_own, kv_partner), (cot, cot_t) = lax.optimization_barrier(((kv_own, kv_partner), (cot, cot_t)))
    block = 384
    const = lambda s: pl.BlockSpec(s, lambda j: (0, 0))
    steps = ff // block
    out_blocks = [pl.BlockSpec((width, PAD), lambda j, o=o: (0, o)) for o in (3 * ff // PAD, 3 * ff // PAD + 1)]
    kv_full, attn_t, attn_b, log_total = call(
        functools.partial(attend_kernel, dims, qc, kc, oc),
        [sds((length, 2 * kc), bf16), sds(q_t.shape, f32), sds((span, qc), bf16), sds((8, q_t.shape[1]), f32)],
        [idx, q_t] + kv_own + kv_partner,
        [pltpu.VMEM(q_t.shape, f32), pltpu.VMEM((8, q_t.shape[1]), f32)],
        flops=4 * span * length * qc,
    )
    res = call(
        functools.partial(out_kernel, dims),
        [sds((span, part), bf16)] * n,
        [idx, attn_b, ffn_w, ffn_w],
        grid=(1,),
        in_specs=[pl.BlockSpec(memory_space=pltpu.SMEM), const((span, qc))] + out_blocks,
        out_specs=[const((span, part))] * n,
        flops=2 * span * width * qc,
    )
    attn_mine = summed(res, "tensor").astype(bf16)
    attn_parts = gathered(attn_mine, "tensor")

    hgrad = call(
        hidden_grad_kernel,
        [sds((span, ff), f32)],
        [cot, ffn_w],
        grid=(steps,),
        in_specs=[const((span, width)), pl.BlockSpec((width, block), lambda j: (0, 2 * steps + j))],
        out_specs=[pl.BlockSpec((span, block), lambda j: (0, j))],
        flops=2 * span * width * ff,
    )[0]
    res = call(
        functools.partial(ffn_kernel, dims, own),
        [sds((span, width), f32), sds((span, width), bf16), sds((span, 3 * ff), bf16)]
        + [sds((span, part), bf16)] * n,
        [idx, base, gains] + attn_parts + [ffn_w, ffn_w, hgrad],
        [pltpu.VMEM((span, width), f32)],
        grid=(steps,),
        in_specs=[pl.BlockSpec(memory_space=pltpu.SMEM)]
        + [const((span, width)), const((8, width))]
        + [const((span, part))] * n
        + [pl.BlockSpec((width, block), lambda j, o=o: (0, o + j)) for o in (0, steps)]
        + [pl.BlockSpec((span, block), lambda j: (0, j))],
        out_specs=[const((span, width)), const((span, width)), const((span, 3 * ff))]
        + [const((span, part))] * n,
        flops=8 * span * width * ff,
    )
    middle, normed_two, big = res[:3]
    grad_got = [shift(res[3 + k], "tensor", k) for k in range(1, n)]
    part_zero = res[3]

    ffn_grad = call(
        ffn_grad_kernel,
        [sds((width, 3 * ff), bf16)],
        [normed_two, cot_t, big],
        [pltpu.VMEM((width, span), bf16)],
        grid=(3,),
        in_specs=[const((span, width)), const((width, span)), pl.BlockSpec((span, ff), lambda j: (0, j))],
        out_specs=[pl.BlockSpec((width, ff), lambda j: (0, j))],
        flops=6 * span * width * ff,
    )[0]
    grad_got, ffn_grad = lax.optimization_barrier((grad_got, ffn_grad))
    grad_mine = sum([g.astype(f32) for g in grad_got], part_zero.astype(f32)).astype(bf16)
    grad_parts = gathered(grad_mine, "tensor")
    ffn_sum = lax.psum_scatter(ffn_grad, ("dp", "z", "core"), scatter_dimension=0, tiled=True)

    down_parts = call(
        functools.partial(down_kernel, dims),
        [sds((span, part), bf16)] * n,
        [idx, big, ffn_w],
        grid=(1,),
        in_specs=[
            pl.BlockSpec(memory_space=pltpu.SMEM),
            pl.BlockSpec((span, ff), lambda j: (0, 2)),
            pl.BlockSpec((width, ff), lambda j: (0, 2)),
        ],
        out_specs=[const((span, part))] * n,
        flops=2 * span * width * ff,
    )
    grad_parts, down_parts = lax.optimization_barrier((grad_parts, down_parts))

    mine, mid, gain_two, q_gb, gq_grad, kv_keep, kv_send = call(
        functools.partial(attend_back_kernel, dims, own, qc, kc, oc),
        [
            sds((span, part), f32),
            sds((span, width), bf16),
            sds((8, width), f32),
            sds((span, qc), bf16),
            sds((HD, 1), f32),
            sds((length // 2, 2 * kc), bf16),
            sds((length // 2, 2 * kc), bf16),
        ],
        [idx, middle, gains, cot] + grad_parts + [ffn_w, ffn_w, attn_t, q_t, raw_t, kv_full, log_total, head_gains, cosine, sine],
        [
            pltpu.VMEM((span, width), bf16),
            pltpu.VMEM(q_t.shape, f32),
            pltpu.VMEM(q_t.shape, bf16),
            pltpu.VMEM((8, q_t.shape[1]), f32),
            pltpu.VMEM((span, width), f32),
            pltpu.VMEM(q_t.shape, f32),
            pltpu.VMEM((kc // HD * q_t.shape[1], HD), bf16),
            pltpu.VMEM((kc // HD * q_t.shape[1], HD), bf16),
        ],
        grid=(1,),
        in_specs=[pl.BlockSpec(memory_space=pltpu.SMEM), const((span, width)), const((8, width)), const((span, width))]
        + [const((span, part))] * n
        + out_blocks
        + [const(v.shape) for v in (attn_t, q_t, raw_t, kv_full, log_total, head_gains, cosine, sine)],
        out_specs=[
            const((span, part)),
            const((span, width)),
            const((8, width)),
            const((span, qc)),
            const((HD, 1)),
            const((length // 2, 2 * kc)),
            const((length // 2, 2 * kc)),
        ],
        flops=10 * span * length * qc,
    )
    kv_pieces = core_sum(kv_keep, kv_send, nz)
    kv_parts = [kv_pieces[0]] + [shift(kv_pieces[k], "z", k) for k in range(1, nz)]
    kv_parts[1], down_parts = lax.optimization_barrier((kv_parts[1], down_parts))
    out_rel = call(
        functools.partial(out_grad_kernel, dims, own),
        [sds((width, oc), bf16)],
        [idx, mid, attn_b],
        [pltpu.VMEM((width, span), bf16)] * 2,
        flops=2 * span * width * oc,
    )[0]
    kv_parts[2], out_rel = lax.optimization_barrier((kv_parts[2], out_rel))
    me_t = idx[3]
    middle_mine = lax.dynamic_slice_in_dim(middle, me_t * part, part, 1)
    down_got = [down_parts[0]] + [shift(down_parts[k], "tensor", k) for k in range(1, n)]

    res = call(
        functools.partial(input_grad_kernel, dims, qc, kc),
        [sds((span, qkv), bf16), sds((8, width), f32), sds((HD, 1), f32)]
        + [sds((span + 16, part), bf16)] * n,
        [idx] + kv_parts + [raw_t, head_gains, cosine, sine, q_gb, w, base, gains],
        [pltpu.VMEM((span, width), f32)],
        flops=2 * span * width * qkv,
    )
    qkv_gb, gain_one, gk_grad = res[:3]
    norm_parts = res[3:]
    keep, send = call(
        functools.partial(attn_grad_kernel, dims, own, qc, kc, oc),
        [sds((width // 2, aw), bf16)] * 2,
        [idx, one_rel, out_rel, qkv_gb, gain_one, gain_two, gq_grad, gk_grad],
        [pltpu.VMEM((width, PAD), bf16), pltpu.VMEM((width, PAD), bf16)],
        flops=2 * span * width * (qkv + oc),
    )
    (keep, send), down_got = lax.optimization_barrier(((keep, send), down_got))
    attn_pieces = core_sum(keep, send, nz)
    attn_got = [shift(attn_pieces[k], "z", k) for k in range(1, nz)]
    attn_got[0], norm_parts = lax.optimization_barrier((attn_got[0], norm_parts))
    attn_x = sum([v.astype(f32) for v in attn_got], attn_pieces[0].astype(f32)).astype(bf16)
    norm_got = [norm_parts[0]] + [shift(norm_parts[k], "tensor", k) for k in range(1, n)]
    attn_x, norm_got = lax.optimization_barrier((attn_x, norm_got))
    z_parts = [attn_x[:own]] + [shift(attn_x[k * own : (k + 1) * own], "dp", k) for k in range(1, nx)]
    wgrads = call(
        functools.partial(sum_kernel, (0, qc, qc + kc, qkv, qkv + oc, aw)),
        [sds((own, v), f32) for v in (qc, kc, kc, oc, PAD)],
        z_parts,
    )
    small = wgrads[4]
    block_output = (middle_mine + sum([v.astype(f32) for v in down_got[1:]], down_got[0].astype(f32))).astype(bf16)
    norm_mine = sum([v.astype(f32) for v in norm_got[1:]], norm_got[0].astype(f32))
    along = (norm_mine[span] + norm_mine[span + 1])[:, None] * (1.0 / width)
    base_f = base.astype(f32)
    scale_one = lax.rsqrt(jnp.mean(base_f * base_f, axis=1, keepdims=True) + EPS)
    unit_mine = block_input.reshape(span, part).astype(f32) * scale_one
    gain_mine = lax.dynamic_slice_in_dim(gains, me_t * part, part, 1)[0:1]
    input_grad = (mine + scale_one * (norm_mine[:span] * gain_mine - unit_mine * along)).astype(bf16)

    fgrads = call(
        functools.partial(sum_kernel, (0, ff, 2 * ff, 3 * ff)),
        [sds((own, ff), f32)] * 3,
        [ffn_sum],
    )
    small_all = sum(gathered(small, "tensor"))
    count = 2 * HD // own
    head_sum = (small_all[:, 4 : 4 + count] + small_all[:, 4 + count : 4 + 2 * count]).T.reshape(-1)
    return (
        block_output.reshape(span, seq_local, part),
        input_grad.reshape(span, seq_local, part),
        small_all[:, 0] + small_all[:, 1],
        small[:, 2] + small[:, 3],
        head_sum[:HD],
        head_sum[HD:],
        *wgrads[:4],
        *fgrads,
    )


def solution(mesh):
    dp, seq, tensor = (mesh.shape[a] for a in ("dp", "seq", "tensor"))
    grid = Mesh(
        np.asarray(mesh.devices).reshape(dp, seq // 2, 2, tensor), ("dp", "z", "core", "tensor")
    )
    tokens = P(("z", "core"), "dp", "tensor")
    rows = P(("dp", "z", "core"))
    weight = P(("dp", "z", "core"), "tensor")
    return jax.shard_map(
        body,
        mesh=grid,
        in_specs=(tokens, rows, rows, P(), P()) + (weight,) * 7 + (tokens,),
        out_specs=(tokens, tokens, rows, rows, P(), P()) + (weight,) * 7,
        check_vma=False,
    )
```
